32 devices in a mesh: grp: 2 (over y), col: 4 (over z), row: 2 (over x), seq: 2 (over core).
Axes of the slice: x: 2, y: 2, z: 4, core: 2. Of those that a mesh axis runs over, the one named last changes fastest.
Arguments:
- alignment_tensor: float32 [192, 2, 128, 64], P(('grp', 'seq'), 'row', 'col'), parts along dimension 0, may hold values from -6 to 6
- residue_couplings: float32 [512, 256, 128], P(('grp', 'row'), 'col'), parts along dimension 0, may hold values from -6 to 6
- first_factor_matrix: float32 [64, 32], replicated, may hold values from -0.75 to 0.75
- second_factor_matrix: float32 [64, 32], replicated, may hold values from -0.75 to 0.75
- tensor_product_matrix: float32 [1024, 128], replicated, may hold values from -0.1875 to 0.1875
- coupling_score_matrix: float32 [128, 8], replicated, may hold values from -10.606602 to 10.606602
- averaged_source_matrix: float32 [64, 256], replicated, may hold values from -0.75 to 0.75
- sigmoid_matrix: float32 [64, 256], replicated, may hold values from -0.75 to 0.75
- final_matrix: float32 [256, 64], replicated, may hold values from -0.375 to 0.375
Outputs:
- revised_alignment: float32 [192, 2, 128, 64], P(('grp', 'seq'), 'row', 'col'), parts along dimension 0
- revised_couplings: float32 [512, 256, 128], P(('grp', 'row'), 'col'), parts along dimension 0
The draws below stay inside these ranges and needn't reach their ends.
There are 2 independent parts, one for each index of `grp`. The reference program is written for one: setup_inputs(seed, part) draws one part's arguments, and reference() takes and returns one part's arrays. A program takes and returns all parts, laid end to end along the dimension named above; an argument that names none is the same for every part. Nothing has to cross between parts.
All inputs are finite; a program needn't handle non-finite values.
Results may differ from the reference program's by a relative error of at most 0.0003.
Values sent between devices are 32-bit elements; how exact they have to be, the bound alone decides.
A program may use at most 64 MiB of HBM per device.

```python
import jax
import jax.numpy as jnp
from jax import lax

ALIGN_DIM = 64
CZ = 128
PRODUCT_DIM = 32
HEAD_NUMBER = 8
HEAD_DIM = 32
N = 256
ALIGNED_SEQS = 96
RESIDUE_TILES = 2
TILE_RESIDUES = 128


def draw_coupling_score_matrix(key, part):
    base = jnp.clip(jax.random.normal(jax.random.fold_in(key, 11), (CZ, HEAD_NUMBER), jnp.float32), -4.0, 4.0)
    return base * (1.5 * CZ ** (-0.5))


def draw_residue_couplings(key, part):
    noise = jnp.clip(jax.random.normal(jax.random.fold_in(key, 21), (N, N, CZ), jnp.float32), -6.0, 6.0)
    return noise


def steps_of(key, shape, cuts, least, high):
    level, own = 1.0, jax.random.fold_in(key, 6)
    for dim, blocks in cuts:
        heights = jnp.exp(jax.random.uniform(jax.random.fold_in(own, dim), (blocks,), jnp.float32, least / len(cuts), high / len(cuts)))
        level = level * jnp.repeat(heights, shape[dim] // blocks).reshape([-1 if axis == dim else 1 for axis in range(len(shape))])
    return level


def normal_values(own_key, extent, deviation, reach, pieces=(), held_as=jnp.bfloat16):
    array = deviation * jax.random.normal(own_key, extent, jnp.float32)
    if pieces:
        array = array * steps_of(own_key, extent, pieces, -0.22, 0.18)
    return jnp.clip(array, -reach, reach).astype(held_as)


def setup_inputs(seed: int = 0, part: int = 0) -> dict:
    keys = jax.random.split(jax.random.key(seed), 10)
    part_keys = jax.random.split(jax.random.fold_in(keys[9], part), 10)
    alignment_tensor = normal_values(part_keys[0], (ALIGNED_SEQS, RESIDUE_TILES, TILE_RESIDUES, ALIGN_DIM), 1.0, 6.0, ((0, 2), (1, 2), (2, 4)), jnp.float32)
    residue_couplings = draw_residue_couplings(jax.random.fold_in(jax.random.fold_in(keys[9], part), 71), part)
    first_factor_matrix = normal_values(keys[2], (ALIGN_DIM, PRODUCT_DIM), ALIGN_DIM ** -0.5, 0.75, (), jnp.float32)
    second_factor_matrix = normal_values(keys[3], (ALIGN_DIM, PRODUCT_DIM), ALIGN_DIM ** -0.5, 0.75, (), jnp.float32)
    tensor_product_matrix = normal_values(keys[4], (PRODUCT_DIM * PRODUCT_DIM, CZ), (PRODUCT_DIM * PRODUCT_DIM) ** -0.5, 0.1875, (), jnp.float32)
    coupling_score_matrix = draw_coupling_score_matrix(jax.random.fold_in(keys[9], 71), part)
    averaged_source_matrix = normal_values(keys[6], (ALIGN_DIM, HEAD_NUMBER * HEAD_DIM), ALIGN_DIM ** -0.5, 0.75, (), jnp.float32)
    sigmoid_matrix = normal_values(keys[7], (ALIGN_DIM, HEAD_NUMBER * HEAD_DIM), ALIGN_DIM ** -0.5, 0.75, (), jnp.float32)
    final_matrix = normal_values(keys[8], (HEAD_NUMBER * HEAD_DIM, ALIGN_DIM), (HEAD_NUMBER * HEAD_DIM) ** -0.5, 0.375, (), jnp.float32)
    return dict(alignment_tensor=alignment_tensor, residue_couplings=residue_couplings, first_factor_matrix=first_factor_matrix, second_factor_matrix=second_factor_matrix, tensor_product_matrix=tensor_product_matrix, coupling_score_matrix=coupling_score_matrix, averaged_source_matrix=averaged_source_matrix, sigmoid_matrix=sigmoid_matrix, final_matrix=final_matrix)


epsilon = 1e-05
exact_arithmetic = lax.Precision.HIGHEST

def standardize_entries(inputs):
    center = inputs - lax.optimization_barrier(jnp.mean(inputs, axis=-1, keepdims=True))
    spread = lax.optimization_barrier(jnp.mean(center * center, axis=-1, keepdims=True))
    return center / jnp.sqrt(spread + epsilon)

def reference(alignment_tensor, residue_couplings, first_factor_matrix, second_factor_matrix, tensor_product_matrix, coupling_score_matrix, averaged_source_matrix, sigmoid_matrix, final_matrix):
    alignment_depth_number = alignment_tensor.shape[0]
    residue_number = alignment_tensor.shape[1] * alignment_tensor.shape[2]
    alignment_depth = alignment_tensor.shape[3]
    raveled_tensor_product = alignment_tensor.reshape(alignment_depth_number, residue_number, alignment_depth)
    standardized_alignment = standardize_entries(raveled_tensor_product)
    first_factor_tile = jnp.einsum('kgd,dl->kgl', standardized_alignment, first_factor_matrix, precision=exact_arithmetic)
    second_factor_tile = jnp.einsum('kgd,dl->kgl', standardized_alignment, second_factor_matrix, precision=exact_arithmetic)
    block_rows = min(64, residue_number)
    left_blocks = first_factor_tile.reshape(alignment_depth_number, residue_number // block_rows, block_rows, -1).transpose(1, 0, 2, 3)

    def outer_block(left_block):
        product = jnp.einsum('sic,sje->ijce', left_block, second_factor_tile, precision=exact_arithmetic) / alignment_depth_number
        flat_prod = product.reshape(block_rows * residue_number, -1)
        return jnp.dot(flat_prod, tensor_product_matrix, precision=exact_arithmetic).reshape(block_rows, residue_number, -1)
    update = lax.map(outer_block, left_blocks).reshape(residue_number, residue_number, -1)
    revised_couplings = residue_couplings + update
    scores = jnp.einsum('ijc,ch->ihj', standardize_entries(revised_couplings), coupling_score_matrix, precision=exact_arithmetic)
    weights = jax.nn.softmax(scores, axis=-1)
    head_count = coupling_score_matrix.shape[1]
    averaged_sources = jnp.einsum('pko,ol->pkl', standardized_alignment, averaged_source_matrix, precision=exact_arithmetic)
    averaged_sources = averaged_sources.reshape(alignment_depth_number, residue_number, head_count, -1)
    sigmoid_factors = jax.nn.sigmoid(jnp.einsum('pko,ol->pkl', standardized_alignment, sigmoid_matrix, precision=exact_arithmetic))
    mixed_rows = jnp.einsum('ihj,sjhd->sihd', weights, averaged_sources, precision=exact_arithmetic).reshape(alignment_depth_number, residue_number, -1)
    coupling_increment = jnp.einsum('snf,fc->snc', mixed_rows * sigmoid_factors, final_matrix, precision=exact_arithmetic)
    revised_alignment = (raveled_tensor_product + coupling_increment).reshape(alignment_tensor.shape)
    return (revised_alignment, revised_couplings)
```

```python
import functools

import jax
import jax.numpy as jnp
from jax import lax
from jax.experimental import pallas as pl
from jax.experimental.pallas import tpu as pltpu
from jax.sharding import PartitionSpec as P

epsilon = 1e-05
exact_arithmetic = lax.Precision.HIGHEST


def broadcast(block, axis, holder):
    block = jnp.where(lax.axis_index(axis) == holder, block, jnp.zeros_like(block))
    return lax.psum(block, axis)


def standardize_entries(inputs):
    center = inputs - jnp.mean(inputs, axis=-1, keepdims=True)
    spread = jnp.mean(center * center, axis=-1, keepdims=True)
    return center / jnp.sqrt(spread + epsilon)


def pair_scores(pair_rows, coupling_score_matrix):
    return jnp.einsum(
        "ijc,ch->ihj",
        standardize_entries(pair_rows),
        coupling_score_matrix,
        precision=exact_arithmetic,
    )


def general_path(
    alignment_tensor,
    residue_couplings,
    first_factor_matrix,
    second_factor_matrix,
    tensor_product_matrix,
    coupling_score_matrix,
    averaged_source_matrix,
    sigmoid_matrix,
    final_matrix,
):
    shard_alignment_entries = alignment_tensor.shape[0]
    total_seqs = shard_alignment_entries * lax.axis_size("seq")
    coupling_lines = residue_couplings.shape[0]
    col_count = residue_couplings.shape[1]
    alignment_depth = alignment_tensor.shape[3]
    outer_width = first_factor_matrix.shape[1]
    head_count = coupling_score_matrix.shape[1]
    gathered_lines = lax.all_gather(alignment_tensor, "col", axis=2, tiled=True)
    alignment_tile_entries = gathered_lines.reshape(
        shard_alignment_entries, coupling_lines, alignment_depth
    )
    standardized_alignment = standardize_entries(alignment_tile_entries)
    first_factor_tile = jnp.einsum(
        "kgd,dl->kgl", standardized_alignment, first_factor_matrix, precision=exact_arithmetic
    )
    combined_matrix = jnp.concatenate([second_factor_matrix, averaged_source_matrix], axis=1)
    first_col = lax.axis_index("col") * col_count
    root_row = first_col // coupling_lines
    offset = first_col % coupling_lines
    raw_piece = lax.dynamic_slice_in_dim(alignment_tile_entries, offset, col_count, 1)
    raw_received = broadcast(raw_piece, "row", root_row)
    received = jnp.einsum(
        "pko,ol->pkl",
        standardize_entries(raw_received),
        combined_matrix,
        precision=exact_arithmetic,
    )
    second_factor_tile = received[:, :, :outer_width]
    averaged_sources = received[:, :, outer_width:].reshape(
        shard_alignment_entries, col_count, head_count, -1
    )
    block_rows = 16
    left_blocks = first_factor_tile.reshape(
        shard_alignment_entries, coupling_lines // block_rows, block_rows, outer_width
    ).transpose(1, 0, 2, 3)

    def outer_block(left_block):
        product = (
            jnp.einsum("sic,sje->ijce", left_block, second_factor_tile, precision=exact_arithmetic)
            / total_seqs
        )
        flat_prod = product.reshape(block_rows * col_count, -1)
        return jnp.dot(flat_prod, tensor_product_matrix, precision=exact_arithmetic).reshape(
            block_rows, col_count, -1
        )

    update = lax.map(outer_block, left_blocks).reshape(coupling_lines, col_count, -1)
    revised_couplings = residue_couplings + lax.psum(update, "seq")
    scores = pair_scores(revised_couplings, coupling_score_matrix)
    local_top = jnp.max(scores, axis=2)
    score_top = lax.pmax(local_top, "col")
    score_total = lax.psum(jnp.sum(jnp.exp(scores - score_top[:, :, None]), axis=2), "col")
    weights = jnp.exp(scores - score_top[:, :, None]) / score_total[:, :, None]
    mixed_rows = jnp.einsum(
        "ihj,sjhd->sihd", weights, averaged_sources, precision=exact_arithmetic
    ).reshape(shard_alignment_entries, coupling_lines, -1)
    summed = lax.psum_scatter(mixed_rows, "col", scatter_dimension=1, tiled=True)
    shard_standardized_alignment = standardize_entries(
        alignment_tensor.reshape(shard_alignment_entries, -1, alignment_depth)
    )
    sigmoid_factors = jax.nn.sigmoid(
        jnp.einsum(
            "pko,ol->pkl", shard_standardized_alignment, sigmoid_matrix, precision=exact_arithmetic
        )
    )
    coupling_increment = jnp.einsum(
        "snf,fc->snc", summed * sigmoid_factors, final_matrix, precision=exact_arithmetic
    )
    revised_alignment = alignment_tensor + coupling_increment.reshape(alignment_tensor.shape)
    return (revised_alignment, revised_couplings)


f32, bf16 = jnp.float32, jnp.bfloat16
LANES = 128


def halves(values):
    high = values.astype(bf16)
    return high, (values - high.astype(f32)).astype(bf16)


def mm(a, b):
    return jnp.dot(a, b, preferred_element_type=f32)


def mm3(a, b):
    (a_high, a_low), (b_high, b_low) = a, b
    return mm(a_high, b_high) + (mm(a_high, b_low) + mm(a_low, b_high))


def nt(a, b):
    return lax.dot_general(a, b, (((1,), (1,)), ((), ())), preferred_element_type=f32)


def nt3(a, b):
    (a_high, a_low), (b_high, b_low) = a, b
    return nt(a_high, b_high) + (nt(a_high, b_low) + nt(a_low, b_high))


def block_kernel(
    row_size,
    col_size,
    seq_size,
    heads,
    raw_in,
    pair_in,
    first_in,
    second_in,
    product_in,
    score_in,
    source_in,
    gate_in,
    final_in,
    out_ref,
    revised_ref,
    raw_ref,
    pair_ref,
    first_ref,
    second_ref,
    product_ref,
    score_ref,
    source_ref,
    gate_ref,
    final_ref,
    load_sem,
    own_s,
    l_s,
    r_own,
    r_s,
    left_s,
    right_s,
    high_s,
    low_s,
    score_s,
    sent_s,
    received_s,
    weight_s,
    gates_s,
    mixed_s,
    block_send,
    block_recv,
    l_recv,
    r_recv,
    local_sem,
    score_send,
    score_recv,
    pair_sem,
):
    loads = []
    for source, place in (
        (raw_in, raw_ref),
        (first_in, first_ref),
        (second_in, second_ref),
        (product_in, product_ref),
        (pair_in, pair_ref),
        (source_in, source_ref),
        (gate_in, gate_ref),
        (score_in, score_ref),
        (final_in, final_ref),
    ):
        loads.append(pltpu.make_async_copy(source, place, load_sem.at[len(loads)]))
        loads[-1].start()
    seqs, own, depth = raw_ref.shape
    groups = seqs // 2
    rows, cols, channels = revised_ref.shape
    outer = first_ref.shape[0]
    half_cols = cols // seq_size
    total = seqs * seq_size
    wide = 2 * source_ref.shape[1]
    entries = heads * own
    members = col_size * seq_size
    row, col, seq = (lax.axis_index(a) for a in ("row", "col", "seq"))
    other_row, other_seq = 1 - row, 1 - seq
    me = col * seq_size + seq
    mine = row * col_size + col

    def normalize(step, carry):
        parts = []
        for t in range(2):
            part = standardize_entries(raw_ref[step + t * groups])
            parts.append(part)
        at = pl.ds(pl.multiple_of(step * own, own), own)
        own_s[mine, at, :] = jnp.concatenate(parts, axis=-1)
        return carry

    for load in loads[:3]:
        load.wait()
    lax.fori_loop(0, groups, normalize, 0, unroll=4)

    first = halves(twice(first_ref[...]))
    second = halves(twice(second_ref[...]))
    pairs = LANES // 2 // own
    left_steps = groups // pairs

    def project_left(step, carry):
        parts = []
        for t in range(pairs):
            at = pl.ds(pl.multiple_of((t * left_steps + step) * own, own), own)
            result = nt3(first, halves(own_s[mine, at, :]))
            parts += [result[:outer], result[outer:]]
        l_s[col, seq, pl.ds(pl.multiple_of(step * outer, outer), outer), :] = jnp.concatenate(parts, axis=1)
        return carry

    lax.fori_loop(0, left_steps, project_left, 0, unroll=4)
    span = LANES // 2
    room = jnp.zeros((outer, span - seqs), f32)
    right_steps = half_cols // 2

    def project_right(step, carry):
        parts = []
        for t in range(2):
            tokens = own_s[mine, pl.ds(t * right_steps + step, groups, stride=own), :]
            result = nt3(second, halves(tokens))
            parts += [result[:outer], result[outer:], room]
        r_own[pl.ds(pl.multiple_of(step * outer, outer), outer), :] = jnp.concatenate(parts, axis=1)
        return carry

    lax.fori_loop(0, right_steps, project_right, 0, unroll=4)

    barrier = pltpu.get_barrier_semaphore()

    def member(offset):
        other = lax.rem(me + offset, members)
        return {"col": other // seq_size, "seq": lax.rem(other, seq_size)}

    for offset in range(1, members):
        pl.semaphore_signal(barrier, inc=1, device_id=member(offset), device_id_type=pl.DeviceIdType.MESH)
    pl.semaphore_signal(barrier, inc=1, device_id={"row": other_row}, device_id_type=pl.DeviceIdType.MESH)
    pl.semaphore_wait(barrier, members)

    started = []

    def ship(source, place, target, sem, condition):
        copy = pltpu.make_async_remote_copy(
            src_ref=source,
            dst_ref=place,
            send_sem=next_send(),
            recv_sem=sem,
            device_id=target,
            device_id_type=pl.DeviceIdType.MESH,
        )
        started.append((copy, condition))
        run(condition, copy.start)

    def run(condition, action):
        if condition is None:
            action()
        else:
            pl.when(condition)(action)

    def both(a, b):
        return b if a is None else (a if b is None else jnp.logical_and(a, b))

    def arrived(place, sem):
        return pltpu.make_async_remote_copy(
            src_ref=place,
            dst_ref=place,
            send_sem=block_send.at[0],
            recv_sem=sem,
            device_id={"row": other_row},
            device_id_type=pl.DeviceIdType.MESH,
        ).wait_recv

    counter = [0]

    def next_send():
        counter[0] += 1
        return block_send.at[counter[0] - 1]

    def relay_left(at, rightward, leftward, exists):
        place, sem = l_s.at[at, seq], l_recv.at[at, seq]
        if rightward:
            ship(place, place, {"col": col + 1}, sem, both(exists, col < col_size - 1))
        if leftward:
            ship(place, place, {"col": col - 1}, sem, both(exists, col > 0))
        ship(place, place, {"seq": other_seq}, sem, exists)

    def relay(slot, rightward, leftward, across, exists):
        place, sem = own_s.at[slot], block_recv.at[slot]
        if rightward:
            ship(place, place, {"col": col + 1}, sem, both(exists, col < col_size - 1))
        if leftward:
            ship(place, place, {"col": col - 1}, sem, both(exists, col > 0))
        if across:
            ship(place, place, {"row": other_row}, sem, exists)

    def relay_step(step):
        run(col >= step, arrived(own_s.at[mine - step], block_recv.at[mine - step]))
        relay(mine - step, True, False, True, col >= step)
        run(col + step < col_size, arrived(own_s.at[mine + step], block_recv.at[mine + step]))
        relay(mine + step, False, True, True, col + step < col_size)

    relay_left(col, True, True, None)
    column_slot = col * seq_size + seq
    here = column_slot // col_size == row
    elsewhere = jnp.logical_not(here)
    target_col, target_seq = mine // seq_size, lax.rem(mine, seq_size)
    own_right = jnp.logical_and(target_col == col, target_seq == seq)
    ship(
        r_own, r_s.at[seq], {"col": target_col, "seq": target_seq}, r_recv.at[seq], jnp.logical_not(own_right)
    )
    ship(own_s.at[mine], own_s.at[mine], {"row": other_row}, block_recv.at[mine], elsewhere)

    @pl.when(own_right)
    def _():
        keep = pltpu.make_async_copy(r_own, r_s.at[seq], local_sem.at[0])
        keep.start()
        keep.wait()

    for step in range(1, col_size):
        run(col >= step, arrived(l_s.at[col - step, seq], l_recv.at[col - step, seq]))
        relay_left(col - step, True, False, col >= step)
        run(col + step < col_size, arrived(l_s.at[col + step, seq], l_recv.at[col + step, seq]))
        relay_left(col + step, False, True, col + step < col_size)
        if step == 1:
            source_here = lax.rem(column_slot, col_size) == col
            for source in range(seq_size):
                kept = jnp.logical_and(source_here, seq == source)
                run(jnp.logical_and(here, jnp.logical_not(kept)), arrived(r_s.at[source], r_recv.at[source]))
                ship(r_s.at[source], r_s.at[source], {"row": other_row}, r_recv.at[source], here)
            ship(own_s.at[mine], own_s.at[mine], {"row": other_row}, block_recv.at[mine], here)
    relay(mine, True, True, False, None)
    for source in range(seq_size):
        run(elsewhere, arrived(r_s.at[source], r_recv.at[source]))
    for at in range(col_size):
        arrived(l_s.at[at, other_seq], l_recv.at[at, other_seq])()

    for load in loads[3:]:
        load.wait()
    blank = jnp.zeros(((span - seqs) * outer, rows), f32)
    for source in range(seq_size):
        left_s[(source * span + seqs) * outer : (source + 1) * span * outer, :] = blank

    def place_left(step, carry):
        at = pl.ds(pl.multiple_of(step * outer, outer), outer)
        for source in range(seq_size):
            blocks = [l_s[t, source, at, :] for t in range(col_size)]
            for t in range(pairs):
                for half in range(2):
                    lane = (2 * t + half) * own
                    line = jnp.concatenate([block[:, lane : lane + own] for block in blocks], axis=1)
                    place = source * span + half * groups + t * left_steps + step
                    left_s[pl.ds(pl.multiple_of(place * outer, outer), outer), :] = line
        return carry

    lax.fori_loop(0, left_steps, place_left, 0, unroll=2)
    for t in range(2):
        right_s[t * right_steps * outer : (t + 1) * right_steps * outer, :] = jnp.concatenate(
            [r_s[source, :, t * span : (t + 1) * span] for source in range(seq_size)], axis=1
        )

    r_high, r_low = halves(right_s[...])
    r_both = jnp.concatenate([r_high, r_low], axis=1)

    def outer_step(step, carry):
        pieces = [left_s[pl.ds(2 * step + t, LANES, stride=outer), :] for t in range(2)]
        l_high, l_low = halves(jnp.concatenate(pieces, axis=1))
        product = mm(r_both, jnp.concatenate([l_high, l_high], axis=0)) + mm(r_high, l_low)
        p_high, p_low = halves(product)
        for t in range(2):
            high_s[2 * step + t] = p_high[:, t * rows : (t + 1) * rows]
            low_s[2 * step + t] = p_low[:, t * rows : (t + 1) * rows]
        return carry

    lax.fori_loop(0, outer // 2, outer_step, 0)
    relay_step(1)
    t_high, t_low = halves(product_ref[...].T)
    t_both = jnp.concatenate([t_high, t_low], axis=0)
    c_halves = halves(score_ref[...])
    first_col = seq * half_cols
    flat_pair = pair_ref.reshape(rows * cols, channels)
    flat_revised = revised_ref.reshape(rows * cols, channels)

    def pair_step(step, carry):
        def block(ref):
            pieces = [
                ref[:, pl.ds(pl.multiple_of((2 * step + t) * outer, outer), outer), :].reshape(outer * outer, rows)
                for t in range(2)
            ]
            return jnp.concatenate(pieces, axis=1)

        joint = mm(t_both, block(high_s))
        update = (joint[:channels] + (joint[channels:] + mm(t_high, block(low_s)))) / total
        for t in range(2):
            column = 2 * step + t
            at = pl.ds(first_col + column, rows, stride=cols)
            revised = flat_pair[at, :].T + update[:, t * rows : (t + 1) * rows]
            flat_revised[at, :] = revised.T
            center = revised - jnp.mean(revised, axis=0, keepdims=True)
            spread = jnp.mean(center * center, axis=0, keepdims=True)
            score_s[column] = mm3(c_halves, halves(center / jnp.sqrt(spread + epsilon)))
        return carry

    bounds = [half_cols // 2 * t // (col_size - 1) for t in range(1, col_size)]
    lax.fori_loop(0, bounds[-2], pair_step, 0)
    for step in range(2, col_size - 1):
        relay_step(step)
    lax.fori_loop(bounds[-2], bounds[-1], pair_step, 0)

    pack_count = LANES // own
    quarter = half_cols // pack_count
    scores = score_s[...].reshape(pack_count, quarter, heads, rows)
    for block in range(col_size):
        cut = [scores[t, :, :, block * own : (block + 1) * own] for t in range(pack_count)]
        sent_s[block] = jnp.concatenate(cut, axis=-1)
    received_s[me] = sent_s[col]
    own_rows = halves(own_s[mine])
    gates_s[...] = jax.nn.sigmoid(mm3(own_rows, halves(twice(gate_ref[...])))).reshape(groups, own, wide)
    score_copies = []
    for offset in range(1, members):
        target = member(offset)
        copy = pltpu.make_async_remote_copy(
            src_ref=sent_s.at[target["col"]],
            dst_ref=received_s.at[me],
            send_sem=score_send.at[offset],
            recv_sem=score_recv.at[me],
            device_id=target,
            device_id_type=pl.DeviceIdType.MESH,
        )
        copy.start()
        score_copies.append(copy)
    if col_size > 2:
        relay_step(col_size - 1)
    half_pair = revised_ref.at[:, pl.ds(pl.multiple_of(first_col, half_cols), half_cols), :]
    pair_copy = pltpu.make_async_remote_copy(
        src_ref=half_pair,
        dst_ref=half_pair,
        send_sem=pair_sem.at[0],
        recv_sem=pair_sem.at[1],
        device_id={"seq": other_seq},
        device_id_type=pl.DeviceIdType.MESH,
    )
    pair_copy.start()
    for offset in range(1, members):
        other = lax.rem(me + offset, members)
        arrived(received_s.at[other], score_recv.at[other])()
    logits = received_s[...].reshape(members * quarter, heads, LANES)

    def over_lanes(values, op):
        result = values
        for t in range(1, pack_count):
            result = op(result, pltpu.roll(values, t * own, 1))
        return result

    top = over_lanes(jnp.max(logits, axis=0), jnp.maximum)
    powers = jnp.exp(logits - top[None])
    weights = powers / over_lanes(jnp.sum(powers, axis=0), jnp.add)[None]
    weight_s[...] = weights.reshape(members * quarter * heads, LANES)
    lines = []
    for head in range(heads):
        turned = weight_s[pl.ds(head, members * quarter, stride=heads), :].T
        lines.append(jnp.concatenate([turned[t * own : (t + 1) * own] for t in range(pack_count)], axis=1))
    w_high, w_low = halves(jnp.concatenate(lines, axis=0))
    w_both = jnp.concatenate([w_high, w_low], axis=0)
    s_high, s_low = halves(twice(source_ref[...]))
    s_twice = jnp.concatenate([s_high, s_high], axis=0)
    row_head = lax.broadcasted_iota(jnp.int32, (entries, wide), 0) // own
    lane_head = lax.broadcasted_iota(jnp.int32, (entries, wide), 1) // (wide // 2 // heads) % heads
    mask = row_head == lane_head

    for at in range(col_size):
        arrived(own_s.at[other_row * col_size + at], block_recv.at[other_row * col_size + at])()

    def mix_step(group, carry):
        pieces = [
            own_s[:, pl.ds(pl.multiple_of(group * own + t * quarter, quarter), quarter), :].reshape(-1, LANES)
            for t in range(pack_count)
        ]
        x_high, x_low = halves(jnp.concatenate(pieces, axis=0))
        values = mm(jnp.concatenate([x_high, x_low], axis=1), s_twice) + mm(x_high, s_low)
        v_high, v_low = halves(values)
        joint = mm(w_both, v_high)
        full = joint[:entries] + (joint[entries:] + mm(w_high, v_low))
        mixed = jnp.sum(jnp.where(mask, full, 0.0).reshape(heads, own, wide), axis=0)
        mixed_s[group] = mixed * gates_s[group]
        return carry

    lax.fori_loop(0, groups, mix_step, 0)
    result = nt3(halves(mixed_s[...].reshape(groups * own, wide)), halves(twice(final_ref[...])))
    result = result.reshape(groups, own, LANES)
    for t in range(2):
        at = pl.ds(t * groups, groups)
        out_ref[at] = raw_ref[at] + result[:, :, t * depth : (t + 1) * depth]

    for copy, condition in started:
        run(condition, copy.wait_send)
    for copy in score_copies:
        copy.wait_send()
    pair_copy.wait_send()
    other_half = revised_ref.at[:, pl.ds(pl.multiple_of(other_seq * half_cols, half_cols), half_cols), :]
    pltpu.make_async_remote_copy(
        src_ref=other_half,
        dst_ref=other_half,
        send_sem=pair_sem.at[0],
        recv_sem=pair_sem.at[1],
        device_id={"seq": other_seq},
        device_id_type=pl.DeviceIdType.MESH,
    ).wait_recv()


def twice(matrix):
    zero = jnp.zeros_like(matrix)
    return jnp.concatenate(
        [jnp.concatenate([matrix, zero], axis=1), jnp.concatenate([zero, matrix], axis=1)], axis=0
    )


FINISH_CUTS = 4


def finish_kernel(*refs):
    count = len(refs) // 2
    copies = []
    for source, target in zip(refs[:count], refs[count:-1]):
        share = source.shape[0] // FINISH_CUTS
        for cut in range(FINISH_CUTS):
            at = pl.ds(cut * share, share)
            copies.append(pltpu.make_async_copy(source.at[at], target.at[at], refs[-1].at[len(copies)]))
            copies[-1].start()
    for copy in copies:
        copy.wait()


def fast_path(
    alignment_tensor,
    residue_couplings,
    first_factor_matrix,
    second_factor_matrix,
    tensor_product_matrix,
    coupling_score_matrix,
    averaged_source_matrix,
    sigmoid_matrix,
    final_matrix,
):
    seqs, _, own, depth = alignment_tensor.shape
    rows, cols, channels = residue_couplings.shape
    outer = first_factor_matrix.shape[1]
    heads = coupling_score_matrix.shape[1]
    row_size, col_size, seq_size = (lax.axis_size(a) for a in ("row", "col", "seq"))
    total = seqs * seq_size
    blocks = row_size * col_size
    half_cols = cols // seq_size
    members = col_size * seq_size
    groups = seqs // 2
    wide = 2 * averaged_source_matrix.shape[1]
    quarter = half_cols * own // LANES
    vmem = pl.BlockSpec(memory_space=pltpu.VMEM)
    dma = pltpu.SemaphoreType.DMA
    arrays = (
        alignment_tensor.reshape(seqs, own, depth),
        residue_couplings,
        first_factor_matrix.T,
        second_factor_matrix.T,
        tensor_product_matrix,
        coupling_score_matrix.T,
        averaged_source_matrix,
        sigmoid_matrix,
        final_matrix.T,
    )
    alignment, couplings = pl.pallas_call(
        functools.partial(block_kernel, row_size, col_size, seq_size, heads),
        out_shape=(
            pltpu.VMEM((seqs, own, depth), f32),
            pltpu.VMEM((rows, cols, channels), f32),
        ),
        in_specs=[pl.BlockSpec(memory_space=pltpu.HBM)] * 9,
        out_specs=(vmem, vmem),
        scratch_shapes=[pltpu.VMEM(a.shape, f32) for a in arrays]
        + [
            dma((len(arrays),)),
            pltpu.VMEM((blocks, groups * own, LANES), f32),
            pltpu.VMEM((col_size, seq_size, groups // (LANES // 2 // own) * outer, LANES), f32),
            pltpu.VMEM((half_cols // 2 * outer, LANES), f32),
            pltpu.VMEM((seq_size, half_cols // 2 * outer, LANES), f32),
            pltpu.VMEM((LANES * outer, rows), f32),
            pltpu.VMEM((half_cols * outer, LANES), f32),
            pltpu.VMEM((outer, half_cols * outer, rows), bf16),
            pltpu.VMEM((outer, half_cols * outer, rows), bf16),
            pltpu.VMEM((half_cols, heads, rows), f32),
            pltpu.VMEM((col_size, quarter, heads, LANES), f32),
            pltpu.VMEM((members, quarter, heads, LANES), f32),
            pltpu.VMEM((members * quarter * heads, LANES), f32),
            pltpu.VMEM((groups, own, wide), f32),
            pltpu.VMEM((groups, own, wide), f32),
            dma((64,)),
            dma((blocks,)),
            dma((col_size, seq_size)),
            dma((seq_size,)),
            dma((1,)),
            dma((members,)),
            dma((members,)),
            dma((2,)),
        ],
        compiler_params=pltpu.CompilerParams(
            collective_id=0, has_side_effects=True, vmem_limit_bytes=59 << 20
        ),
    )(*arrays)
    revised_alignment, revised_couplings = pl.pallas_call(
        finish_kernel,
        out_shape=(
            jax.ShapeDtypeStruct((seqs, own, depth), f32),
            jax.ShapeDtypeStruct((rows, cols, channels), f32),
        ),
        in_specs=[vmem] * 2,
        out_specs=(pl.BlockSpec(memory_space=pltpu.HBM),) * 2,
        scratch_shapes=[dma((2 * FINISH_CUTS,))],
        compiler_params=pltpu.CompilerParams(vmem_limit_bytes=12 << 20),
    )(alignment, couplings)
    return revised_alignment.reshape(alignment_tensor.shape), revised_couplings


def on_device(alignment_tensor, residue_couplings, first_factor_matrix, *rest):
    seqs, tiles, own, depth = alignment_tensor.shape
    rows, cols, channels = residue_couplings.shape
    row_size, col_size, seq_size = (lax.axis_size(a) for a in ("row", "col", "seq"))
    fits = (
        tiles == 1
        and rows == own * col_size == LANES
        and cols == own * seq_size
        and row_size * rows == col_size * cols
        and own % 16 == 0
        and seqs % 6 == 0
        and 2 * depth == channels == LANES
        and first_factor_matrix.shape[1] % 16 == 0
        and seq_size == row_size == 2
        and rest[2].shape[1] == 8 == own * own // LANES
        and seqs * seq_size <= LANES
        and seqs // 2 % (LANES // 2 // own) == 0
        and col_size > 2
    )
    path = fast_path if fits else general_path
    return path(alignment_tensor, residue_couplings, first_factor_matrix, *rest)


def solution(mesh):
    return jax.shard_map(
        on_device,
        mesh=mesh,
        in_specs=(
            P(("grp", "seq"), "row", "col", None),
            P(("grp", "row"), "col", None),
            P(),
            P(),
            P(),
            P(),
            P(),
            P(),
            P(),
        ),
        out_specs=(P(("grp", "seq"), "row", "col", None), P(("grp", "row"), "col", None)),
        check_vma=False,
    )
```

```python
import functools

import jax
import jax.numpy as jnp
from jax import lax
from jax.experimental import pallas as pl
from jax.experimental.pallas import tpu as pltpu
from jax.sharding import PartitionSpec as P

epsilon = 1e-05
exact_arithmetic = lax.Precision.HIGHEST


def broadcast(block, axis, holder):
    block = jnp.where(lax.axis_index(axis) == holder, block, jnp.zeros_like(block))
    return lax.psum(block, axis)


def standardize_entries(inputs):
    center = inputs - jnp.mean(inputs, axis=-1, keepdims=True)
    spread = jnp.mean(center * center, axis=-1, keepdims=True)
    return center / jnp.sqrt(spread + epsilon)


def pair_scores(pair_rows, coupling_score_matrix):
    return jnp.einsum(
        "ijc,ch->ihj",
        standardize_entries(pair_rows),
        coupling_score_matrix,
        precision=exact_arithmetic,
    )


def general_path(
    alignment_tensor,
    residue_couplings,
    first_factor_matrix,
    second_factor_matrix,
    tensor_product_matrix,
    coupling_score_matrix,
    averaged_source_matrix,
    sigmoid_matrix,
    final_matrix,
):
    shard_alignment_entries = alignment_tensor.shape[0]
    total_seqs = shard_alignment_entries * lax.axis_size("seq")
    coupling_lines = residue_couplings.shape[0]
    col_count = residue_couplings.shape[1]
    alignment_depth = alignment_tensor.shape[3]
    outer_width = first_factor_matrix.shape[1]
    head_count = coupling_score_matrix.shape[1]
    gathered_lines = lax.all_gather(alignment_tensor, "col", axis=2, tiled=True)
    alignment_tile_entries = gathered_lines.reshape(
        shard_alignment_entries, coupling_lines, alignment_depth
    )
    standardized_alignment = standardize_entries(alignment_tile_entries)
    first_factor_tile = jnp.einsum(
        "kgd,dl->kgl", standardized_alignment, first_factor_matrix, precision=exact_arithmetic
    )
    combined_matrix = jnp.concatenate([second_factor_matrix, averaged_source_matrix], axis=1)
    first_col = lax.axis_index("col") * col_count
    root_row = first_col // coupling_lines
    offset = first_col % coupling_lines
    raw_piece = lax.dynamic_slice_in_dim(alignment_tile_entries, offset, col_count, 1)
    raw_received = broadcast(raw_piece, "row", root_row)
    received = jnp.einsum(
        "pko,ol->pkl",
        standardize_entries(raw_received),
        combined_matrix,
        precision=exact_arithmetic,
    )
    second_factor_tile = received[:, :, :outer_width]
    averaged_sources = received[:, :, outer_width:].reshape(
        shard_alignment_entries, col_count, head_count, -1
    )
    block_rows = 16
    left_blocks = first_factor_tile.reshape(
        shard_alignment_entries, coupling_lines // block_rows, block_rows, outer_width
    ).transpose(1, 0, 2, 3)

    def outer_block(left_block):
        product = (
            jnp.einsum("sic,sje->ijce", left_block, second_factor_tile, precision=exact_arithmetic)
            / total_seqs
        )
        flat_prod = product.reshape(block_rows * col_count, -1)
        return jnp.dot(flat_prod, tensor_product_matrix, precision=exact_arithmetic).reshape(
            block_rows, col_count, -1
        )

    update = lax.map(outer_block, left_blocks).reshape(coupling_lines, col_count, -1)
    revised_couplings = residue_couplings + lax.psum(update, "seq")
    scores = pair_scores(revised_couplings, coupling_score_matrix)
    local_top = jnp.max(scores, axis=2)
    score_top = lax.pmax(local_top, "col")
    score_total = lax.psum(jnp.sum(jnp.exp(scores - score_top[:, :, None]), axis=2), "col")
    weights = jnp.exp(scores - score_top[:, :, None]) / score_total[:, :, None]
    mixed_rows = jnp.einsum(
        "ihj,sjhd->sihd", weights, averaged_sources, precision=exact_arithmetic
    ).reshape(shard_alignment_entries, coupling_lines, -1)
    summed = lax.psum_scatter(mixed_rows, "col", scatter_dimension=1, tiled=True)
    shard_standardized_alignment = standardize_entries(
        alignment_tensor.reshape(shard_alignment_entries, -1, alignment_depth)
    )
    sigmoid_factors = jax.nn.sigmoid(
        jnp.einsum(
            "pko,ol->pkl", shard_standardized_alignment, sigmoid_matrix, precision=exact_arithmetic
        )
    )
    coupling_increment = jnp.einsum(
        "snf,fc->snc", summed * sigmoid_factors, final_matrix, precision=exact_arithmetic
    )
    revised_alignment = alignment_tensor + coupling_increment.reshape(alignment_tensor.shape)
    return (revised_alignment, revised_couplings)


f32, bf16 = jnp.float32, jnp.bfloat16
LANES = 128
CHUNKS = 4


def halves(values):
    high = values.astype(bf16)
    return high, (values - high.astype(f32)).astype(bf16)


def mm(a, b):
    return jnp.dot(a, b, preferred_element_type=f32)


def mm3(a, b):
    (a_high, a_low), (b_high, b_low) = a, b
    return mm(a_high, b_high) + (mm(a_high, b_low) + mm(a_low, b_high))


def nt(a, b):
    return lax.dot_general(a, b, (((1,), (1,)), ((), ())), preferred_element_type=f32)


def nt3(a, b):
    (a_high, a_low), (b_high, b_low) = a, b
    return nt(a_high, b_high) + (nt(a_high, b_low) + nt(a_low, b_high))


def block_kernel(
    row_size,
    col_size,
    seq_size,
    heads,
    raw_in,
    pair_in,
    first_in,
    second_in,
    product_in,
    score_in,
    source_in,
    gate_in,
    final_in,
    out_ref,
    revised_ref,
    raw_ref,
    pair_ref,
    first_ref,
    second_ref,
    product_ref,
    score_ref,
    source_ref,
    gate_ref,
    final_ref,
    load_sem,
    own_s,
    l_s,
    r_own,
    r_s,
    left_s,
    right_s,
    high_s,
    low_s,
    turned_s,
    x_s,
    logit_s,
    weight_s,
    mixer_s,
    v_high_s,
    v_low_s,
    gates_s,
    part_s,
    whole_s,
    send_sem,
    l_recv,
    r_recv,
    x_recv,
    logit_recv,
    part_recv,
    pair_sem,
):
    loads = []
    for source, place in (
        (raw_in, raw_ref),
        (second_in, second_ref),
        (first_in, first_ref),
        (pair_in, pair_ref),
        (product_in, product_ref),
        (source_in, source_ref),
        (gate_in, gate_ref),
        (score_in, score_ref),
        (final_in, final_ref),
    ):
        loads.append(pltpu.make_async_copy(source, place, load_sem.at[len(loads)]))
        loads[-1].start()
    seqs, own, depth = raw_ref.shape
    groups = seqs // 2
    rows, cols, channels = revised_ref.shape
    outer = first_ref.shape[0]
    half_cols = cols // seq_size
    total = seqs * seq_size
    wide = 2 * source_ref.shape[1]
    members = col_size * seq_size
    tokens_all = members * half_cols
    share = groups // col_size
    row, col, seq = (lax.axis_index(a) for a in ("row", "col", "seq"))
    other_row, other_seq = 1 - row, 1 - seq
    me = col * seq_size + seq
    mine = row * col_size + col
    mesh_ids = pl.DeviceIdType.MESH

    barrier = pltpu.get_barrier_semaphore()

    def member(offset):
        other = lax.rem(me + offset, members)
        return {"col": other // seq_size, "seq": lax.rem(other, seq_size)}

    for offset in range(1, members):
        pl.semaphore_signal(barrier, inc=1, device_id=member(offset), device_id_type=mesh_ids)
    pl.semaphore_signal(barrier, inc=1, device_id={"row": other_row}, device_id_type=mesh_ids)

    for load in loads[:3]:
        load.wait()

    def normalize(step, carry):
        parts = []
        for t in range(2):
            part = standardize_entries(raw_ref[step + t * groups])
            parts.append(part)
        at = pl.ds(pl.multiple_of(step * own, own), own)
        own_s[at, :] = jnp.concatenate(parts, axis=-1)
        return carry

    lax.fori_loop(0, groups, normalize, 0, unroll=4)

    first = halves(twice(first_ref[...]))
    second = halves(twice(second_ref[...]))
    span = LANES // 2
    room = jnp.zeros((outer, span - seqs), f32)
    right_steps = half_cols // 2

    def project_right(step, carry):
        parts = []
        for t in range(2):
            tokens = own_s[pl.ds(t * right_steps + step, groups, stride=own), :]
            result = nt3(second, halves(tokens))
            parts += [result[:outer], result[outer:], room]
        r_own[pl.ds(pl.multiple_of(step * outer, outer), outer), :] = jnp.concatenate(parts, axis=1)
        return carry

    lax.fori_loop(0, right_steps, project_right, 0, unroll=4)

    started = []

    def run(condition, action):
        if condition is None:
            action()
        else:
            pl.when(condition)(action)

    def both(a, b):
        return b if a is None else (a if b is None else jnp.logical_and(a, b))

    def ship(source, place, target, sem, condition=None):
        copy = pltpu.make_async_remote_copy(
            src_ref=source,
            dst_ref=place,
            send_sem=send_sem.at[len(started)],
            recv_sem=sem,
            device_id=target,
            device_id_type=mesh_ids,
        )
        started.append((copy, condition))
        run(condition, copy.start)

    def arrived(place, sem, condition=None):
        copy = pltpu.make_async_remote_copy(
            src_ref=place,
            dst_ref=place,
            send_sem=send_sem.at[0],
            recv_sem=sem,
            device_id={"row": other_row},
            device_id_type=mesh_ids,
        )
        run(condition, copy.wait_recv)

    pl.semaphore_wait(barrier, members)
    column_slot = me
    here = column_slot // col_size == row
    elsewhere = jnp.logical_not(here)
    target_col, target_seq = mine // seq_size, lax.rem(mine, seq_size)
    own_right = jnp.logical_and(target_col == col, target_seq == seq)
    ship(
        r_own, r_s.at[seq], {"col": target_col, "seq": target_seq}, r_recv.at[seq], jnp.logical_not(own_right)
    )

    chunk = outer // CHUNKS
    pairs = LANES // 2 // own
    left_steps = groups // pairs

    def project_left(step, carry):
        parts = []
        for t in range(pairs):
            at = pl.ds(pl.multiple_of((t * left_steps + step) * own, own), own)
            result = nt3(first, halves(own_s[at, :]))
            parts += [result[:outer], result[outer:]]
        line = jnp.concatenate(parts, axis=1)
        at = pl.ds(pl.multiple_of(step * chunk, chunk), chunk)
        for k in range(CHUNKS):
            l_s[k, col, seq, at, :] = line[k * chunk : (k + 1) * chunk]
        return carry

    lax.fori_loop(0, left_steps, project_left, 0, unroll=4)

    def relay_left(k, at, rightward, leftward, exists):
        place, sem = l_s.at[k, at, seq], l_recv.at[k, at, seq]
        if rightward:
            ship(place, place, {"col": col + 1}, sem, both(exists, col < col_size - 1))
        if leftward:
            ship(place, place, {"col": col - 1}, sem, both(exists, col > 0))
        ship(place, place, {"seq": other_seq}, sem, exists)

    for k in range(CHUNKS):
        relay_left(k, col, True, True, None)

    @pl.when(own_right)
    def _():
        r_s[seq] = r_own[...]

    for load in loads[3:]:
        load.wait()

    blank = jnp.zeros(((span - seqs) * chunk, rows), f32)
    for k in range(CHUNKS):
        for source in range(seq_size):
            left_s[k, (source * span + seqs) * chunk : (source + 1) * span * chunk, :] = blank
    first_col = seq * half_cols
    flat_pair = pair_ref.reshape(rows * cols, channels)
    flat_revised = revised_ref.reshape(rows * cols, channels)

    def turn_in(column, carry):
        turned_s[column] = flat_pair[pl.ds(first_col + column, rows, stride=cols), :].T
        return carry

    lax.fori_loop(0, half_cols, turn_in, 0, unroll=2)
    x_s[mine] = own_s[pl.ds(pl.multiple_of(col * share * own, share * own), share * own), :]

    for step in range(1, col_size):
        for k in range(CHUNKS):
            arrived(l_s.at[k, col - step, seq], l_recv.at[k, col - step, seq], col >= step)
            relay_left(k, col - step, True, False, col >= step)
            arrived(l_s.at[k, col + step, seq], l_recv.at[k, col + step, seq], col + step < col_size)
            relay_left(k, col + step, False, True, col + step < col_size)
        if step == 1:
            source_here = lax.rem(column_slot, col_size) == col
            for source in range(seq_size):
                kept = jnp.logical_and(source_here, seq == source)
                arrived(r_s.at[source], r_recv.at[source], jnp.logical_and(here, jnp.logical_not(kept)))
                ship(r_s.at[source], r_s.at[source], {"row": other_row}, r_recv.at[source], here)
    for offset in range(1, col_size):
        target = lax.rem(col + offset, col_size)
        ship(
            own_s.at[pl.ds(pl.multiple_of(target * share * own, share * own), share * own), :],
            x_s.at[mine],
            {"col": target},
            x_recv.at[mine],
        )
    ship(x_s.at[mine], x_s.at[mine], {"row": other_row}, x_recv.at[mine])

    for source in range(seq_size):
        arrived(r_s.at[source], r_recv.at[source], elsewhere)
    for t in range(2):
        right_s[t * right_steps * outer : (t + 1) * right_steps * outer, :] = jnp.concatenate(
            [r_s[source, :, t * span : (t + 1) * span] for source in range(seq_size)], axis=1
        )
    r_high, r_low = halves(right_s[...])
    r_both = jnp.concatenate([r_high, r_low], axis=1)

    for k in range(CHUNKS):
        for at in range(col_size):
            arrived(l_s.at[k, at, other_seq], l_recv.at[k, at, other_seq])

        def place_left(step, carry):
            at = pl.ds(pl.multiple_of(step * chunk, chunk), chunk)
            for source in range(seq_size):
                blocks = [l_s[k, t, source, at, :] for t in range(col_size)]
                for t in range(pairs):
                    for half in range(2):
                        lane = (2 * t + half) * own
                        line = jnp.concatenate([block[:, lane : lane + own] for block in blocks], axis=1)
                        place = source * span + half * groups + t * left_steps + step
                        left_s[k, pl.ds(pl.multiple_of(place * chunk, chunk), chunk), :] = line
            return carry

        lax.fori_loop(0, left_steps, place_left, 0, unroll=2)

        def outer_step(step, carry):
            pieces = [left_s[k, pl.ds(2 * step + t, LANES, stride=chunk), :] for t in range(2)]
            l_high, l_low = halves(jnp.concatenate(pieces, axis=1))
            product = mm(r_both, jnp.concatenate([l_high, l_high], axis=0)) + mm(r_high, l_low)
            p_high, p_low = halves(product)
            for t in range(2):
                high_s[k * chunk + 2 * step + t] = p_high[:, t * rows : (t + 1) * rows]
                low_s[k * chunk + 2 * step + t] = p_low[:, t * rows : (t + 1) * rows]
            return carry

        lax.fori_loop(0, chunk // 2, outer_step, 0)

    for offset in range(1, col_size):
        at = row * col_size + lax.rem(col + offset, col_size)
        arrived(x_s.at[at], x_recv.at[at])
        ship(x_s.at[at], x_s.at[at], {"row": other_row}, x_recv.at[at])

    t_high, t_low = halves(product_ref[...].T * (1.0 / total))
    t_both = jnp.concatenate([t_high, t_low], axis=0)
    c_high, c_low = halves(score_ref[...])
    c_both = jnp.concatenate([c_high, c_low], axis=0)

    def pair_step(step, carry):
        def block(ref):
            pieces = [
                ref[:, pl.ds(pl.multiple_of((2 * step + t) * outer, outer), outer), :].reshape(outer * outer, rows)
                for t in range(2)
            ]
            return jnp.concatenate(pieces, axis=1)

        joint = mm(t_both, block(high_s))
        update = joint[:channels] + (joint[channels:] + mm(t_high, block(low_s)))
        revised = jnp.concatenate([turned_s[2 * step + t] for t in range(2)], axis=1) + update
        center = revised - jnp.mean(revised, axis=0, keepdims=True)
        spread = jnp.mean(center * center, axis=0, keepdims=True)
        n_high, n_low = halves(center)
        turn = mm(c_both, n_high)
        logits = turn[:heads] + (turn[heads:] + mm(c_high, n_low))
        logits = logits / jnp.sqrt(spread + epsilon)
        for t in range(2):
            turned_s[2 * step + t] = revised[:, t * rows : (t + 1) * rows]
            logit_s[me, 2 * step + t] = logits[:, t * rows : (t + 1) * rows]
        return carry

    section = half_cols // CHUNKS

    def logits_of(slot, k):
        return logit_s.at[slot, pl.ds(k * section, section)], logit_recv.at[slot, k]

    for k in range(CHUNKS):
        lax.fori_loop(k * section // 2, (k + 1) * section // 2, pair_step, 0)
        place, sem = logits_of(me, k)
        for offset in range(1, col_size):
            ship(place, place, {"col": lax.rem(col + offset, col_size)}, sem)
        ship(place, place, {"seq": other_seq}, sem)

    def pass_on(k):
        for offset in range(1, col_size):
            place, sem = logits_of(lax.rem(col + offset, col_size) * seq_size + seq, k)
            arrived(place, sem)
            ship(place, place, {"seq": other_seq}, sem)

    def turn_out(column, carry):
        flat_revised[pl.ds(first_col + column, rows, stride=cols), :] = turned_s[column].T
        return carry

    lax.fori_loop(0, half_cols, turn_out, 0, unroll=2)
    half_pair = revised_ref.at[:, pl.ds(pl.multiple_of(first_col, half_cols), half_cols), :]
    pair_copy = pltpu.make_async_remote_copy(
        src_ref=half_pair,
        dst_ref=half_pair,
        send_sem=pair_sem.at[0],
        recv_sem=pair_sem.at[1],
        device_id={"seq": other_seq},
        device_id_type=mesh_ids,
    )
    pair_copy.start()
    pass_on(0)

    def spread_heads(matrix):
        width = matrix.shape[1] // heads
        zero = jnp.zeros((matrix.shape[0], width), f32)
        upper, lower = [], []
        for head in range(heads):
            piece = matrix[:, head * width : (head + 1) * width]
            upper += [piece, zero]
            lower += [zero, piece]
        return jnp.concatenate([jnp.concatenate(upper, axis=1), jnp.concatenate(lower, axis=1)], axis=0)

    g_high, g_low = halves(spread_heads(gate_ref[...]))
    g_twice = jnp.concatenate([g_high, g_high], axis=0)

    def gate_step(group, carry):
        at = pl.ds(pl.multiple_of(group * own, own), own)
        x_high, x_low = halves(x_s[pl.ds(row * col_size, col_size), at, :].reshape(rows, LANES))
        inner = mm(jnp.concatenate([x_high, x_low], axis=1), g_twice) + mm(x_high, g_low)
        gates_s[group] = jax.nn.sigmoid(inner)
        return carry

    lax.fori_loop(0, share, gate_step, 0)
    for k in range(1, CHUNKS - 1):
        pass_on(k)
    for at in range(col_size):
        arrived(x_s.at[other_row * col_size + at], x_recv.at[other_row * col_size + at])
    s_high, s_low = halves(spread_heads(source_ref[...]))
    s_twice = jnp.concatenate([s_high, s_high], axis=0)

    def value_step(group, carry):
        at = pl.ds(pl.multiple_of(group * own, own), own)
        x_high, x_low = halves(x_s[:, at, :].reshape(tokens_all, LANES))
        values = mm(jnp.concatenate([x_high, x_low], axis=1), s_twice) + mm(x_high, s_low)
        v_high, v_low = halves(values)
        v_high_s[group] = v_high
        v_low_s[group] = v_low
        return carry

    lax.fori_loop(0, share, value_step, 0)
    f_halves = halves(spread_heads(final_ref[...]))
    pass_on(CHUNKS - 1)
    for k in range(CHUNKS):
        for at in range(col_size):
            place, sem = logits_of(at * seq_size + other_seq, k)
            arrived(place, sem)

    logits = logit_s[...].reshape(tokens_all, heads, rows)
    powers = jnp.exp(logits - jnp.max(logits, axis=0)[None])
    weights = powers * (1.0 / jnp.sum(powers, axis=0))[None]
    weight_s[...] = weights.reshape(tokens_all * heads, rows)
    for head in range(heads):
        w_high, w_low = halves(weight_s[pl.ds(head, tokens_all, stride=heads), :].T)
        at = head % 2 * rows
        mixer_s[head // 2, at : at + rows, :] = w_high
        mixer_s[head // 2, 2 * rows + at : 2 * rows + at + rows, :] = w_low
    lane_head = lax.broadcasted_iota(jnp.int32, (rows, 2 * LANES), 1) % LANES
    upper_head = lane_head < LANES // 2

    for turn in range(share // 2):
        parts = []
        for p in range(heads // 2):
            lanes = slice(p * LANES, (p + 1) * LANES)
            v_high, v_low = (
                jnp.concatenate([ref[2 * turn + t, :, lanes] for t in range(2)], axis=1)
                for ref in (v_high_s, v_low_s)
            )
            joint = mm(mixer_s[p], v_high)
            full = joint[: 2 * rows] + (joint[2 * rows :] + mm(mixer_s[p, : 2 * rows, :], v_low))
            parts.append(jnp.where(upper_head, full[:rows], full[rows:]))
        mixed = []
        for t in range(2):
            line = jnp.concatenate([part[:, t * LANES : (t + 1) * LANES] for part in parts], axis=1)
            mixed.append(line * gates_s[2 * turn + t])
        result = nt3(halves(jnp.concatenate(mixed, axis=0)), f_halves)
        for t in range(2):
            part_s[:, 2 * turn + t] = result[t * rows : (t + 1) * rows].reshape(col_size, own, LANES)
        at = pl.ds(col * share + 2 * turn, 2)
        for offset in range(1, col_size):
            target = lax.rem(col + offset, col_size)
            ship(
                part_s.at[target, pl.ds(2 * turn, 2)],
                whole_s.at[at],
                {"col": target},
                part_recv.at[col, turn],
            )
        whole_s[at] = part_s[col, 2 * turn : 2 * turn + 2]

    for offset in range(1, col_size):
        source = lax.rem(col + offset, col_size)
        for turn in range(share // 2):
            arrived(whole_s.at[pl.ds(source * share + 2 * turn, 2)], part_recv.at[source, turn])
    for t in range(2):
        at = pl.ds(t * groups, groups)
        out_ref[at] = raw_ref[at] + whole_s[:, :, t * depth : (t + 1) * depth]

    for copy, condition in started:
        run(condition, copy.wait_send)
    pair_copy.wait_send()
    other_half = revised_ref.at[:, pl.ds(pl.multiple_of(other_seq * half_cols, half_cols), half_cols), :]
    arrived(other_half, pair_sem.at[1])


def twice(matrix):
    zero = jnp.zeros_like(matrix)
    return jnp.concatenate(
        [jnp.concatenate([matrix, zero], axis=1), jnp.concatenate([zero, matrix], axis=1)], axis=0
    )


FINISH_CUTS = 4


def finish_kernel(*refs):
    count = len(refs) // 2
    copies = []
    for source, target in zip(refs[:count], refs[count:-1]):
        share = source.shape[0] // FINISH_CUTS
        for cut in range(FINISH_CUTS):
            at = pl.ds(cut * share, share)
            copies.append(pltpu.make_async_copy(source.at[at], target.at[at], refs[-1].at[len(copies)]))
            copies[-1].start()
    for copy in copies:
        copy.wait()


def fast_path(
    alignment_tensor,
    residue_couplings,
    first_factor_matrix,
    second_factor_matrix,
    tensor_product_matrix,
    coupling_score_matrix,
    averaged_source_matrix,
    sigmoid_matrix,
    final_matrix,
):
    seqs, _, own, depth = alignment_tensor.shape
    rows, cols, channels = residue_couplings.shape
    outer = first_factor_matrix.shape[1]
    heads = coupling_score_matrix.shape[1]
    row_size, col_size, seq_size = (lax.axis_size(a) for a in ("row", "col", "seq"))
    blocks = row_size * col_size
    half_cols = cols // seq_size
    members = col_size * seq_size
    groups = seqs // 2
    wide = 2 * averaged_source_matrix.shape[1]
    share = groups // col_size
    vmem = pl.BlockSpec(memory_space=pltpu.VMEM)
    dma = pltpu.SemaphoreType.DMA
    arrays = (
        alignment_tensor.reshape(seqs, own, depth),
        residue_couplings,
        first_factor_matrix.T,
        second_factor_matrix.T,
        tensor_product_matrix,
        coupling_score_matrix.T,
        averaged_source_matrix,
        sigmoid_matrix,
        final_matrix.T,
    )
    alignment, couplings = pl.pallas_call(
        functools.partial(block_kernel, row_size, col_size, seq_size, heads),
        out_shape=(
            pltpu.VMEM((seqs, own, depth), f32),
            pltpu.VMEM((rows, cols, channels), f32),
        ),
        in_specs=[pl.BlockSpec(memory_space=pltpu.HBM)] * 9,
        out_specs=(vmem, vmem),
        scratch_shapes=[pltpu.VMEM(a.shape, f32) for a in arrays]
        + [
            dma((len(arrays),)),
            pltpu.VMEM((groups * own, LANES), f32),
            pltpu.VMEM((CHUNKS, col_size, seq_size, groups // (LANES // 2 // own) * outer // CHUNKS, LANES), f32),
            pltpu.VMEM((half_cols // 2 * outer, LANES), f32),
            pltpu.VMEM((seq_size, half_cols // 2 * outer, LANES), f32),
            pltpu.VMEM((CHUNKS, LANES * outer // CHUNKS, rows), f32),
            pltpu.VMEM((half_cols * outer, LANES), f32),
            pltpu.VMEM((outer, half_cols * outer, rows), bf16),
            pltpu.VMEM((outer, half_cols * outer, rows), bf16),
            pltpu.VMEM((half_cols, channels, rows), f32),
            pltpu.VMEM((blocks, share * own, LANES), f32),
            pltpu.VMEM((members, half_cols, heads, rows), f32),
            pltpu.VMEM((members * half_cols * heads, rows), f32),
            pltpu.VMEM((heads // 2, 4 * rows, members * half_cols), bf16),
            pltpu.VMEM((share, members * half_cols, wide), bf16),
            pltpu.VMEM((share, members * half_cols, wide), bf16),
            pltpu.VMEM((share, rows, wide), f32),
            pltpu.VMEM((col_size, share, own, LANES), f32),
            pltpu.VMEM((groups, own, LANES), f32),
            dma((128,)),
            dma((CHUNKS, col_size, seq_size)),
            dma((seq_size,)),
            dma((blocks,)),
            dma((members, CHUNKS)),
            dma((col_size, share // 2)),
            dma((2,)),
        ],
        compiler_params=pltpu.CompilerParams(
            collective_id=0, has_side_effects=True, vmem_limit_bytes=59 << 20
        ),
    )(*arrays)
    revised_alignment, revised_couplings = pl.pallas_call(
        finish_kernel,
        out_shape=(
            jax.ShapeDtypeStruct((seqs, own, depth), f32),
            jax.ShapeDtypeStruct((rows, cols, channels), f32),
        ),
        in_specs=[vmem] * 2,
        out_specs=(pl.BlockSpec(memory_space=pltpu.HBM),) * 2,
        scratch_shapes=[dma((2 * FINISH_CUTS,))],
        compiler_params=pltpu.CompilerParams(vmem_limit_bytes=12 << 20),
    )(alignment, couplings)
    return revised_alignment.reshape(alignment_tensor.shape), revised_couplings


def on_device(alignment_tensor, residue_couplings, first_factor_matrix, *rest):
    seqs, tiles, own, depth = alignment_tensor.shape
    rows, cols, channels = residue_couplings.shape
    row_size, col_size, seq_size = (lax.axis_size(a) for a in ("row", "col", "seq"))
    fits = (
        tiles == 1
        and rows == own * col_size == LANES
        and cols == own * seq_size
        and row_size * rows == col_size * cols
        and own % 16 == 0
        and seqs % 6 == 0
        and 2 * depth == channels == LANES
        and first_factor_matrix.shape[1] % (8 * CHUNKS) == 0
        and seqs % (4 * col_size) == 0
        and rest[3].shape[1] == 8 * LANES // 4
        and cols % (4 * CHUNKS) == 0
        and seq_size == row_size == 2
        and rest[2].shape[1] == 8 == own * own // LANES
        and seqs * seq_size <= LANES
        and seqs // 2 % (LANES // 2 // own) == 0
        and col_size > 2
    )
    path = fast_path if fits else general_path
    return path(alignment_tensor, residue_couplings, first_factor_matrix, *rest)


def solution(mesh):
    return jax.shard_map(
        on_device,
        mesh=mesh,
        in_specs=(
            P(("grp", "seq"), "row", "col", None),
            P(("grp", "row"), "col", None),
            P(),
            P(),
            P(),
            P(),
            P(),
            P(),
            P(),
        ),
        out_specs=(P(("grp", "seq"), "row", "col", None), P(("grp", "row"), "col", None)),
        check_vma=False,
    )
```

```python
import functools

import jax
import jax.numpy as jnp
from jax import lax
from jax.experimental import pallas as pl
from jax.experimental.pallas import tpu as pltpu
from jax.sharding import PartitionSpec as P

epsilon = 1e-05
exact_arithmetic = lax.Precision.HIGHEST


def broadcast(block, axis, holder):
    block = jnp.where(lax.axis_index(axis) == holder, block, jnp.zeros_like(block))
    return lax.psum(block, axis)


def standardize_entries(inputs):
    center = inputs - jnp.mean(inputs, axis=-1, keepdims=True)
    spread = jnp.mean(center * center, axis=-1, keepdims=True)
    return center / jnp.sqrt(spread + epsilon)


def pair_scores(pair_rows, coupling_score_matrix):
    return jnp.einsum(
        "ijc,ch->ihj",
        standardize_entries(pair_rows),
        coupling_score_matrix,
        precision=exact_arithmetic,
    )


def general_path(
    alignment_tensor,
    residue_couplings,
    first_factor_matrix,
    second_factor_matrix,
    tensor_product_matrix,
    coupling_score_matrix,
    averaged_source_matrix,
    sigmoid_matrix,
    final_matrix,
):
    shard_alignment_entries = alignment_tensor.shape[0]
    total_seqs = shard_alignment_entries * lax.axis_size("seq")
    coupling_lines = residue_couplings.shape[0]
    col_count = residue_couplings.shape[1]
    alignment_depth = alignment_tensor.shape[3]
    outer_width = first_factor_matrix.shape[1]
    head_count = coupling_score_matrix.shape[1]
    gathered_lines = lax.all_gather(alignment_tensor, "col", axis=2, tiled=True)
    alignment_tile_entries = gathered_lines.reshape(
        shard_alignment_entries, coupling_lines, alignment_depth
    )
    standardized_alignment = standardize_entries(alignment_tile_entries)
    first_factor_tile = jnp.einsum(
        "kgd,dl->kgl", standardized_alignment, first_factor_matrix, precision=exact_arithmetic
    )
    combined_matrix = jnp.concatenate([second_factor_matrix, averaged_source_matrix], axis=1)
    first_col = lax.axis_index("col") * col_count
    root_row = first_col // coupling_lines
    offset = first_col % coupling_lines
    raw_piece = lax.dynamic_slice_in_dim(alignment_tile_entries, offset, col_count, 1)
    raw_received = broadcast(raw_piece, "row", root_row)
    received = jnp.einsum(
        "pko,ol->pkl",
        standardize_entries(raw_received),
        combined_matrix,
        precision=exact_arithmetic,
    )
    second_factor_tile = received[:, :, :outer_width]
    averaged_sources = received[:, :, outer_width:].reshape(
        shard_alignment_entries, col_count, head_count, -1
    )
    block_rows = 16
    left_blocks = first_factor_tile.reshape(
        shard_alignment_entries, coupling_lines // block_rows, block_rows, outer_width
    ).transpose(1, 0, 2, 3)

    def outer_block(left_block):
        product = (
            jnp.einsum("sic,sje->ijce", left_block, second_factor_tile, precision=exact_arithmetic)
            / total_seqs
        )
        flat_prod = product.reshape(block_rows * col_count, -1)
        return jnp.dot(flat_prod, tensor_product_matrix, precision=exact_arithmetic).reshape(
            block_rows, col_count, -1
        )

    update = lax.map(outer_block, left_blocks).reshape(coupling_lines, col_count, -1)
    revised_couplings = residue_couplings + lax.psum(update, "seq")
    scores = pair_scores(revised_couplings, coupling_score_matrix)
    local_top = jnp.max(scores, axis=2)
    score_top = lax.pmax(local_top, "col")
    score_total = lax.psum(jnp.sum(jnp.exp(scores - score_top[:, :, None]), axis=2), "col")
    weights = jnp.exp(scores - score_top[:, :, None]) / score_total[:, :, None]
    mixed_rows = jnp.einsum(
        "ihj,sjhd->sihd", weights, averaged_sources, precision=exact_arithmetic
    ).reshape(shard_alignment_entries, coupling_lines, -1)
    summed = lax.psum_scatter(mixed_rows, "col", scatter_dimension=1, tiled=True)
    shard_standardized_alignment = standardize_entries(
        alignment_tensor.reshape(shard_alignment_entries, -1, alignment_depth)
    )
    sigmoid_factors = jax.nn.sigmoid(
        jnp.einsum(
            "pko,ol->pkl", shard_standardized_alignment, sigmoid_matrix, precision=exact_arithmetic
        )
    )
    coupling_increment = jnp.einsum(
        "snf,fc->snc", summed * sigmoid_factors, final_matrix, precision=exact_arithmetic
    )
    revised_alignment = alignment_tensor + coupling_increment.reshape(alignment_tensor.shape)
    return (revised_alignment, revised_couplings)


f32, bf16 = jnp.float32, jnp.bfloat16
LANES = 128
CHUNKS = 4
GATHERED = 8
PAIRED = 4


def halves(values):
    high = values.astype(bf16)
    return high, (values - high.astype(f32)).astype(bf16)


def mm(a, b):
    return jnp.dot(a, b, preferred_element_type=f32)


def mm3(a, b):
    (a_high, a_low), (b_high, b_low) = a, b
    return mm(a_high, b_high) + (mm(a_high, b_low) + mm(a_low, b_high))


def nt(a, b):
    return lax.dot_general(a, b, (((1,), (1,)), ((), ())), preferred_element_type=f32)


def nt3(a, b):
    (a_high, a_low), (b_high, b_low) = a, b
    return nt(a_high, b_high) + (nt(a_high, b_low) + nt(a_low, b_high))


def block_kernel(
    row_size,
    col_size,
    seq_size,
    heads,
    raw_in,
    pair_in,
    first_in,
    second_in,
    product_in,
    score_in,
    source_in,
    gate_in,
    final_in,
    out_ref,
    revised_ref,
    raw_ref,
    pair_ref,
    first_ref,
    second_ref,
    product_ref,
    score_ref,
    source_ref,
    gate_ref,
    final_ref,
    load_sem,
    own_s,
    l_s,
    r_own,
    hop_s,
    r_s,
    left_s,
    right_s,
    high_s,
    low_s,
    product_s,
    turned_s,
    x_s,
    logit_s,
    weight_s,
    mixer_s,
    v_high_s,
    v_low_s,
    gates_s,
    part_s,
    whole_s,
    send_sem,
    l_recv,
    r_recv,
    hop_recv,
    x_recv,
    logit_recv,
    part_recv,
    pair_sem,
):
    loads = []
    for source, place in (
        (raw_in, raw_ref),
        (second_in, second_ref),
        (first_in, first_ref),
        (pair_in, pair_ref),
        (product_in, product_ref),
        (source_in, source_ref),
        (gate_in, gate_ref),
        (score_in, score_ref),
        (final_in, final_ref),
    ):
        loads.append(pltpu.make_async_copy(source, place, load_sem.at[len(loads)]))
        loads[-1].start()
    seqs, own, depth = raw_ref.shape
    groups = seqs // 2
    rows, cols, channels = revised_ref.shape
    outer = first_ref.shape[0]
    half_cols = cols // seq_size
    total = seqs * seq_size
    wide = 2 * source_ref.shape[1]
    members = col_size * seq_size
    tokens_all = members * half_cols
    share = groups // col_size
    row, col, seq = (lax.axis_index(a) for a in ("row", "col", "seq"))
    other_row, other_seq = 1 - row, 1 - seq
    me = col * seq_size + seq
    mine = row * col_size + col
    mesh_ids = pl.DeviceIdType.MESH

    barrier = pltpu.get_barrier_semaphore()

    def member(offset):
        other = lax.rem(me + offset, members)
        return {"col": other // seq_size, "seq": lax.rem(other, seq_size)}

    for offset in range(1, members):
        pl.semaphore_signal(barrier, inc=1, device_id=member(offset), device_id_type=mesh_ids)
    pl.semaphore_signal(barrier, inc=1, device_id={"row": other_row}, device_id_type=mesh_ids)

    for load in loads[:3]:
        load.wait()

    def normalize(step, carry):
        parts = []
        for t in range(2):
            part = standardize_entries(raw_ref[step + t * groups])
            parts.append(part)
        at = pl.ds(pl.multiple_of(step * own, own), own)
        own_s[at, :] = jnp.concatenate(parts, axis=-1)
        return carry

    lax.fori_loop(0, groups, normalize, 0, unroll=4)

    first = halves(twice(first_ref[...]))
    second = halves(twice(second_ref[...]))
    span = LANES // 2
    room = jnp.zeros((outer, span - seqs), f32)
    right_steps = half_cols // 2

    def project_right(step, carry):
        parts = []
        for t in range(2):
            tokens = own_s[pl.ds(t * right_steps + step, groups, stride=own), :]
            result = nt3(second, halves(tokens))
            parts += [result[:outer], result[outer:], room]
        r_own[pl.ds(pl.multiple_of(step * outer, outer), outer), :] = jnp.concatenate(parts, axis=1)
        return carry

    lax.fori_loop(0, right_steps, project_right, 0, unroll=4)

    started = []

    def run(condition, action):
        if condition is None:
            action()
        else:
            pl.when(condition)(action)

    def both(a, b):
        return b if a is None else (a if b is None else jnp.logical_and(a, b))

    def ship(source, place, target, sem, condition=None):
        copy = pltpu.make_async_remote_copy(
            src_ref=source,
            dst_ref=place,
            send_sem=send_sem.at[len(started)],
            recv_sem=sem,
            device_id=target,
            device_id_type=mesh_ids,
        )
        started.append((copy, condition))
        run(condition, copy.start)

    def arrived(place, sem, condition=None):
        copy = pltpu.make_async_remote_copy(
            src_ref=place,
            dst_ref=place,
            send_sem=send_sem.at[0],
            recv_sem=sem,
            device_id={"row": other_row},
            device_id_type=mesh_ids,
        )
        run(condition, copy.wait_recv)

    pl.semaphore_wait(barrier, members)
    column_slot = me
    here = column_slot // col_size == row
    elsewhere = jnp.logical_not(here)
    other_mine = other_row * col_size + col
    cut = right_steps * outer // CHUNKS
    straight, crossed = range(CHUNKS // 2), range(CHUNKS // 2, CHUNKS)

    def right_target(block):
        return {"col": block // seq_size, "seq": lax.rem(block, seq_size)}

    own_right = column_slot == mine
    own_crossed = column_slot == other_mine
    for j in crossed:
        at = pl.ds(j * cut, cut)
        ship(r_own.at[at], hop_s.at[at], {"row": other_row}, hop_recv.at[j])
    for j in straight:
        at = pl.ds(j * cut, cut)
        ship(
            r_own.at[at],
            r_s.at[seq, at],
            right_target(mine),
            r_recv.at[seq, j],
            jnp.logical_not(own_right),
        )

    chunk = outer // CHUNKS
    pairs = LANES // 2 // own
    left_steps = groups // pairs

    def project_left(step, carry):
        parts = []
        for t in range(pairs):
            at = pl.ds(pl.multiple_of((t * left_steps + step) * own, own), own)
            result = nt3(first, halves(own_s[at, :]))
            parts += [result[:outer], result[outer:]]
        line = jnp.concatenate(parts, axis=1)
        at = pl.ds(pl.multiple_of(step * chunk, chunk), chunk)
        for k in range(CHUNKS):
            l_s[k, col, seq, at, :] = line[k * chunk : (k + 1) * chunk]
        return carry

    lax.fori_loop(0, left_steps, project_left, 0, unroll=4)

    def relay_left(k, at, rightward, leftward, exists):
        place, sem = l_s.at[k, at, seq], l_recv.at[k, at, seq]
        if rightward:
            ship(place, place, {"col": col + 1}, sem, both(exists, col < col_size - 1))
        if leftward:
            ship(place, place, {"col": col - 1}, sem, both(exists, col > 0))
        ship(place, place, {"seq": other_seq}, sem, exists)

    def relay(place_of, k, distance):
        for sign in (-1, 1):
            at = col + sign * distance
            exists = at >= 0 if sign < 0 else at < col_size
            onward = at - sign * (distance + 1)
            inside = onward < col_size if sign < 0 else onward >= 0
            place, sem = place_of(k, at)
            if distance:
                arrived(place, sem, exists)
            ship(place, place, {"col": onward}, sem, both(exists, inside) if distance else inside)
            if distance or sign < 0:
                ship(place, place, {"seq": other_seq}, sem, exists if distance else None)

    def left_of(k, at):
        return l_s.at[k, at, seq], l_recv.at[k, at, seq]

    def left_slot(slot):
        for distance in range(1, col_size):
            k = slot - distance + 1
            if 0 <= k < CHUNKS:
                relay(left_of, k, distance)
        if slot + 2 < CHUNKS:
            relay(left_of, slot + 2, 0)

    relay(left_of, 0, 0)
    relay(left_of, 1, 0)

    for load in loads[3:]:
        load.wait()
    first_col = seq * half_cols
    flat_pair = pair_ref.reshape(rows * cols, channels)
    flat_revised = revised_ref.reshape(rows * cols, channels)

    def turn_in(column, carry):
        turned_s[column] = flat_pair[pl.ds(first_col + column, rows, stride=cols), :].T
        return carry

    lax.fori_loop(0, half_cols // 2, turn_in, 0, unroll=2)

    @pl.when(own_right)
    def _():
        for j in straight:
            r_s[seq, j * cut : (j + 1) * cut] = r_own[j * cut : (j + 1) * cut]

    for j in crossed:
        at = pl.ds(j * cut, cut)
        arrived(hop_s.at[at], hop_recv.at[j])
        ship(
            hop_s.at[at],
            r_s.at[seq, at],
            right_target(other_mine),
            r_recv.at[seq, j],
            jnp.logical_not(own_crossed),
        )

    @pl.when(own_crossed)
    def _():
        for j in crossed:
            r_s[seq, j * cut : (j + 1) * cut] = hop_s[j * cut : (j + 1) * cut]

    left_slot(0)
    source_here = lax.rem(column_slot, col_size) == col
    for js, kind in ((straight, here), (crossed, elsewhere)):
        for j in js:
            for source in range(seq_size):
                kept = jnp.logical_and(source_here, seq == source)
                place, sem = r_s.at[source, pl.ds(j * cut, cut)], r_recv.at[source, j]
                arrived(place, sem, jnp.logical_and(kind, jnp.logical_not(kept)))
                ship(place, place, {"row": other_row}, sem, kind)
    blank = jnp.zeros(((span - seqs) * chunk, rows), f32)
    for k in range(CHUNKS):
        for source in range(seq_size):
            left_s[k, (source * span + seqs) * chunk : (source + 1) * span * chunk, :] = blank
    lax.fori_loop(half_cols // 2, half_cols, turn_in, 0, unroll=2)
    left_slot(1)
    t_high, t_low = halves(product_ref[...].T * (1.0 / total))
    product_s[...] = jnp.concatenate([t_high, t_low], axis=0)
    c_high, c_low = halves(score_ref[...])
    c_both = jnp.concatenate([c_high, c_low], axis=0)
    x_s[mine] = own_s[pl.ds(pl.multiple_of(col * share * own, share * own), share * own), :]
    left_slot(2)

    for js, kind in ((straight, elsewhere), (crossed, here)):
        for j in js:
            for source in range(seq_size):
                arrived(r_s.at[source, pl.ds(j * cut, cut)], r_recv.at[source, j], kind)
    for t in range(2):
        right_s[t * right_steps * outer : (t + 1) * right_steps * outer, :] = jnp.concatenate(
            [r_s[source, :, t * span : (t + 1) * span] for source in range(seq_size)], axis=1
        )
    r_high, r_low = halves(right_s[...])
    r_both = jnp.concatenate([r_high, r_low], axis=1)

    def outer_chunk(k):
        for at in range(col_size):
            arrived(l_s.at[k, at, other_seq], l_recv.at[k, at, other_seq])

        def place_left(step, carry):
            at = pl.ds(pl.multiple_of(step * chunk, chunk), chunk)
            for source in range(seq_size):
                blocks = [l_s[k, t, source, at, :] for t in range(col_size)]
                for t in range(pairs):
                    for half in range(2):
                        lane = (2 * t + half) * own
                        line = jnp.concatenate([block[:, lane : lane + own] for block in blocks], axis=1)
                        place = source * span + half * groups + t * left_steps + step
                        left_s[k, pl.ds(pl.multiple_of(place * chunk, chunk), chunk), :] = line
            return carry

        lax.fori_loop(0, left_steps, place_left, 0, unroll=2)

        def outer_step(step, carry):
            pieces = [left_s[k, pl.ds(2 * step + t, LANES, stride=chunk), :] for t in range(2)]
            l_high, l_low = halves(jnp.concatenate(pieces, axis=1))
            product = mm(r_both, jnp.concatenate([l_high, l_high], axis=0)) + mm(r_high, l_low)
            p_high, p_low = halves(product)
            for t in range(2):
                high_s[2 * step + t] = p_high[:, t * rows : (t + 1) * rows]
                low_s[2 * step + t] = p_low[:, t * rows : (t + 1) * rows]
            return carry

        lax.fori_loop(0, chunk // 2, outer_step, 0, unroll=2)

    def project(k, step):
        def block(ref):
            pieces = [
                ref[:, pl.ds(pl.multiple_of((2 * step + t) * outer, outer), outer), :].reshape(chunk * outer, rows)
                for t in range(2)
            ]
            return jnp.concatenate(pieces, axis=1)

        t_both = product_s[:, k * chunk * outer : (k + 1) * chunk * outer]
        joint = mm(t_both, block(high_s))
        update = joint[:channels] + (joint[channels:] + mm(t_both[:channels], block(low_s)))
        return jnp.concatenate([turned_s[2 * step + t] for t in range(2)], axis=1) + update

    for k in range(CHUNKS - 1):
        outer_chunk(k)
        left_slot(k + CHUNKS - 1)

        def gather_step(turn, carry):
            steps = [GATHERED * turn + u for u in range(GATHERED)]
            for step, revised in [(step, project(k, step)) for step in steps]:
                for t in range(2):
                    turned_s[2 * step + t] = revised[:, t * rows : (t + 1) * rows]
            return carry

        lax.fori_loop(0, half_cols // 2 // GATHERED, gather_step, 0)
    for offset in range(1, col_size):
        target = lax.rem(col + offset, col_size)
        ship(
            own_s.at[pl.ds(pl.multiple_of(target * share * own, share * own), share * own), :],
            x_s.at[mine],
            {"col": target},
            x_recv.at[mine],
        )
    ship(x_s.at[mine], x_s.at[mine], {"row": other_row}, x_recv.at[mine])
    outer_chunk(CHUNKS - 1)

    def pair_step(turn, carry):
        steps = [PAIRED * turn + u for u in range(PAIRED)]
        results = []
        for step in steps:
            revised = project(CHUNKS - 1, step)
            center = revised - jnp.mean(revised, axis=0, keepdims=True)
            spread = jnp.mean(center * center, axis=0, keepdims=True)
            n_high, n_low = halves(center)
            turned = mm(c_both, n_high)
            logits = turned[:heads] + (turned[heads:] + mm(c_high, n_low))
            results.append((step, revised, logits / jnp.sqrt(spread + epsilon)))
        for step, revised, logits in results:
            for t in range(2):
                turned_s[2 * step + t] = revised[:, t * rows : (t + 1) * rows]
                logit_s[me, 2 * step + t] = logits[:, t * rows : (t + 1) * rows]
        return carry

    section = half_cols // CHUNKS

    def logits_of(k, at):
        slot = at * seq_size + seq
        return logit_s.at[slot, pl.ds(k * section, section)], logit_recv.at[slot, k]

    def logit_slot(slot):
        for distance in range(1, col_size):
            k = slot - distance + 1
            if 0 <= k < CHUNKS:
                relay(logits_of, k, distance)

    for k in range(CHUNKS):
        lax.fori_loop(k * section // 2 // PAIRED, (k + 1) * section // 2 // PAIRED, pair_step, 0)
        relay(logits_of, k, 0)
    for offset in range(1, col_size):
        at = row * col_size + lax.rem(col + offset, col_size)
        arrived(x_s.at[at], x_recv.at[at])
        ship(x_s.at[at], x_s.at[at], {"row": other_row}, x_recv.at[at])
    logit_slot(0)

    def turn_out(column, carry):
        flat_revised[pl.ds(first_col + column, rows, stride=cols), :] = turned_s[column].T
        return carry

    lax.fori_loop(0, half_cols, turn_out, 0, unroll=2)
    half_pair = revised_ref.at[:, pl.ds(pl.multiple_of(first_col, half_cols), half_cols), :]
    pair_copy = pltpu.make_async_remote_copy(
        src_ref=half_pair,
        dst_ref=half_pair,
        send_sem=pair_sem.at[0],
        recv_sem=pair_sem.at[1],
        device_id={"seq": other_seq},
        device_id_type=mesh_ids,
    )
    pair_copy.start()
    logit_slot(1)
    logit_slot(2)

    def spread_heads(matrix):
        width = matrix.shape[1] // heads
        zero = jnp.zeros((matrix.shape[0], width), f32)
        upper, lower = [], []
        for head in range(heads):
            piece = matrix[:, head * width : (head + 1) * width]
            upper += [piece, zero]
            lower += [zero, piece]
        return jnp.concatenate([jnp.concatenate(upper, axis=1), jnp.concatenate(lower, axis=1)], axis=0)

    g_high, g_low = halves(spread_heads(gate_ref[...]))
    g_twice = jnp.concatenate([g_high, g_high], axis=0)

    def gate_step(group, carry):
        at = pl.ds(pl.multiple_of(group * own, own), own)
        x_high, x_low = halves(x_s[pl.ds(row * col_size, col_size), at, :].reshape(rows, LANES))
        inner = mm(jnp.concatenate([x_high, x_low], axis=1), g_twice) + mm(x_high, g_low)
        gates_s[group] = jax.nn.sigmoid(inner)
        return carry

    lax.fori_loop(0, share, gate_step, 0)
    logit_slot(3)
    for at in range(col_size):
        arrived(x_s.at[other_row * col_size + at], x_recv.at[other_row * col_size + at])
    s_high, s_low = halves(spread_heads(source_ref[...]))
    s_twice = jnp.concatenate([s_high, s_high], axis=0)

    def value_step(group, carry):
        at = pl.ds(pl.multiple_of(group * own, own), own)
        x_high, x_low = halves(x_s[:, at, :].reshape(tokens_all, LANES))
        values = mm(jnp.concatenate([x_high, x_low], axis=1), s_twice) + mm(x_high, s_low)
        v_high, v_low = halves(values)
        v_high_s[group] = v_high
        v_low_s[group] = v_low
        return carry

    lax.fori_loop(0, share, value_step, 0)
    f_halves = halves(spread_heads(final_ref[...]))
    for slot in range(4, CHUNKS + col_size - 2):
        logit_slot(slot)
    for k in range(CHUNKS):
        for at in range(col_size):
            slot = at * seq_size + other_seq
            arrived(logit_s.at[slot, pl.ds(k * section, section)], logit_recv.at[slot, k])

    logits = logit_s[...].reshape(tokens_all, heads, rows)
    powers = jnp.exp(logits - jnp.max(logits, axis=0)[None])
    weights = powers * (1.0 / jnp.sum(powers, axis=0))[None]
    weight_s[...] = weights.reshape(tokens_all * heads, rows)
    for head in range(heads):
        w_high, w_low = halves(weight_s[pl.ds(head, tokens_all, stride=heads), :].T)
        at = head % 2 * rows
        mixer_s[head // 2, at : at + rows, :] = w_high
        mixer_s[head // 2, 2 * rows + at : 2 * rows + at + rows, :] = w_low
    lane_head = lax.broadcasted_iota(jnp.int32, (rows, 2 * LANES), 1) % LANES
    upper_head = lane_head < LANES // 2

    for turn in range(share // 2):
        parts = []
        for p in range(heads // 2):
            lanes = slice(p * LANES, (p + 1) * LANES)
            v_high, v_low = (
                jnp.concatenate([ref[2 * turn + t, :, lanes] for t in range(2)], axis=1)
                for ref in (v_high_s, v_low_s)
            )
            joint = mm(mixer_s[p], v_high)
            full = joint[: 2 * rows] + (joint[2 * rows :] + mm(mixer_s[p, : 2 * rows, :], v_low))
            parts.append(jnp.where(upper_head, full[:rows], full[rows:]))
        mixed = []
        for t in range(2):
            line = jnp.concatenate([part[:, t * LANES : (t + 1) * LANES] for part in parts], axis=1)
            mixed.append(line * gates_s[2 * turn + t])
        result = nt3(halves(jnp.concatenate(mixed, axis=0)), f_halves)
        for t in range(2):
            part_s[:, 2 * turn + t] = result[t * rows : (t + 1) * rows].reshape(col_size, own, LANES)
        at = pl.ds(col * share + 2 * turn, 2)
        for offset in range(1, col_size):
            target = lax.rem(col + offset, col_size)
            ship(
                part_s.at[target, pl.ds(2 * turn, 2)],
                whole_s.at[at],
                {"col": target},
                part_recv.at[col, turn],
            )
        whole_s[at] = part_s[col, 2 * turn : 2 * turn + 2]

    for offset in range(1, col_size):
        source = lax.rem(col + offset, col_size)
        for turn in range(share // 2):
            arrived(whole_s.at[pl.ds(source * share + 2 * turn, 2)], part_recv.at[source, turn])
    for t in range(2):
        at = pl.ds(t * groups, groups)
        out_ref[at] = raw_ref[at] + whole_s[:, :, t * depth : (t + 1) * depth]

    for copy, condition in started:
        run(condition, copy.wait_send)
    pair_copy.wait_send()
    other_half = revised_ref.at[:, pl.ds(pl.multiple_of(other_seq * half_cols, half_cols), half_cols), :]
    arrived(other_half, pair_sem.at[1])


def twice(matrix):
    zero = jnp.zeros_like(matrix)
    return jnp.concatenate(
        [jnp.concatenate([matrix, zero], axis=1), jnp.concatenate([zero, matrix], axis=1)], axis=0
    )


FINISH_CUTS = 4


def finish_kernel(*refs):
    count = len(refs) // 2
    copies = []
    for source, target in zip(refs[:count], refs[count:-1]):
        share = source.shape[0] // FINISH_CUTS
        for cut in range(FINISH_CUTS):
            at = pl.ds(cut * share, share)
            copies.append(pltpu.make_async_copy(source.at[at], target.at[at], refs[-1].at[len(copies)]))
            copies[-1].start()
    for copy in copies:
        copy.wait()


def fast_path(
    alignment_tensor,
    residue_couplings,
    first_factor_matrix,
    second_factor_matrix,
    tensor_product_matrix,
    coupling_score_matrix,
    averaged_source_matrix,
    sigmoid_matrix,
    final_matrix,
):
    seqs, _, own, depth = alignment_tensor.shape
    rows, cols, channels = residue_couplings.shape
    outer = first_factor_matrix.shape[1]
    heads = coupling_score_matrix.shape[1]
    row_size, col_size, seq_size = (lax.axis_size(a) for a in ("row", "col", "seq"))
    blocks = row_size * col_size
    half_cols = cols // seq_size
    members = col_size * seq_size
    groups = seqs // 2
    wide = 2 * averaged_source_matrix.shape[1]
    share = groups // col_size
    vmem = pl.BlockSpec(memory_space=pltpu.VMEM)
    dma = pltpu.SemaphoreType.DMA
    arrays = (
        alignment_tensor.reshape(seqs, own, depth),
        residue_couplings,
        first_factor_matrix.T,
        second_factor_matrix.T,
        tensor_product_matrix,
        coupling_score_matrix.T,
        averaged_source_matrix,
        sigmoid_matrix,
        final_matrix.T,
    )
    alignment, couplings = pl.pallas_call(
        functools.partial(block_kernel, row_size, col_size, seq_size, heads),
        out_shape=(
            pltpu.VMEM((seqs, own, depth), f32),
            pltpu.VMEM((rows, cols, channels), f32),
        ),
        in_specs=[pl.BlockSpec(memory_space=pltpu.HBM)] * 9,
        out_specs=(vmem, vmem),
        scratch_shapes=[pltpu.VMEM(a.shape, f32) for a in arrays]
        + [
            dma((len(arrays),)),
            pltpu.VMEM((groups * own, LANES), f32),
            pltpu.VMEM((CHUNKS, col_size, seq_size, groups // (LANES // 2 // own) * outer // CHUNKS, LANES), f32),
            pltpu.VMEM((half_cols // 2 * outer, LANES), f32),
            pltpu.VMEM((half_cols // 2 * outer, LANES), f32),
            pltpu.VMEM((seq_size, half_cols // 2 * outer, LANES), f32),
            pltpu.VMEM((CHUNKS, LANES * outer // CHUNKS, rows), f32),
            pltpu.VMEM((half_cols * outer, LANES), f32),
            pltpu.VMEM((outer // CHUNKS, half_cols * outer, rows), bf16),
            pltpu.VMEM((outer // CHUNKS, half_cols * outer, rows), bf16),
            pltpu.VMEM((2 * channels, outer * outer), bf16),
            pltpu.VMEM((half_cols, channels, rows), f32),
            pltpu.VMEM((blocks, share * own, LANES), f32),
            pltpu.VMEM((members, half_cols, heads, rows), f32),
            pltpu.VMEM((members * half_cols * heads, rows), f32),
            pltpu.VMEM((heads // 2, 4 * rows, members * half_cols), bf16),
            pltpu.VMEM((share, members * half_cols, wide), bf16),
            pltpu.VMEM((share, members * half_cols, wide), bf16),
            pltpu.VMEM((share, rows, wide), f32),
            pltpu.VMEM((col_size, share, own, LANES), f32),
            pltpu.VMEM((groups, own, LANES), f32),
            dma((192,)),
            dma((CHUNKS, col_size, seq_size)),
            dma((seq_size, CHUNKS)),
            dma((CHUNKS,)),
            dma((blocks,)),
            dma((members, CHUNKS)),
            dma((col_size, share // 2)),
            dma((2,)),
        ],
        compiler_params=pltpu.CompilerParams(
            collective_id=0, has_side_effects=True, vmem_limit_bytes=59 << 20
        ),
    )(*arrays)
    revised_alignment, revised_couplings = pl.pallas_call(
        finish_kernel,
        out_shape=(
            jax.ShapeDtypeStruct((seqs, own, depth), f32),
            jax.ShapeDtypeStruct((rows, cols, channels), f32),
        ),
        in_specs=[vmem] * 2,
        out_specs=(pl.BlockSpec(memory_space=pltpu.HBM),) * 2,
        scratch_shapes=[dma((2 * FINISH_CUTS,))],
        compiler_params=pltpu.CompilerParams(vmem_limit_bytes=12 << 20),
    )(alignment, couplings)
    return revised_alignment.reshape(alignment_tensor.shape), revised_couplings


def on_device(alignment_tensor, residue_couplings, first_factor_matrix, *rest):
    seqs, tiles, own, depth = alignment_tensor.shape
    rows, cols, channels = residue_couplings.shape
    row_size, col_size, seq_size = (lax.axis_size(a) for a in ("row", "col", "seq"))
    fits = (
        tiles == 1
        and rows == own * col_size == LANES
        and cols == own * seq_size
        and row_size * rows == col_size * cols
        and own % 16 == 0
        and seqs % 6 == 0
        and 2 * depth == channels == LANES
        and first_factor_matrix.shape[1] % (8 * CHUNKS) == 0
        and seqs % (4 * col_size) == 0
        and rest[3].shape[1] == 8 * LANES // 4
        and cols % (4 * CHUNKS) == 0
        and seq_size == row_size == 2
        and rest[2].shape[1] == 8 == own * own // LANES
        and seqs * seq_size <= LANES
        and seqs // 2 % (LANES // 2 // own) == 0
        and col_size == CHUNKS
    )
    path = fast_path if fits else general_path
    return path(alignment_tensor, residue_couplings, first_factor_matrix, *rest)


def solution(mesh):
    return jax.shard_map(
        on_device,
        mesh=mesh,
        in_specs=(
            P(("grp", "seq"), "row", "col", None),
            P(("grp", "row"), "col", None),
            P(),
            P(),
            P(),
            P(),
            P(),
            P(),
            P(),
        ),
        out_specs=(P(("grp", "seq"), "row", "col", None), P(("grp", "row"), "col", None)),
        check_vma=False,
    )
```

```python
import functools

import jax
import jax.numpy as jnp
from jax import lax
from jax.experimental import pallas as pl
from jax.experimental.pallas import tpu as pltpu
from jax.sharding import PartitionSpec as P

epsilon = 1e-05
exact_arithmetic = lax.Precision.HIGHEST


def broadcast(block, axis, holder):
    block = jnp.where(lax.axis_index(axis) == holder, block, jnp.zeros_like(block))
    return lax.psum(block, axis)


def standardize_entries(inputs):
    center = inputs - jnp.mean(inputs, axis=-1, keepdims=True)
    spread = jnp.mean(center * center, axis=-1, keepdims=True)
    return center / jnp.sqrt(spread + epsilon)


def pair_scores(pair_rows, coupling_score_matrix):
    return jnp.einsum(
        "ijc,ch->ihj",
        standardize_entries(pair_rows),
        coupling_score_matrix,
        precision=exact_arithmetic,
    )


def general_path(
    alignment_tensor,
    residue_couplings,
    first_factor_matrix,
    second_factor_matrix,
    tensor_product_matrix,
    coupling_score_matrix,
    averaged_source_matrix,
    sigmoid_matrix,
    final_matrix,
):
    shard_alignment_entries = alignment_tensor.shape[0]
    total_seqs = shard_alignment_entries * lax.axis_size("seq")
    coupling_lines = residue_couplings.shape[0]
    col_count = residue_couplings.shape[1]
    alignment_depth = alignment_tensor.shape[3]
    outer_width = first_factor_matrix.shape[1]
    head_count = coupling_score_matrix.shape[1]
    gathered_lines = lax.all_gather(alignment_tensor, "col", axis=2, tiled=True)
    alignment_tile_entries = gathered_lines.reshape(
        shard_alignment_entries, coupling_lines, alignment_depth
    )
    standardized_alignment = standardize_entries(alignment_tile_entries)
    first_factor_tile = jnp.einsum(
        "kgd,dl->kgl", standardized_alignment, first_factor_matrix, precision=exact_arithmetic
    )
    combined_matrix = jnp.concatenate([second_factor_matrix, averaged_source_matrix], axis=1)
    first_col = lax.axis_index("col") * col_count
    root_row = first_col // coupling_lines
    offset = first_col % coupling_lines
    raw_piece = lax.dynamic_slice_in_dim(alignment_tile_entries, offset, col_count, 1)
    raw_received = broadcast(raw_piece, "row", root_row)
    received = jnp.einsum(
        "pko,ol->pkl",
        standardize_entries(raw_received),
        combined_matrix,
        precision=exact_arithmetic,
    )
    second_factor_tile = received[:, :, :outer_width]
    averaged_sources = received[:, :, outer_width:].reshape(
        shard_alignment_entries, col_count, head_count, -1
    )
    block_rows = 16
    left_blocks = first_factor_tile.reshape(
        shard_alignment_entries, coupling_lines // block_rows, block_rows, outer_width
    ).transpose(1, 0, 2, 3)

    def outer_block(left_block):
        product = (
            jnp.einsum("sic,sje->ijce", left_block, second_factor_tile, precision=exact_arithmetic)
            / total_seqs
        )
        flat_prod = product.reshape(block_rows * col_count, -1)
        return jnp.dot(flat_prod, tensor_product_matrix, precision=exact_arithmetic).reshape(
            block_rows, col_count, -1
        )

    update = lax.map(outer_block, left_blocks).reshape(coupling_lines, col_count, -1)
    revised_couplings = residue_couplings + lax.psum(update, "seq")
    scores = pair_scores(revised_couplings, coupling_score_matrix)
    local_top = jnp.max(scores, axis=2)
    score_top = lax.pmax(local_top, "col")
    score_total = lax.psum(jnp.sum(jnp.exp(scores - score_top[:, :, None]), axis=2), "col")
    weights = jnp.exp(scores - score_top[:, :, None]) / score_total[:, :, None]
    mixed_rows = jnp.einsum(
        "ihj,sjhd->sihd", weights, averaged_sources, precision=exact_arithmetic
    ).reshape(shard_alignment_entries, coupling_lines, -1)
    summed = lax.psum_scatter(mixed_rows, "col", scatter_dimension=1, tiled=True)
    shard_standardized_alignment = standardize_entries(
        alignment_tensor.reshape(shard_alignment_entries, -1, alignment_depth)
    )
    sigmoid_factors = jax.nn.sigmoid(
        jnp.einsum(
            "pko,ol->pkl", shard_standardized_alignment, sigmoid_matrix, precision=exact_arithmetic
        )
    )
    coupling_increment = jnp.einsum(
        "snf,fc->snc", summed * sigmoid_factors, final_matrix, precision=exact_arithmetic
    )
    revised_alignment = alignment_tensor + coupling_increment.reshape(alignment_tensor.shape)
    return (revised_alignment, revised_couplings)


f32, bf16 = jnp.float32, jnp.bfloat16
LANES = 128
CHUNKS = 4
LEFT_REACH = 1
LOGIT_REACH = 1
GATHERED = 8
PAIRED = 4


def halves(values):
    high = values.astype(bf16)
    return high, (values - high.astype(f32)).astype(bf16)


def mm(a, b):
    return jnp.dot(a, b, preferred_element_type=f32)


def mm3(a, b):
    (a_high, a_low), (b_high, b_low) = a, b
    return mm(a_high, b_high) + (mm(a_high, b_low) + mm(a_low, b_high))


def nt(a, b):
    return lax.dot_general(a, b, (((1,), (1,)), ((), ())), preferred_element_type=f32)


def nt3(a, b):
    (a_high, a_low), (b_high, b_low) = a, b
    return nt(a_high, b_high) + (nt(a_high, b_low) + nt(a_low, b_high))


def block_kernel(
    row_size,
    col_size,
    seq_size,
    heads,
    raw_in,
    pair_in,
    first_in,
    second_in,
    product_in,
    score_in,
    source_in,
    gate_in,
    final_in,
    out_ref,
    revised_ref,
    raw_ref,
    pair_ref,
    first_ref,
    second_ref,
    product_ref,
    score_ref,
    source_ref,
    gate_ref,
    final_ref,
    load_sem,
    own_s,
    l_s,
    spread_s,
    r_own,
    hop_s,
    r_s,
    left_s,
    right_s,
    high_s,
    low_s,
    product_s,
    turned_s,
    x_s,
    logit_s,
    weight_s,
    mixer_s,
    v_high_s,
    v_low_s,
    gates_s,
    part_s,
    whole_s,
    send_sem,
    l_recv,
    r_recv,
    hop_recv,
    x_recv,
    logit_recv,
    part_recv,
    pair_sem,
):
    loads = []
    for source, place in (
        (raw_in, raw_ref),
        (second_in, second_ref),
        (first_in, first_ref),
        (pair_in, pair_ref),
        (product_in, product_ref),
        (source_in, source_ref),
        (gate_in, gate_ref),
        (score_in, score_ref),
        (final_in, final_ref),
    ):
        loads.append(pltpu.make_async_copy(source, place, load_sem.at[len(loads)]))
        loads[-1].start()
    seqs, own, depth = raw_ref.shape
    groups = seqs // 2
    rows, cols, channels = revised_ref.shape
    outer = first_ref.shape[0]
    half_cols = cols // seq_size
    total = seqs * seq_size
    wide = 2 * source_ref.shape[1]
    members = col_size * seq_size
    tokens_all = members * half_cols
    share = groups // col_size
    row, col, seq = (lax.axis_index(a) for a in ("row", "col", "seq"))
    other_row, other_seq = 1 - row, 1 - seq
    me = col * seq_size + seq
    mine = row * col_size + col
    mesh_ids = pl.DeviceIdType.MESH

    barrier = pltpu.get_barrier_semaphore()

    def member(offset):
        other = lax.rem(me + offset, members)
        return {"col": other // seq_size, "seq": lax.rem(other, seq_size)}

    for offset in range(1, members):
        pl.semaphore_signal(barrier, inc=1, device_id=member(offset), device_id_type=mesh_ids)
    pl.semaphore_signal(barrier, inc=1, device_id={"row": other_row}, device_id_type=mesh_ids)

    for load in loads[:3]:
        load.wait()

    def normalize(step, carry):
        parts = []
        for t in range(2):
            part = standardize_entries(raw_ref[step + t * groups])
            parts.append(part)
        at = pl.ds(pl.multiple_of(step * own, own), own)
        own_s[at, :] = jnp.concatenate(parts, axis=-1)
        return carry

    lax.fori_loop(0, groups, normalize, 0, unroll=4)

    first = halves(twice(first_ref[...]))
    second = halves(twice(second_ref[...]))
    span = LANES // 2
    packs = LANES // outer
    sets = half_cols // packs
    x_high, x_low = halves(own_s[...])
    projected = nt(x_high, second[0]) + (nt(x_high, second[1]) + nt(x_low, second[0]))
    for t in range(2):
        spread_s[:, t * outer : (t + 1) * outer] = projected[:, t * outer : (t + 1) * outer]

    def pack_right(step, carry):
        tokens = [spread_s[pl.ds(packs * step + u, groups, stride=own), :] for u in range(packs)]
        for t in range(2):
            line = jnp.concatenate([token[:, t * outer : (t + 1) * outer] for token in tokens], axis=1)
            r_own[step, t * groups : (t + 1) * groups, :] = line
        return carry

    lax.fori_loop(0, sets, pack_right, 0, unroll=2)

    started = []

    def run(condition, action):
        if condition is None:
            action()
        else:
            pl.when(condition)(action)

    def both(a, b):
        return b if a is None else (a if b is None else jnp.logical_and(a, b))

    def ship(source, place, target, sem, condition=None):
        copy = pltpu.make_async_remote_copy(
            src_ref=source,
            dst_ref=place,
            send_sem=send_sem.at[len(started)],
            recv_sem=sem,
            device_id=target,
            device_id_type=mesh_ids,
        )
        started.append((copy, condition))
        run(condition, copy.start)

    def arrived(place, sem, condition=None):
        copy = pltpu.make_async_remote_copy(
            src_ref=place,
            dst_ref=place,
            send_sem=send_sem.at[0],
            recv_sem=sem,
            device_id={"row": other_row},
            device_id_type=mesh_ids,
        )
        run(condition, copy.wait_recv)

    pl.semaphore_wait(barrier, members)
    column_slot = me
    here = column_slot // col_size == row
    elsewhere = jnp.logical_not(here)
    other_mine = other_row * col_size + col
    cut = sets // CHUNKS
    straight, crossed = range(CHUNKS // 2), range(CHUNKS // 2, CHUNKS)

    def right_target(block):
        return {"col": block // seq_size, "seq": lax.rem(block, seq_size)}

    own_right = column_slot == mine
    own_crossed = column_slot == other_mine
    for j in crossed:
        at = pl.ds(j * cut, cut)
        ship(r_own.at[at], hop_s.at[at], {"row": other_row}, hop_recv.at[j])
    for j in straight:
        at = pl.ds(j * cut, cut)
        ship(
            r_own.at[at],
            r_s.at[seq, at],
            right_target(mine),
            r_recv.at[seq, j],
            jnp.logical_not(own_right),
        )

    chunk = outer // CHUNKS
    pairs = LANES // 2 // own
    left_steps = groups // pairs

    def project_left(step, carry):
        parts = []
        for t in range(pairs):
            at = pl.ds(pl.multiple_of((t * left_steps + step) * own, own), own)
            result = nt3(first, halves(own_s[at, :]))
            parts += [result[:outer], result[outer:]]
        line = jnp.concatenate(parts, axis=1)
        at = pl.ds(pl.multiple_of(step * chunk, chunk), chunk)
        for k in range(CHUNKS):
            l_s[k, col, seq, at, :] = line[k * chunk : (k + 1) * chunk]
        return carry

    lax.fori_loop(0, left_steps, project_left, 0, unroll=4)

    def relay_left(k, at, rightward, leftward, exists):
        place, sem = l_s.at[k, at, seq], l_recv.at[k, at, seq]
        if rightward:
            ship(place, place, {"col": col + 1}, sem, both(exists, col < col_size - 1))
        if leftward:
            ship(place, place, {"col": col - 1}, sem, both(exists, col > 0))
        ship(place, place, {"seq": other_seq}, sem, exists)

    def relay(place_of, k, distance, reach):
        for sign in (-1, 1):
            at = col + sign * distance
            exists = at >= 0 if sign < 0 else at < col_size
            place, sem = place_of(k, at)
            if distance:
                arrived(place, sem, exists)
            first_hop, last_hop = (reach, 1) if distance == 0 else (1, 1 if distance >= reach else 0)
            for hop in range(first_hop, 0, -1) if last_hop else ():
                onward = col - sign * hop
                inside = onward < col_size if sign < 0 else onward >= 0
                ship(place, place, {"col": onward}, sem, both(exists, inside) if distance else inside)
            if distance or sign < 0:
                ship(place, place, {"seq": other_seq}, sem, exists if distance else None)

    def stage(k, distance, reach):
        return k + max(0, distance - reach)

    def left_of(k, at):
        return l_s.at[k, at, seq], l_recv.at[k, at, seq]

    def left_slot(slot):
        for distance in range(1, col_size):
            for k in range(CHUNKS):
                if stage(k, distance, LEFT_REACH) == slot:
                    relay(left_of, k, distance, LEFT_REACH)
        if slot + 2 < CHUNKS:
            relay(left_of, slot + 2, 0, LEFT_REACH)

    relay(left_of, 0, 0, LEFT_REACH)
    relay(left_of, 1, 0, LEFT_REACH)

    for load in loads[3:]:
        load.wait()
    first_col = seq * half_cols
    flat_pair = pair_ref.reshape(rows * cols, channels)
    flat_revised = revised_ref.reshape(rows * cols, channels)

    def turn_in(column, carry):
        turned_s[column] = flat_pair[pl.ds(first_col + column, rows, stride=cols), :].T
        return carry

    lax.fori_loop(0, half_cols // 2, turn_in, 0, unroll=2)

    @pl.when(own_right)
    def _():
        for j in straight:
            r_s[seq, j * cut : (j + 1) * cut] = r_own[j * cut : (j + 1) * cut]

    for j in crossed:
        at = pl.ds(j * cut, cut)
        arrived(hop_s.at[at], hop_recv.at[j])
        ship(
            hop_s.at[at],
            r_s.at[seq, at],
            right_target(other_mine),
            r_recv.at[seq, j],
            jnp.logical_not(own_crossed),
        )

    @pl.when(own_crossed)
    def _():
        for j in crossed:
            r_s[seq, j * cut : (j + 1) * cut] = hop_s[j * cut : (j + 1) * cut]

    left_slot(0)
    source_here = lax.rem(column_slot, col_size) == col
    for js, kind in ((straight, here), (crossed, elsewhere)):
        for j in js:
            for source in range(seq_size):
                kept = jnp.logical_and(source_here, seq == source)
                place, sem = r_s.at[source, pl.ds(j * cut, cut)], r_recv.at[source, j]
                arrived(place, sem, jnp.logical_and(kind, jnp.logical_not(kept)))
                ship(place, place, {"row": other_row}, sem, kind)
    blank = jnp.zeros(((span - seqs) * chunk, rows), f32)
    for k in range(CHUNKS):
        for source in range(seq_size):
            left_s[k, (source * span + seqs) * chunk : (source + 1) * span * chunk, :] = blank
    lax.fori_loop(half_cols // 2, half_cols, turn_in, 0, unroll=2)
    left_slot(1)
    t_high, t_low = halves(product_ref[...].T * (1.0 / total))
    product_s[...] = jnp.concatenate([t_high, t_low], axis=0)
    c_high, c_low = halves(score_ref[...])
    c_both = jnp.concatenate([c_high, c_low], axis=0)
    x_s[mine] = own_s[pl.ds(pl.multiple_of(col * share * own, share * own), share * own), :]
    left_slot(2)

    for js, kind in ((straight, elsewhere), (crossed, here)):
        for j in js:
            for source in range(seq_size):
                arrived(r_s.at[source, pl.ds(j * cut, cut)], r_recv.at[source, j], kind)
    empty = jnp.zeros((span - seqs, LANES), f32)

    def turn_right(step, carry):
        lines = [part for source in range(seq_size) for part in (r_s[source, step], empty)]
        at = pl.ds(pl.multiple_of(step * LANES, LANES), LANES)
        right_s[at, :] = jnp.concatenate(lines, axis=0).T
        return carry

    lax.fori_loop(0, sets, turn_right, 0, unroll=2)
    r_high, r_low = halves(right_s[...])
    r_both = jnp.concatenate([r_high, r_low], axis=1)

    def outer_chunk(k):
        for at in range(col_size):
            arrived(l_s.at[k, at, other_seq], l_recv.at[k, at, other_seq])

        def place_left(step, carry):
            at = pl.ds(pl.multiple_of(step * chunk, chunk), chunk)
            for source in range(seq_size):
                blocks = [l_s[k, t, source, at, :] for t in range(col_size)]
                for t in range(pairs):
                    for half in range(2):
                        lane = (2 * t + half) * own
                        line = jnp.concatenate([block[:, lane : lane + own] for block in blocks], axis=1)
                        place = source * span + half * groups + t * left_steps + step
                        left_s[k, pl.ds(pl.multiple_of(place * chunk, chunk), chunk), :] = line
            return carry

        lax.fori_loop(0, left_steps, place_left, 0, unroll=2)

        def outer_step(step, carry):
            pieces = [left_s[k, pl.ds(2 * step + t, LANES, stride=chunk), :] for t in range(2)]
            l_high, l_low = halves(jnp.concatenate(pieces, axis=1))
            product = mm(r_both, jnp.concatenate([l_high, l_high], axis=0)) + mm(r_high, l_low)
            p_high, p_low = halves(product)
            for t in range(2):
                high_s[2 * step + t] = p_high[:, t * rows : (t + 1) * rows]
                low_s[2 * step + t] = p_low[:, t * rows : (t + 1) * rows]
            return carry

        lax.fori_loop(0, chunk // 2, outer_step, 0, unroll=2)

    def project(k, step):
        def block(ref):
            pieces = [
                ref[:, pl.ds(pl.multiple_of((2 * step + t) * outer, outer), outer), :].reshape(chunk * outer, rows)
                for t in range(2)
            ]
            return jnp.concatenate(pieces, axis=1)

        t_both = product_s[:, k * chunk * outer : (k + 1) * chunk * outer]
        joint = mm(t_both, block(high_s))
        update = joint[:channels] + (joint[channels:] + mm(t_both[:channels], block(low_s)))
        return jnp.concatenate([turned_s[2 * step + t] for t in range(2)], axis=1) + update

    def send_x():
        for offset in range(1, col_size):
            target = lax.rem(col + offset, col_size)
            ship(
                own_s.at[pl.ds(pl.multiple_of(target * share * own, share * own), share * own), :],
                x_s.at[mine],
                {"col": target},
                x_recv.at[mine],
            )
        ship(x_s.at[mine], x_s.at[mine], {"row": other_row}, x_recv.at[mine])

    for k in range(CHUNKS - 1):
        outer_chunk(k)
        left_slot(k + CHUNKS - 1)
        if k == 1:
            send_x()

        def gather_step(turn, carry):
            steps = [GATHERED * turn + u for u in range(GATHERED)]
            for step, revised in [(step, project(k, step)) for step in steps]:
                for t in range(2):
                    turned_s[2 * step + t] = revised[:, t * rows : (t + 1) * rows]
            return carry

        lax.fori_loop(0, half_cols // 2 // GATHERED, gather_step, 0)
    outer_chunk(CHUNKS - 1)

    def pair_step(turn, carry):
        steps = [PAIRED * turn + u for u in range(PAIRED)]
        results = []
        for step in steps:
            revised = project(CHUNKS - 1, step)
            center = revised - jnp.mean(revised, axis=0, keepdims=True)
            spread = jnp.mean(center * center, axis=0, keepdims=True)
            n_high, n_low = halves(center)
            turned = mm(c_both, n_high)
            logits = turned[:heads] + (turned[heads:] + mm(c_high, n_low))
            results.append((step, revised, logits / jnp.sqrt(spread + epsilon)))
        for step, revised, logits in results:
            for t in range(2):
                turned_s[2 * step + t] = revised[:, t * rows : (t + 1) * rows]
                logit_s[me, 2 * step + t] = logits[:, t * rows : (t + 1) * rows]
        return carry

    section = half_cols // CHUNKS

    def logits_of(k, at):
        slot = at * seq_size + seq
        return logit_s.at[slot, pl.ds(k * section, section)], logit_recv.at[slot, k]

    def logit_slot(slot):
        for distance in range(1, col_size):
            for k in range(CHUNKS):
                if stage(k, distance, LOGIT_REACH) == slot:
                    relay(logits_of, k, distance, LOGIT_REACH)

    for k in range(CHUNKS):
        lax.fori_loop(k * section // 2 // PAIRED, (k + 1) * section // 2 // PAIRED, pair_step, 0)
        relay(logits_of, k, 0, LOGIT_REACH)
        if k == 1:
            for offset in range(1, col_size):
                at = row * col_size + lax.rem(col + offset, col_size)
                arrived(x_s.at[at], x_recv.at[at])
                ship(x_s.at[at], x_s.at[at], {"row": other_row}, x_recv.at[at])
    logit_slot(0)

    def turn_out(column, carry):
        flat_revised[pl.ds(first_col + column, rows, stride=cols), :] = turned_s[column].T
        return carry

    lax.fori_loop(0, half_cols, turn_out, 0, unroll=2)
    half_pair = revised_ref.at[:, pl.ds(pl.multiple_of(first_col, half_cols), half_cols), :]
    pair_copy = pltpu.make_async_remote_copy(
        src_ref=half_pair,
        dst_ref=half_pair,
        send_sem=pair_sem.at[0],
        recv_sem=pair_sem.at[1],
        device_id={"seq": other_seq},
        device_id_type=mesh_ids,
    )
    pair_copy.start()
    logit_slot(1)
    logit_slot(2)

    def spread_heads(matrix):
        width = matrix.shape[1] // heads
        zero = jnp.zeros((matrix.shape[0], width), f32)
        upper, lower = [], []
        for head in range(heads):
            piece = matrix[:, head * width : (head + 1) * width]
            upper += [piece, zero]
            lower += [zero, piece]
        return jnp.concatenate([jnp.concatenate(upper, axis=1), jnp.concatenate(lower, axis=1)], axis=0)

    g_high, g_low = halves(spread_heads(gate_ref[...]))
    g_twice = jnp.concatenate([g_high, g_high], axis=0)

    def gate_step(group, carry):
        at = pl.ds(pl.multiple_of(group * own, own), own)
        x_high, x_low = halves(x_s[pl.ds(row * col_size, col_size), at, :].reshape(rows, LANES))
        inner = mm(jnp.concatenate([x_high, x_low], axis=1), g_twice) + mm(x_high, g_low)
        gates_s[group] = jax.nn.sigmoid(inner)
        return carry

    lax.fori_loop(0, share, gate_step, 0)
    logit_slot(3)
    for at in range(col_size):
        arrived(x_s.at[other_row * col_size + at], x_recv.at[other_row * col_size + at])
    s_high, s_low = halves(spread_heads(source_ref[...]))
    s_twice = jnp.concatenate([s_high, s_high], axis=0)

    def value_step(group, carry):
        at = pl.ds(pl.multiple_of(group * own, own), own)
        x_high, x_low = halves(x_s[:, at, :].reshape(tokens_all, LANES))
        values = mm(jnp.concatenate([x_high, x_low], axis=1), s_twice) + mm(x_high, s_low)
        v_high, v_low = halves(values)
        v_high_s[group] = v_high
        v_low_s[group] = v_low
        return carry

    lax.fori_loop(0, share, value_step, 0)
    f_halves = halves(spread_heads(final_ref[...]))
    for slot in range(4, CHUNKS + col_size - 2):
        logit_slot(slot)
    for k in range(CHUNKS):
        for at in range(col_size):
            slot = at * seq_size + other_seq
            arrived(logit_s.at[slot, pl.ds(k * section, section)], logit_recv.at[slot, k])

    logits = logit_s[...].reshape(tokens_all, heads, rows)
    powers = jnp.exp(logits - jnp.max(logits, axis=0)[None])
    weights = powers * (1.0 / jnp.sum(powers, axis=0))[None]
    weight_s[...] = weights.reshape(tokens_all * heads, rows)
    for head in range(heads):
        w_high, w_low = halves(weight_s[pl.ds(head, tokens_all, stride=heads), :].T)
        at = head % 2 * rows
        mixer_s[head // 2, at : at + rows, :] = w_high
        mixer_s[head // 2, 2 * rows + at : 2 * rows + at + rows, :] = w_low
    lane_head = lax.broadcasted_iota(jnp.int32, (rows, 2 * LANES), 1) % LANES
    upper_head = lane_head < LANES // 2

    for turn in range(share // 2):
        parts = []
        for p in range(heads // 2):
            lanes = slice(p * LANES, (p + 1) * LANES)
            v_high, v_low = (
                jnp.concatenate([ref[2 * turn + t, :, lanes] for t in range(2)], axis=1)
                for ref in (v_high_s, v_low_s)
            )
            joint = mm(mixer_s[p], v_high)
            full = joint[: 2 * rows] + (joint[2 * rows :] + mm(mixer_s[p, : 2 * rows, :], v_low))
            parts.append(jnp.where(upper_head, full[:rows], full[rows:]))
        mixed = []
        for t in range(2):
            line = jnp.concatenate([part[:, t * LANES : (t + 1) * LANES] for part in parts], axis=1)
            mixed.append(line * gates_s[2 * turn + t])
        result = nt3(halves(jnp.concatenate(mixed, axis=0)), f_halves)
        for t in range(2):
            part_s[:, 2 * turn + t] = result[t * rows : (t + 1) * rows].reshape(col_size, own, LANES)
        at = pl.ds(col * share + 2 * turn, 2)
        for offset in range(1, col_size):
            target = lax.rem(col + offset, col_size)
            ship(
                part_s.at[target, pl.ds(2 * turn, 2)],
                whole_s.at[at],
                {"col": target},
                part_recv.at[col, turn],
            )
        whole_s[at] = part_s[col, 2 * turn : 2 * turn + 2]

    for offset in range(1, col_size):
        source = lax.rem(col + offset, col_size)
        for turn in range(share // 2):
            arrived(whole_s.at[pl.ds(source * share + 2 * turn, 2)], part_recv.at[source, turn])
    for t in range(2):
        at = pl.ds(t * groups, groups)
        out_ref[at] = raw_ref[at] + whole_s[:, :, t * depth : (t + 1) * depth]

    for copy, condition in started:
        run(condition, copy.wait_send)
    pair_copy.wait_send()
    other_half = revised_ref.at[:, pl.ds(pl.multiple_of(other_seq * half_cols, half_cols), half_cols), :]
    arrived(other_half, pair_sem.at[1])


def twice(matrix):
    zero = jnp.zeros_like(matrix)
    return jnp.concatenate(
        [jnp.concatenate([matrix, zero], axis=1), jnp.concatenate([zero, matrix], axis=1)], axis=0
    )


FINISH_CUTS = 4


def finish_kernel(*refs):
    count = len(refs) // 2
    copies = []
    for source, target in zip(refs[:count], refs[count:-1]):
        share = source.shape[0] // FINISH_CUTS
        for cut in range(FINISH_CUTS):
            at = pl.ds(cut * share, share)
            copies.append(pltpu.make_async_copy(source.at[at], target.at[at], refs[-1].at[len(copies)]))
            copies[-1].start()
    for copy in copies:
        copy.wait()


def fast_path(
    alignment_tensor,
    residue_couplings,
    first_factor_matrix,
    second_factor_matrix,
    tensor_product_matrix,
    coupling_score_matrix,
    averaged_source_matrix,
    sigmoid_matrix,
    final_matrix,
):
    seqs, _, own, depth = alignment_tensor.shape
    rows, cols, channels = residue_couplings.shape
    outer = first_factor_matrix.shape[1]
    heads = coupling_score_matrix.shape[1]
    row_size, col_size, seq_size = (lax.axis_size(a) for a in ("row", "col", "seq"))
    blocks = row_size * col_size
    half_cols = cols // seq_size
    members = col_size * seq_size
    groups = seqs // 2
    wide = 2 * averaged_source_matrix.shape[1]
    share = groups // col_size
    vmem = pl.BlockSpec(memory_space=pltpu.VMEM)
    dma = pltpu.SemaphoreType.DMA
    arrays = (
        alignment_tensor.reshape(seqs, own, depth),
        residue_couplings,
        first_factor_matrix.T,
        second_factor_matrix.T,
        tensor_product_matrix,
        coupling_score_matrix.T,
        averaged_source_matrix,
        sigmoid_matrix,
        final_matrix.T,
    )
    alignment, couplings = pl.pallas_call(
        functools.partial(block_kernel, row_size, col_size, seq_size, heads),
        out_shape=(
            pltpu.VMEM((seqs, own, depth), f32),
            pltpu.VMEM((rows, cols, channels), f32),
        ),
        in_specs=[pl.BlockSpec(memory_space=pltpu.HBM)] * 9,
        out_specs=(vmem, vmem),
        scratch_shapes=[pltpu.VMEM(a.shape, f32) for a in arrays]
        + [
            dma((len(arrays),)),
            pltpu.VMEM((groups * own, LANES), f32),
            pltpu.VMEM((CHUNKS, col_size, seq_size, groups // (LANES // 2 // own) * outer // CHUNKS, LANES), f32),
            pltpu.VMEM((groups * own, LANES), f32),
            pltpu.VMEM((half_cols * outer // LANES, seqs, LANES), f32),
            pltpu.VMEM((half_cols * outer // LANES, seqs, LANES), f32),
            pltpu.VMEM((seq_size, half_cols * outer // LANES, seqs, LANES), f32),
            pltpu.VMEM((CHUNKS, LANES * outer // CHUNKS, rows), f32),
            pltpu.VMEM((half_cols * outer, LANES), f32),
            pltpu.VMEM((outer // CHUNKS, half_cols * outer, rows), bf16),
            pltpu.VMEM((outer // CHUNKS, half_cols * outer, rows), bf16),
            pltpu.VMEM((2 * channels, outer * outer), bf16),
            pltpu.VMEM((half_cols, channels, rows), f32),
            pltpu.VMEM((blocks, share * own, LANES), f32),
            pltpu.VMEM((members, half_cols, heads, rows), f32),
            pltpu.VMEM((members * half_cols * heads, rows), f32),
            pltpu.VMEM((heads // 2, 4 * rows, members * half_cols), bf16),
            pltpu.VMEM((share, members * half_cols, wide), bf16),
            pltpu.VMEM((share, members * half_cols, wide), bf16),
            pltpu.VMEM((share, rows, wide), f32),
            pltpu.VMEM((col_size, share, own, LANES), f32),
            pltpu.VMEM((groups, own, LANES), f32),
            dma((192,)),
            dma((CHUNKS, col_size, seq_size)),
            dma((seq_size, CHUNKS)),
            dma((CHUNKS,)),
            dma((blocks,)),
            dma((members, CHUNKS)),
            dma((col_size, share // 2)),
            dma((2,)),
        ],
        compiler_params=pltpu.CompilerParams(
            collective_id=0, has_side_effects=True, vmem_limit_bytes=59 << 20
        ),
    )(*arrays)
    revised_alignment, revised_couplings = pl.pallas_call(
        finish_kernel,
        out_shape=(
            jax.ShapeDtypeStruct((seqs, own, depth), f32),
            jax.ShapeDtypeStruct((rows, cols, channels), f32),
        ),
        in_specs=[vmem] * 2,
        out_specs=(pl.BlockSpec(memory_space=pltpu.HBM),) * 2,
        scratch_shapes=[dma((2 * FINISH_CUTS,))],
        compiler_params=pltpu.CompilerParams(vmem_limit_bytes=12 << 20),
    )(alignment, couplings)
    return revised_alignment.reshape(alignment_tensor.shape), revised_couplings


def on_device(alignment_tensor, residue_couplings, first_factor_matrix, *rest):
    seqs, tiles, own, depth = alignment_tensor.shape
    rows, cols, channels = residue_couplings.shape
    row_size, col_size, seq_size = (lax.axis_size(a) for a in ("row", "col", "seq"))
    fits = (
        tiles == 1
        and rows == own * col_size == LANES
        and cols == own * seq_size
        and row_size * rows == col_size * cols
        and own % 16 == 0
        and seqs % 6 == 0
        and 2 * depth == channels == LANES
        and first_factor_matrix.shape[1] % (8 * CHUNKS) == 0
        and seqs % (4 * col_size) == 0
        and rest[3].shape[1] == 8 * LANES // 4
        and cols % (4 * CHUNKS) == 0
        and seq_size == row_size == 2
        and rest[2].shape[1] == 8 == own * own // LANES
        and seqs * seq_size <= LANES
        and seqs // 2 % (LANES // 2 // own) == 0
        and col_size == CHUNKS
    )
    path = fast_path if fits else general_path
    return path(alignment_tensor, residue_couplings, first_factor_matrix, *rest)


def solution(mesh):
    return jax.shard_map(
        on_device,
        mesh=mesh,
        in_specs=(
            P(("grp", "seq"), "row", "col", None),
            P(("grp", "row"), "col", None),
            P(),
            P(),
            P(),
            P(),
            P(),
            P(),
            P(),
        ),
        out_specs=(P(("grp", "seq"), "row", "col", None), P(("grp", "row"), "col", None)),
        check_vma=False,
    )
```

```python
import functools

import jax
import jax.numpy as jnp
from jax import lax
from jax.experimental import pallas as pl
from jax.experimental.pallas import tpu as pltpu
from jax.sharding import PartitionSpec as P

epsilon = 1e-05
exact_arithmetic = lax.Precision.HIGHEST


def broadcast(block, axis, holder):
    block = jnp.where(lax.axis_index(axis) == holder, block, jnp.zeros_like(block))
    return lax.psum(block, axis)


def standardize_entries(inputs):
    center = inputs - jnp.mean(inputs, axis=-1, keepdims=True)
    spread = jnp.mean(center * center, axis=-1, keepdims=True)
    return center / jnp.sqrt(spread + epsilon)


def pair_scores(pair_rows, coupling_score_matrix):
    return jnp.einsum(
        "ijc,ch->ihj",
        standardize_entries(pair_rows),
        coupling_score_matrix,
        precision=exact_arithmetic,
    )


def general_path(
    alignment_tensor,
    residue_couplings,
    first_factor_matrix,
    second_factor_matrix,
    tensor_product_matrix,
    coupling_score_matrix,
    averaged_source_matrix,
    sigmoid_matrix,
    final_matrix,
):
    shard_alignment_entries = alignment_tensor.shape[0]
    total_seqs = shard_alignment_entries * lax.axis_size("seq")
    coupling_lines = residue_couplings.shape[0]
    col_count = residue_couplings.shape[1]
    alignment_depth = alignment_tensor.shape[3]
    outer_width = first_factor_matrix.shape[1]
    head_count = coupling_score_matrix.shape[1]
    gathered_lines = lax.all_gather(alignment_tensor, "col", axis=2, tiled=True)
    alignment_tile_entries = gathered_lines.reshape(
        shard_alignment_entries, coupling_lines, alignment_depth
    )
    standardized_alignment = standardize_entries(alignment_tile_entries)
    first_factor_tile = jnp.einsum(
        "kgd,dl->kgl", standardized_alignment, first_factor_matrix, precision=exact_arithmetic
    )
    combined_matrix = jnp.concatenate([second_factor_matrix, averaged_source_matrix], axis=1)
    first_col = lax.axis_index("col") * col_count
    root_row = first_col // coupling_lines
    offset = first_col % coupling_lines
    raw_piece = lax.dynamic_slice_in_dim(alignment_tile_entries, offset, col_count, 1)
    raw_received = broadcast(raw_piece, "row", root_row)
    received = jnp.einsum(
        "pko,ol->pkl",
        standardize_entries(raw_received),
        combined_matrix,
        precision=exact_arithmetic,
    )
    second_factor_tile = received[:, :, :outer_width]
    averaged_sources = received[:, :, outer_width:].reshape(
        shard_alignment_entries, col_count, head_count, -1
    )
    block_rows = 16
    left_blocks = first_factor_tile.reshape(
        shard_alignment_entries, coupling_lines // block_rows, block_rows, outer_width
    ).transpose(1, 0, 2, 3)

    def outer_block(left_block):
        product = (
            jnp.einsum("sic,sje->ijce", left_block, second_factor_tile, precision=exact_arithmetic)
            / total_seqs
        )
        flat_prod = product.reshape(block_rows * col_count, -1)
        return jnp.dot(flat_prod, tensor_product_matrix, precision=exact_arithmetic).reshape(
            block_rows, col_count, -1
        )

    update = lax.map(outer_block, left_blocks).reshape(coupling_lines, col_count, -1)
    revised_couplings = residue_couplings + lax.psum(update, "seq")
    scores = pair_scores(revised_couplings, coupling_score_matrix)
    local_top = jnp.max(scores, axis=2)
    score_top = lax.pmax(local_top, "col")
    score_total = lax.psum(jnp.sum(jnp.exp(scores - score_top[:, :, None]), axis=2), "col")
    weights = jnp.exp(scores - score_top[:, :, None]) / score_total[:, :, None]
    mixed_rows = jnp.einsum(
        "ihj,sjhd->sihd", weights, averaged_sources, precision=exact_arithmetic
    ).reshape(shard_alignment_entries, coupling_lines, -1)
    summed = lax.psum_scatter(mixed_rows, "col", scatter_dimension=1, tiled=True)
    shard_standardized_alignment = standardize_entries(
        alignment_tensor.reshape(shard_alignment_entries, -1, alignment_depth)
    )
    sigmoid_factors = jax.nn.sigmoid(
        jnp.einsum(
            "pko,ol->pkl", shard_standardized_alignment, sigmoid_matrix, precision=exact_arithmetic
        )
    )
    coupling_increment = jnp.einsum(
        "snf,fc->snc", summed * sigmoid_factors, final_matrix, precision=exact_arithmetic
    )
    revised_alignment = alignment_tensor + coupling_increment.reshape(alignment_tensor.shape)
    return (revised_alignment, revised_couplings)


f32, bf16 = jnp.float32, jnp.bfloat16
LANES = 128
CHUNKS = 4
LEFT_REACH = 1
LOGIT_REACH = 1
GATHERED = 8
PAIRED = 4


def halves(values):
    high = values.astype(bf16)
    return high, (values - high.astype(f32)).astype(bf16)


def mm(a, b):
    return jnp.dot(a, b, preferred_element_type=f32)


def mm3(a, b):
    (a_high, a_low), (b_high, b_low) = a, b
    return mm(a_high, b_high) + (mm(a_high, b_low) + mm(a_low, b_high))


def nt(a, b):
    return lax.dot_general(a, b, (((1,), (1,)), ((), ())), preferred_element_type=f32)


def nt3(a, b):
    (a_high, a_low), (b_high, b_low) = a, b
    return nt(a_high, b_high) + (nt(a_high, b_low) + nt(a_low, b_high))


def block_kernel(
    row_size,
    col_size,
    seq_size,
    heads,
    raw_in,
    pair_in,
    first_in,
    second_in,
    product_in,
    score_in,
    source_in,
    gate_in,
    final_in,
    out_ref,
    revised_ref,
    raw_ref,
    pair_ref,
    first_ref,
    second_ref,
    product_ref,
    score_ref,
    source_ref,
    gate_ref,
    final_ref,
    load_sem,
    own_s,
    l_s,
    spread_s,
    r_own,
    hop_s,
    r_s,
    left_s,
    right_s,
    high_s,
    low_s,
    product_s,
    turned_s,
    x_s,
    logit_s,
    weight_s,
    mixer_s,
    v_high_s,
    v_low_s,
    gates_s,
    part_s,
    whole_s,
    send_sem,
    l_recv,
    r_recv,
    hop_recv,
    x_recv,
    logit_recv,
    part_recv,
    pair_sem,
):
    loads = []
    for source, place in (
        (raw_in, raw_ref),
        (second_in, second_ref),
        (first_in, first_ref),
        (pair_in, pair_ref),
        (product_in, product_ref),
        (source_in, source_ref),
        (gate_in, gate_ref),
        (score_in, score_ref),
        (final_in, final_ref),
    ):
        loads.append(pltpu.make_async_copy(source, place, load_sem.at[len(loads)]))
        loads[-1].start()
    seqs, own, depth = raw_ref.shape
    groups = seqs // 2
    rows, cols, channels = revised_ref.shape
    outer = first_ref.shape[0]
    half_cols = cols // seq_size
    total = seqs * seq_size
    wide = 2 * source_ref.shape[1]
    members = col_size * seq_size
    tokens_all = members * half_cols
    share = groups // col_size
    row, col, seq = (lax.axis_index(a) for a in ("row", "col", "seq"))
    other_row, other_seq = 1 - row, 1 - seq
    me = col * seq_size + seq
    mine = row * col_size + col
    mesh_ids = pl.DeviceIdType.MESH

    barrier = pltpu.get_barrier_semaphore()

    def member(offset):
        other = lax.rem(me + offset, members)
        return {"col": other // seq_size, "seq": lax.rem(other, seq_size)}

    for offset in range(1, members):
        pl.semaphore_signal(barrier, inc=1, device_id=member(offset), device_id_type=mesh_ids)
    pl.semaphore_signal(barrier, inc=1, device_id={"row": other_row}, device_id_type=mesh_ids)

    for load in loads[:3]:
        load.wait()

    def normalize(step, carry):
        parts = []
        for t in range(2):
            part = standardize_entries(raw_ref[step + t * groups])
            parts.append(part)
        at = pl.ds(pl.multiple_of(step * own, own), own)
        own_s[at, :] = jnp.concatenate(parts, axis=-1)
        return carry

    lax.fori_loop(0, groups, normalize, 0, unroll=4)

    first = halves(twice(first_ref[...]))
    second = halves(twice(second_ref[...]))
    span = LANES // 2
    packs = LANES // outer
    sets = half_cols // packs
    x_high, x_low = halves(own_s[...])
    projected = nt(x_high, second[0]) + (nt(x_high, second[1]) + nt(x_low, second[0]))
    for t in range(2):
        spread_s[:, t * outer : (t + 1) * outer] = projected[:, t * outer : (t + 1) * outer]

    def pack_right(step, carry):
        tokens = [spread_s[pl.ds(packs * step + u, groups, stride=own), :] for u in range(packs)]
        for t in range(2):
            line = jnp.concatenate([token[:, t * outer : (t + 1) * outer] for token in tokens], axis=1)
            r_own[step, t * groups : (t + 1) * groups, :] = line
        return carry

    lax.fori_loop(0, sets, pack_right, 0, unroll=2)

    started = []

    def run(condition, action):
        if condition is None:
            action()
        else:
            pl.when(condition)(action)

    def both(a, b):
        return b if a is None else (a if b is None else jnp.logical_and(a, b))

    def ship(source, place, target, sem, condition=None):
        copy = pltpu.make_async_remote_copy(
            src_ref=source,
            dst_ref=place,
            send_sem=send_sem.at[len(started)],
            recv_sem=sem,
            device_id=target,
            device_id_type=mesh_ids,
        )
        started.append((copy, condition))
        run(condition, copy.start)

    def arrived(place, sem, condition=None):
        copy = pltpu.make_async_remote_copy(
            src_ref=place,
            dst_ref=place,
            send_sem=send_sem.at[0],
            recv_sem=sem,
            device_id={"row": other_row},
            device_id_type=mesh_ids,
        )
        run(condition, copy.wait_recv)

    pl.semaphore_wait(barrier, members)
    column_slot = me
    here = column_slot // col_size == row
    elsewhere = jnp.logical_not(here)
    other_mine = other_row * col_size + col
    cut = sets // CHUNKS
    straight, crossed = range(CHUNKS // 2), range(CHUNKS // 2, CHUNKS)

    def right_target(block):
        return {"col": block // seq_size, "seq": lax.rem(block, seq_size)}

    own_right = column_slot == mine
    own_crossed = column_slot == other_mine
    for j in crossed:
        at = pl.ds(j * cut, cut)
        ship(r_own.at[at], hop_s.at[at], {"row": other_row}, hop_recv.at[j])
    for j in straight:
        at = pl.ds(j * cut, cut)
        ship(
            r_own.at[at],
            r_s.at[seq, at],
            right_target(mine),
            r_recv.at[seq, j],
            jnp.logical_not(own_right),
        )

    chunk = outer // CHUNKS
    pairs = LANES // 2 // own
    left_steps = groups // pairs

    def project_left(step, carry):
        parts = []
        for t in range(pairs):
            at = pl.ds(pl.multiple_of((t * left_steps + step) * own, own), own)
            result = nt3(first, halves(own_s[at, :]))
            parts += [result[:outer], result[outer:]]
        line = jnp.concatenate(parts, axis=1)
        at = pl.ds(pl.multiple_of(step * chunk, chunk), chunk)
        for k in range(CHUNKS):
            l_s[k, col, seq, at, :] = line[k * chunk : (k + 1) * chunk]
        return carry

    lax.fori_loop(0, left_steps, project_left, 0, unroll=4)

    def relay_left(k, at, rightward, leftward, exists):
        place, sem = l_s.at[k, at, seq], l_recv.at[k, at, seq]
        if rightward:
            ship(place, place, {"col": col + 1}, sem, both(exists, col < col_size - 1))
        if leftward:
            ship(place, place, {"col": col - 1}, sem, both(exists, col > 0))
        ship(place, place, {"seq": other_seq}, sem, exists)

    def relay(place_of, k, distance, reach):
        for sign in (-1, 1):
            at = col + sign * distance
            exists = at >= 0 if sign < 0 else at < col_size
            place, sem = place_of(k, at)
            if distance:
                arrived(place, sem, exists)
            first_hop, last_hop = (reach, 1) if distance == 0 else (1, 1 if distance >= reach else 0)
            for hop in range(first_hop, 0, -1) if last_hop else ():
                onward = col - sign * hop
                inside = onward < col_size if sign < 0 else onward >= 0
                ship(place, place, {"col": onward}, sem, both(exists, inside) if distance else inside)
            if distance or sign < 0:
                ship(place, place, {"seq": other_seq}, sem, exists if distance else None)

    def stage(k, distance, reach):
        return k + max(0, distance - reach)

    def left_of(k, at):
        return l_s.at[k, at, seq], l_recv.at[k, at, seq]

    def left_slot(slot):
        for distance in range(1, col_size):
            for k in range(CHUNKS):
                if stage(k, distance, LEFT_REACH) == slot:
                    relay(left_of, k, distance, LEFT_REACH)
        if slot + 2 < CHUNKS:
            relay(left_of, slot + 2, 0, LEFT_REACH)

    relay(left_of, 0, 0, LEFT_REACH)
    relay(left_of, 1, 0, LEFT_REACH)

    for load in loads[3:]:
        load.wait()
    first_col = seq * half_cols
    flat_pair = pair_ref.reshape(rows * cols, channels)
    flat_revised = revised_ref.reshape(rows * cols, channels)

    def turn_in(column, carry):
        turned_s[column] = flat_pair[pl.ds(first_col + column, rows, stride=cols), :].T
        return carry

    lax.fori_loop(0, half_cols // 2, turn_in, 0, unroll=2)

    @pl.when(own_right)
    def _():
        for j in straight:
            r_s[seq, j * cut : (j + 1) * cut] = r_own[j * cut : (j + 1) * cut]

    for j in crossed:
        at = pl.ds(j * cut, cut)
        arrived(hop_s.at[at], hop_recv.at[j])
        ship(
            hop_s.at[at],
            r_s.at[seq, at],
            right_target(other_mine),
            r_recv.at[seq, j],
            jnp.logical_not(own_crossed),
        )

    @pl.when(own_crossed)
    def _():
        for j in crossed:
            r_s[seq, j * cut : (j + 1) * cut] = hop_s[j * cut : (j + 1) * cut]

    left_slot(0)
    source_here = lax.rem(column_slot, col_size) == col
    for js, kind in ((straight, here), (crossed, elsewhere)):
        for j in js:
            for source in range(seq_size):
                kept = jnp.logical_and(source_here, seq == source)
                place, sem = r_s.at[source, pl.ds(j * cut, cut)], r_recv.at[source, j]
                arrived(place, sem, jnp.logical_and(kind, jnp.logical_not(kept)))
                ship(place, place, {"row": other_row}, sem, kind)
    blank = jnp.zeros(((span - seqs) * chunk, rows), f32)
    for k in range(CHUNKS):
        for source in range(seq_size):
            left_s[k, (source * span + seqs) * chunk : (source + 1) * span * chunk, :] = blank
    lax.fori_loop(half_cols // 2, half_cols, turn_in, 0, unroll=2)
    left_slot(1)
    t_high, t_low = halves(product_ref[...].T * (1.0 / total))
    product_s[...] = jnp.concatenate([t_high, t_low], axis=0)
    c_high, c_low = halves(score_ref[...])
    c_both = jnp.concatenate([c_high, c_low], axis=0)
    x_s[mine] = own_s[pl.ds(pl.multiple_of(col * share * own, share * own), share * own), :]
    left_slot(2)

    for js, kind in ((straight, elsewhere), (crossed, here)):
        for j in js:
            for source in range(seq_size):
                arrived(r_s.at[source, pl.ds(j * cut, cut)], r_recv.at[source, j], kind)
    empty = jnp.zeros((span - seqs, LANES), f32)

    def turn_right(step, carry):
        lines = [part for source in range(seq_size) for part in (r_s[source, step], empty)]
        at = pl.ds(pl.multiple_of(step * LANES, LANES), LANES)
        right_s[at, :] = jnp.concatenate(lines, axis=0).T
        return carry

    lax.fori_loop(0, sets, turn_right, 0, unroll=2)
    r_high, r_low = halves(right_s[...])
    r_both = jnp.concatenate([r_high, r_low], axis=1)

    def chunk_arrived(k):
        for at in range(col_size):
            arrived(l_s.at[k, at, other_seq], l_recv.at[k, at, other_seq])

    def place_left(k, step):
        at = pl.ds(pl.multiple_of(step * chunk, chunk), chunk)
        for source in range(seq_size):
            blocks = [l_s[k, t, source, at, :] for t in range(col_size)]
            for t in range(pairs):
                for half in range(2):
                    lane = (2 * t + half) * own
                    line = jnp.concatenate([block[:, lane : lane + own] for block in blocks], axis=1)
                    place = source * span + half * groups + t * left_steps + step
                    left_s[k, pl.ds(pl.multiple_of(place * chunk, chunk), chunk), :] = line

    def outer_chunk(k):
        def outer_step(step, carry):
            pieces = [left_s[k, pl.ds(2 * step + t, LANES, stride=chunk), :] for t in range(2)]
            l_high, l_low = halves(jnp.concatenate(pieces, axis=1))
            product = mm(r_both, jnp.concatenate([l_high, l_high], axis=0)) + mm(r_high, l_low)
            p_high, p_low = halves(product)
            for t in range(2):
                high_s[2 * step + t] = p_high[:, t * rows : (t + 1) * rows]
                low_s[2 * step + t] = p_low[:, t * rows : (t + 1) * rows]
            return carry

        lax.fori_loop(0, chunk // 2, outer_step, 0, unroll=2)

    def project(k, step):
        def block(ref):
            pieces = [
                ref[:, pl.ds(pl.multiple_of((2 * step + t) * outer, outer), outer), :].reshape(chunk * outer, rows)
                for t in range(2)
            ]
            return jnp.concatenate(pieces, axis=1)

        t_both = product_s[:, k * chunk * outer : (k + 1) * chunk * outer]
        joint = mm(t_both, block(high_s))
        update = joint[:channels] + (joint[channels:] + mm(t_both[:channels], block(low_s)))
        return jnp.concatenate([turned_s[2 * step + t] for t in range(2)], axis=1) + update

    def send_x():
        for offset in range(1, col_size):
            target = lax.rem(col + offset, col_size)
            ship(
                own_s.at[pl.ds(pl.multiple_of(target * share * own, share * own), share * own), :],
                x_s.at[mine],
                {"col": target},
                x_recv.at[mine],
            )
        ship(x_s.at[mine], x_s.at[mine], {"row": other_row}, x_recv.at[mine])

    chunk_arrived(0)

    def place_first(step, carry):
        place_left(0, step)
        return carry

    lax.fori_loop(0, left_steps, place_first, 0, unroll=6)
    for k in range(CHUNKS - 1):
        left_slot(k + CHUNKS - 1)
        outer_chunk(k)
        chunk_arrived(k + 1)
        if k == 1:
            send_x()

        def gather_step(turn, carry):
            steps = [GATHERED * turn + u for u in range(GATHERED)]
            share_steps = left_steps * 2 * GATHERED // half_cols
            for u in range(share_steps):
                place_left(k + 1, share_steps * turn + u)
            for step, revised in [(step, project(k, step)) for step in steps]:
                for t in range(2):
                    turned_s[2 * step + t] = revised[:, t * rows : (t + 1) * rows]
            return carry

        lax.fori_loop(0, half_cols // 2 // GATHERED, gather_step, 0)
    outer_chunk(CHUNKS - 1)

    def pair_step(turn, carry):
        steps = [PAIRED * turn + u for u in range(PAIRED)]
        results = []
        for step in steps:
            revised = project(CHUNKS - 1, step)
            center = revised - jnp.mean(revised, axis=0, keepdims=True)
            spread = jnp.mean(center * center, axis=0, keepdims=True)
            n_high, n_low = halves(center)
            turned = mm(c_both, n_high)
            logits = turned[:heads] + (turned[heads:] + mm(c_high, n_low))
            results.append((step, revised, logits / jnp.sqrt(spread + epsilon)))
        for step, revised, logits in results:
            for t in range(2):
                turned_s[2 * step + t] = revised[:, t * rows : (t + 1) * rows]
                logit_s[me, 2 * step + t] = logits[:, t * rows : (t + 1) * rows]
        return carry

    section = half_cols // CHUNKS

    def logits_of(k, at):
        slot = at * seq_size + seq
        return logit_s.at[slot, pl.ds(k * section, section)], logit_recv.at[slot, k]

    def logit_slot(slot):
        for distance in range(1, col_size):
            for k in range(CHUNKS):
                if stage(k, distance, LOGIT_REACH) == slot:
                    relay(logits_of, k, distance, LOGIT_REACH)

    for k in range(CHUNKS):
        lax.fori_loop(k * section // 2 // PAIRED, (k + 1) * section // 2 // PAIRED, pair_step, 0)
        relay(logits_of, k, 0, LOGIT_REACH)
        if k == 1:
            for offset in range(1, col_size):
                at = row * col_size + lax.rem(col + offset, col_size)
                arrived(x_s.at[at], x_recv.at[at])
                ship(x_s.at[at], x_s.at[at], {"row": other_row}, x_recv.at[at])
    logit_slot(0)

    def turn_out(column, carry):
        flat_revised[pl.ds(first_col + column, rows, stride=cols), :] = turned_s[column].T
        return carry

    lax.fori_loop(0, half_cols, turn_out, 0, unroll=4)
    half_pair = revised_ref.at[:, pl.ds(pl.multiple_of(first_col, half_cols), half_cols), :]
    pair_copy = pltpu.make_async_remote_copy(
        src_ref=half_pair,
        dst_ref=half_pair,
        send_sem=pair_sem.at[0],
        recv_sem=pair_sem.at[1],
        device_id={"seq": other_seq},
        device_id_type=mesh_ids,
    )
    pair_copy.start()
    logit_slot(1)
    logit_slot(2)

    def spread_heads(matrix):
        width = matrix.shape[1] // heads
        zero = jnp.zeros((matrix.shape[0], width), f32)
        upper, lower = [], []
        for head in range(heads):
            piece = matrix[:, head * width : (head + 1) * width]
            upper += [piece, zero]
            lower += [zero, piece]
        return jnp.concatenate([jnp.concatenate(upper, axis=1), jnp.concatenate(lower, axis=1)], axis=0)

    g_high, g_low = halves(spread_heads(gate_ref[...]))
    g_twice = jnp.concatenate([g_high, g_high], axis=0)

    def gate_step(group, carry):
        at = pl.ds(pl.multiple_of(group * own, own), own)
        x_high, x_low = halves(x_s[pl.ds(row * col_size, col_size), at, :].reshape(rows, LANES))
        inner = mm(jnp.concatenate([x_high, x_low], axis=1), g_twice) + mm(x_high, g_low)
        gates_s[group] = jax.nn.sigmoid(inner)
        return carry

    lax.fori_loop(0, share, gate_step, 0, unroll=2)
    logit_slot(3)
    for at in range(col_size):
        arrived(x_s.at[other_row * col_size + at], x_recv.at[other_row * col_size + at])
    s_high, s_low = halves(spread_heads(source_ref[...]))
    s_twice = jnp.concatenate([s_high, s_high], axis=0)

    def value_step(group, carry):
        at = pl.ds(pl.multiple_of(group * own, own), own)
        x_high, x_low = halves(x_s[:, at, :].reshape(tokens_all, LANES))
        values = mm(jnp.concatenate([x_high, x_low], axis=1), s_twice) + mm(x_high, s_low)
        v_high, v_low = halves(values)
        v_high_s[group] = v_high
        v_low_s[group] = v_low
        return carry

    lax.fori_loop(0, share, value_step, 0, unroll=2)
    f_halves = halves(spread_heads(final_ref[...]))
    for slot in range(4, CHUNKS + col_size - 2):
        logit_slot(slot)
    for k in range(CHUNKS):
        for at in range(col_size):
            slot = at * seq_size + other_seq
            arrived(logit_s.at[slot, pl.ds(k * section, section)], logit_recv.at[slot, k])

    logits = logit_s[...].reshape(tokens_all, heads, rows)
    powers = jnp.exp(logits - jnp.max(logits, axis=0)[None])
    weights = powers * (1.0 / jnp.sum(powers, axis=0))[None]
    weight_s[...] = weights.reshape(tokens_all * heads, rows)
    for head in range(heads):
        w_high, w_low = halves(weight_s[pl.ds(head, tokens_all, stride=heads), :].T)
        at = head % 2 * rows
        mixer_s[head // 2, at : at + rows, :] = w_high
        mixer_s[head // 2, 2 * rows + at : 2 * rows + at + rows, :] = w_low
    lane_head = lax.broadcasted_iota(jnp.int32, (rows, 2 * LANES), 1) % LANES
    upper_head = lane_head < LANES // 2

    for turn in range(share // 2):
        parts = []
        for p in range(heads // 2):
            lanes = slice(p * LANES, (p + 1) * LANES)
            v_high, v_low = (
                jnp.concatenate([ref[2 * turn + t, :, lanes] for t in range(2)], axis=1)
                for ref in (v_high_s, v_low_s)
            )
            joint = mm(mixer_s[p], v_high)
            full = joint[: 2 * rows] + (joint[2 * rows :] + mm(mixer_s[p, : 2 * rows, :], v_low))
            parts.append(jnp.where(upper_head, full[:rows], full[rows:]))
        mixed = []
        for t in range(2):
            line = jnp.concatenate([part[:, t * LANES : (t + 1) * LANES] for part in parts], axis=1)
            mixed.append(line * gates_s[2 * turn + t])
        result = nt3(halves(jnp.concatenate(mixed, axis=0)), f_halves)
        for t in range(2):
            part_s[:, 2 * turn + t] = result[t * rows : (t + 1) * rows].reshape(col_size, own, LANES)
        at = pl.ds(col * share + 2 * turn, 2)
        for offset in range(1, col_size):
            target = lax.rem(col + offset, col_size)
            ship(
                part_s.at[target, pl.ds(2 * turn, 2)],
                whole_s.at[at],
                {"col": target},
                part_recv.at[col, turn],
            )
        whole_s[at] = part_s[col, 2 * turn : 2 * turn + 2]

    for offset in range(1, col_size):
        source = lax.rem(col + offset, col_size)
        for turn in range(share // 2):
            arrived(whole_s.at[pl.ds(source * share + 2 * turn, 2)], part_recv.at[source, turn])
    for t in range(2):
        at = pl.ds(t * groups, groups)
        out_ref[at] = raw_ref[at] + whole_s[:, :, t * depth : (t + 1) * depth]

    for copy, condition in started:
        run(condition, copy.wait_send)
    pair_copy.wait_send()
    other_half = revised_ref.at[:, pl.ds(pl.multiple_of(other_seq * half_cols, half_cols), half_cols), :]
    arrived(other_half, pair_sem.at[1])


def twice(matrix):
    zero = jnp.zeros_like(matrix)
    return jnp.concatenate(
        [jnp.concatenate([matrix, zero], axis=1), jnp.concatenate([zero, matrix], axis=1)], axis=0
    )


FINISH_CUTS = 4


def finish_kernel(*refs):
    count = len(refs) // 2
    copies = []
    for source, target in zip(refs[:count], refs[count:-1]):
        share = source.shape[0] // FINISH_CUTS
        for cut in range(FINISH_CUTS):
            at = pl.ds(cut * share, share)
            copies.append(pltpu.make_async_copy(source.at[at], target.at[at], refs[-1].at[len(copies)]))
            copies[-1].start()
    for copy in copies:
        copy.wait()


def fast_path(
    alignment_tensor,
    residue_couplings,
    first_factor_matrix,
    second_factor_matrix,
    tensor_product_matrix,
    coupling_score_matrix,
    averaged_source_matrix,
    sigmoid_matrix,
    final_matrix,
):
    seqs, _, own, depth = alignment_tensor.shape
    rows, cols, channels = residue_couplings.shape
    outer = first_factor_matrix.shape[1]
    heads = coupling_score_matrix.shape[1]
    row_size, col_size, seq_size = (lax.axis_size(a) for a in ("row", "col", "seq"))
    blocks = row_size * col_size
    half_cols = cols // seq_size
    members = col_size * seq_size
    groups = seqs // 2
    wide = 2 * averaged_source_matrix.shape[1]
    share = groups // col_size
    vmem = pl.BlockSpec(memory_space=pltpu.VMEM)
    dma = pltpu.SemaphoreType.DMA
    arrays = (
        alignment_tensor.reshape(seqs, own, depth),
        residue_couplings,
        first_factor_matrix.T,
        second_factor_matrix.T,
        tensor_product_matrix,
        coupling_score_matrix.T,
        averaged_source_matrix,
        sigmoid_matrix,
        final_matrix.T,
    )
    alignment, couplings = pl.pallas_call(
        functools.partial(block_kernel, row_size, col_size, seq_size, heads),
        out_shape=(
            pltpu.VMEM((seqs, own, depth), f32),
            pltpu.VMEM((rows, cols, channels), f32),
        ),
        in_specs=[pl.BlockSpec(memory_space=pltpu.HBM)] * 9,
        out_specs=(vmem, vmem),
        scratch_shapes=[pltpu.VMEM(a.shape, f32) for a in arrays]
        + [
            dma((len(arrays),)),
            pltpu.VMEM((groups * own, LANES), f32),
            pltpu.VMEM((CHUNKS, col_size, seq_size, groups // (LANES // 2 // own) * outer // CHUNKS, LANES), f32),
            pltpu.VMEM((groups * own, LANES), f32),
            pltpu.VMEM((half_cols * outer // LANES, seqs, LANES), f32),
            pltpu.VMEM((half_cols * outer // LANES, seqs, LANES), f32),
            pltpu.VMEM((seq_size, half_cols * outer // LANES, seqs, LANES), f32),
            pltpu.VMEM((CHUNKS, LANES * outer // CHUNKS, rows), f32),
            pltpu.VMEM((half_cols * outer, LANES), f32),
            pltpu.VMEM((outer // CHUNKS, half_cols * outer, rows), bf16),
            pltpu.VMEM((outer // CHUNKS, half_cols * outer, rows), bf16),
            pltpu.VMEM((2 * channels, outer * outer), bf16),
            pltpu.VMEM((half_cols, channels, rows), f32),
            pltpu.VMEM((blocks, share * own, LANES), f32),
            pltpu.VMEM((members, half_cols, heads, rows), f32),
            pltpu.VMEM((members * half_cols * heads, rows), f32),
            pltpu.VMEM((heads // 2, 4 * rows, members * half_cols), bf16),
            pltpu.VMEM((share, members * half_cols, wide), bf16),
            pltpu.VMEM((share, members * half_cols, wide), bf16),
            pltpu.VMEM((share, rows, wide), f32),
            pltpu.VMEM((col_size, share, own, LANES), f32),
            pltpu.VMEM((groups, own, LANES), f32),
            dma((192,)),
            dma((CHUNKS, col_size, seq_size)),
            dma((seq_size, CHUNKS)),
            dma((CHUNKS,)),
            dma((blocks,)),
            dma((members, CHUNKS)),
            dma((col_size, share // 2)),
            dma((2,)),
        ],
        compiler_params=pltpu.CompilerParams(
            collective_id=0, has_side_effects=True, vmem_limit_bytes=59 << 20
        ),
    )(*arrays)
    revised_alignment, revised_couplings = pl.pallas_call(
        finish_kernel,
        out_shape=(
            jax.ShapeDtypeStruct((seqs, own, depth), f32),
            jax.ShapeDtypeStruct((rows, cols, channels), f32),
        ),
        in_specs=[vmem] * 2,
        out_specs=(pl.BlockSpec(memory_space=pltpu.HBM),) * 2,
        scratch_shapes=[dma((2 * FINISH_CUTS,))],
        compiler_params=pltpu.CompilerParams(vmem_limit_bytes=12 << 20),
    )(alignment, couplings)
    return revised_alignment.reshape(alignment_tensor.shape), revised_couplings


def on_device(alignment_tensor, residue_couplings, first_factor_matrix, *rest):
    seqs, tiles, own, depth = alignment_tensor.shape
    rows, cols, channels = residue_couplings.shape
    row_size, col_size, seq_size = (lax.axis_size(a) for a in ("row", "col", "seq"))
    fits = (
        tiles == 1
        and rows == own * col_size == LANES
        and cols == own * seq_size
        and row_size * rows == col_size * cols
        and own % 16 == 0
        and seqs % 6 == 0
        and 2 * depth == channels == LANES
        and first_factor_matrix.shape[1] % (8 * CHUNKS) == 0
        and seqs % (4 * col_size) == 0
        and rest[3].shape[1] == 8 * LANES // 4
        and cols % (4 * CHUNKS) == 0
        and seq_size == row_size == 2
        and rest[2].shape[1] == 8 == own * own // LANES
        and seqs * seq_size <= LANES
        and seqs // 2 % (LANES // 2 // own) == 0
        and col_size == CHUNKS
    )
    path = fast_path if fits else general_path
    return path(alignment_tensor, residue_couplings, first_factor_matrix, *rest)


def solution(mesh):
    return jax.shard_map(
        on_device,
        mesh=mesh,
        in_specs=(
            P(("grp", "seq"), "row", "col", None),
            P(("grp", "row"), "col", None),
            P(),
            P(),
            P(),
            P(),
            P(),
            P(),
            P(),
        ),
        out_specs=(P(("grp", "seq"), "row", "col", None), P(("grp", "row"), "col", None)),
        check_vma=False,
    )
```

```python
import functools

import jax
import jax.numpy as jnp
from jax import lax
from jax.experimental import pallas as pl
from jax.experimental.pallas import tpu as pltpu
from jax.sharding import PartitionSpec as P

epsilon = 1e-05
exact_arithmetic = lax.Precision.HIGHEST


def broadcast(block, axis, holder):
    block = jnp.where(lax.axis_index(axis) == holder, block, jnp.zeros_like(block))
    return lax.psum(block, axis)


def standardize_entries(inputs):
    center = inputs - jnp.mean(inputs, axis=-1, keepdims=True)
    spread = jnp.mean(center * center, axis=-1, keepdims=True)
    return center / jnp.sqrt(spread + epsilon)


def pair_scores(pair_rows, coupling_score_matrix):
    return jnp.einsum(
        "ijc,ch->ihj",
        standardize_entries(pair_rows),
        coupling_score_matrix,
        precision=exact_arithmetic,
    )


def general_path(
    alignment_tensor,
    residue_couplings,
    first_factor_matrix,
    second_factor_matrix,
    tensor_product_matrix,
    coupling_score_matrix,
    averaged_source_matrix,
    sigmoid_matrix,
    final_matrix,
):
    shard_alignment_entries = alignment_tensor.shape[0]
    total_seqs = shard_alignment_entries * lax.axis_size("seq")
    coupling_lines = residue_couplings.shape[0]
    col_count = residue_couplings.shape[1]
    alignment_depth = alignment_tensor.shape[3]
    outer_width = first_factor_matrix.shape[1]
    head_count = coupling_score_matrix.shape[1]
    gathered_lines = lax.all_gather(alignment_tensor, "col", axis=2, tiled=True)
    alignment_tile_entries = gathered_lines.reshape(
        shard_alignment_entries, coupling_lines, alignment_depth
    )
    standardized_alignment = standardize_entries(alignment_tile_entries)
    first_factor_tile = jnp.einsum(
        "kgd,dl->kgl", standardized_alignment, first_factor_matrix, precision=exact_arithmetic
    )
    combined_matrix = jnp.concatenate([second_factor_matrix, averaged_source_matrix], axis=1)
    first_col = lax.axis_index("col") * col_count
    root_row = first_col // coupling_lines
    offset = first_col % coupling_lines
    raw_piece = lax.dynamic_slice_in_dim(alignment_tile_entries, offset, col_count, 1)
    raw_received = broadcast(raw_piece, "row", root_row)
    received = jnp.einsum(
        "pko,ol->pkl",
        standardize_entries(raw_received),
        combined_matrix,
        precision=exact_arithmetic,
    )
    second_factor_tile = received[:, :, :outer_width]
    averaged_sources = received[:, :, outer_width:].reshape(
        shard_alignment_entries, col_count, head_count, -1
    )
    block_rows = 16
    left_blocks = first_factor_tile.reshape(
        shard_alignment_entries, coupling_lines // block_rows, block_rows, outer_width
    ).transpose(1, 0, 2, 3)

    def outer_block(left_block):
        product = (
            jnp.einsum("sic,sje->ijce", left_block, second_factor_tile, precision=exact_arithmetic)
            / total_seqs
        )
        flat_prod = product.reshape(block_rows * col_count, -1)
        return jnp.dot(flat_prod, tensor_product_matrix, precision=exact_arithmetic).reshape(
            block_rows, col_count, -1
        )

    update = lax.map(outer_block, left_blocks).reshape(coupling_lines, col_count, -1)
    revised_couplings = residue_couplings + lax.psum(update, "seq")
    scores = pair_scores(revised_couplings, coupling_score_matrix)
    local_top = jnp.max(scores, axis=2)
    score_top = lax.pmax(local_top, "col")
    score_total = lax.psum(jnp.sum(jnp.exp(scores - score_top[:, :, None]), axis=2), "col")
    weights = jnp.exp(scores - score_top[:, :, None]) / score_total[:, :, None]
    mixed_rows = jnp.einsum(
        "ihj,sjhd->sihd", weights, averaged_sources, precision=exact_arithmetic
    ).reshape(shard_alignment_entries, coupling_lines, -1)
    summed = lax.psum_scatter(mixed_rows, "col", scatter_dimension=1, tiled=True)
    shard_standardized_alignment = standardize_entries(
        alignment_tensor.reshape(shard_alignment_entries, -1, alignment_depth)
    )
    sigmoid_factors = jax.nn.sigmoid(
        jnp.einsum(
            "pko,ol->pkl", shard_standardized_alignment, sigmoid_matrix, precision=exact_arithmetic
        )
    )
    coupling_increment = jnp.einsum(
        "snf,fc->snc", summed * sigmoid_factors, final_matrix, precision=exact_arithmetic
    )
    revised_alignment = alignment_tensor + coupling_increment.reshape(alignment_tensor.shape)
    return (revised_alignment, revised_couplings)


f32, bf16 = jnp.float32, jnp.bfloat16
LANES = 128
CHUNKS = 4
LEFT_REACH = 1
LOGIT_REACH = 1
GATHERED = 8
PAIRED = 4


def halves(values):
    high = values.astype(bf16)
    return high, (values - high.astype(f32)).astype(bf16)


def mm(a, b):
    return jnp.dot(a, b, preferred_element_type=f32)


def mm3(a, b):
    (a_high, a_low), (b_high, b_low) = a, b
    return mm(a_high, b_high) + (mm(a_high, b_low) + mm(a_low, b_high))


def nt(a, b):
    return lax.dot_general(a, b, (((1,), (1,)), ((), ())), preferred_element_type=f32)


def nt3(a, b):
    (a_high, a_low), (b_high, b_low) = a, b
    return nt(a_high, b_high) + (nt(a_high, b_low) + nt(a_low, b_high))


def block_kernel(
    row_size,
    col_size,
    seq_size,
    heads,
    raw_in,
    pair_in,
    first_in,
    second_in,
    product_in,
    score_in,
    source_in,
    gate_in,
    final_in,
    out_ref,
    revised_ref,
    raw_ref,
    pair_ref,
    first_ref,
    second_ref,
    product_ref,
    score_ref,
    source_ref,
    gate_ref,
    final_ref,
    load_sem,
    own_s,
    l_s,
    spread_s,
    r_own,
    hop_s,
    r_s,
    left_s,
    right_s,
    high_s,
    low_s,
    product_s,
    turned_s,
    x_s,
    logit_s,
    weight_s,
    mixer_s,
    v_high_s,
    v_low_s,
    gates_s,
    part_s,
    whole_s,
    send_sem,
    l_recv,
    r_recv,
    hop_recv,
    x_recv,
    logit_recv,
    part_recv,
    pair_sem,
):
    loads = []
    for source, place in (
        (raw_in, raw_ref),
        (second_in, second_ref),
        (first_in, first_ref),
        (pair_in, pair_ref),
        (product_in, product_ref),
        (source_in, source_ref),
        (gate_in, gate_ref),
        (score_in, score_ref),
        (final_in, final_ref),
    ):
        loads.append(pltpu.make_async_copy(source, place, load_sem.at[len(loads)]))
        loads[-1].start()
    seqs, own, depth = raw_ref.shape
    groups = seqs // 2
    rows, cols, channels = revised_ref.shape
    outer = first_ref.shape[0]
    half_cols = cols // seq_size
    total = seqs * seq_size
    wide = 2 * source_ref.shape[1]
    members = col_size * seq_size
    tokens_all = members * half_cols
    share = groups // col_size
    row, col, seq = (lax.axis_index(a) for a in ("row", "col", "seq"))
    other_row, other_seq = 1 - row, 1 - seq
    me = col * seq_size + seq
    mine = row * col_size + col
    mesh_ids = pl.DeviceIdType.MESH

    barrier = pltpu.get_barrier_semaphore()

    def member(offset):
        other = lax.rem(me + offset, members)
        return {"col": other // seq_size, "seq": lax.rem(other, seq_size)}

    for offset in range(1, members):
        pl.semaphore_signal(barrier, inc=1, device_id=member(offset), device_id_type=mesh_ids)
    pl.semaphore_signal(barrier, inc=1, device_id={"row": other_row}, device_id_type=mesh_ids)

    for load in loads[:3]:
        load.wait()

    def normalize(step, carry):
        parts = []
        for t in range(2):
            part = standardize_entries(raw_ref[step + t * groups])
            parts.append(part)
        at = pl.ds(pl.multiple_of(step * own, own), own)
        own_s[at, :] = jnp.concatenate(parts, axis=-1)
        return carry

    lax.fori_loop(0, groups, normalize, 0, unroll=4)

    first = halves(twice(first_ref[...]))
    second = halves(twice(second_ref[...]))
    span = LANES // 2
    packs = LANES // outer
    sets = half_cols // packs
    x_high, x_low = halves(own_s[...])
    projected = nt(x_high, second[0]) + (nt(x_high, second[1]) + nt(x_low, second[0]))
    for t in range(2):
        spread_s[:, t * outer : (t + 1) * outer] = projected[:, t * outer : (t + 1) * outer]

    def pack_right(step, carry):
        tokens = [spread_s[pl.ds(packs * step + u, groups, stride=own), :] for u in range(packs)]
        for t in range(2):
            line = jnp.concatenate([token[:, t * outer : (t + 1) * outer] for token in tokens], axis=1)
            r_own[step, t * groups : (t + 1) * groups, :] = line
        return carry

    lax.fori_loop(0, sets, pack_right, 0, unroll=2)

    started = []

    def run(condition, action):
        if condition is None:
            action()
        else:
            pl.when(condition)(action)

    def both(a, b):
        return b if a is None else (a if b is None else jnp.logical_and(a, b))

    def ship(source, place, target, sem, condition=None):
        copy = pltpu.make_async_remote_copy(
            src_ref=source,
            dst_ref=place,
            send_sem=send_sem.at[len(started)],
            recv_sem=sem,
            device_id=target,
            device_id_type=mesh_ids,
        )
        started.append((copy, condition))
        run(condition, copy.start)

    def arrived(place, sem, condition=None):
        copy = pltpu.make_async_remote_copy(
            src_ref=place,
            dst_ref=place,
            send_sem=send_sem.at[0],
            recv_sem=sem,
            device_id={"row": other_row},
            device_id_type=mesh_ids,
        )
        run(condition, copy.wait_recv)

    pl.semaphore_wait(barrier, members)
    column_slot = me
    here = column_slot // col_size == row
    elsewhere = jnp.logical_not(here)
    other_mine = other_row * col_size + col
    cut = sets // CHUNKS
    straight, crossed = range(CHUNKS // 2), range(CHUNKS // 2, CHUNKS)

    def right_target(block):
        return {"col": block // seq_size, "seq": lax.rem(block, seq_size)}

    own_right = column_slot == mine
    own_crossed = column_slot == other_mine
    for j in crossed:
        at = pl.ds(j * cut, cut)
        ship(r_own.at[at], hop_s.at[at], {"row": other_row}, hop_recv.at[j])
    for j in straight:
        at = pl.ds(j * cut, cut)
        ship(
            r_own.at[at],
            r_s.at[seq, at],
            right_target(mine),
            r_recv.at[seq, j],
            jnp.logical_not(own_right),
        )

    chunk = outer // CHUNKS
    pairs = LANES // 2 // own
    left_steps = groups // pairs

    def project_left(step, carry):
        parts = []
        for t in range(pairs):
            at = pl.ds(pl.multiple_of((t * left_steps + step) * own, own), own)
            result = nt3(first, halves(own_s[at, :]))
            parts += [result[:outer], result[outer:]]
        line = jnp.concatenate(parts, axis=1)
        at = pl.ds(pl.multiple_of(step * chunk, chunk), chunk)
        for k in range(CHUNKS):
            l_s[k, col, seq, at, :] = line[k * chunk : (k + 1) * chunk]
        return carry

    lax.fori_loop(0, left_steps, project_left, 0, unroll=4)

    def relay_left(k, at, rightward, leftward, exists):
        place, sem = l_s.at[k, at, seq], l_recv.at[k, at, seq]
        if rightward:
            ship(place, place, {"col": col + 1}, sem, both(exists, col < col_size - 1))
        if leftward:
            ship(place, place, {"col": col - 1}, sem, both(exists, col > 0))
        ship(place, place, {"seq": other_seq}, sem, exists)

    def relay(place_of, k, distance, reach):
        for sign in (-1, 1):
            at = col + sign * distance
            exists = at >= 0 if sign < 0 else at < col_size
            place, sem = place_of(k, at)
            if distance:
                arrived(place, sem, exists)
            first_hop, last_hop = (reach, 1) if distance == 0 else (1, 1 if distance >= reach else 0)
            for hop in range(first_hop, 0, -1) if last_hop else ():
                onward = col - sign * hop
                inside = onward < col_size if sign < 0 else onward >= 0
                ship(place, place, {"col": onward}, sem, both(exists, inside) if distance else inside)
            if distance or sign < 0:
                ship(place, place, {"seq": other_seq}, sem, exists if distance else None)

    def stage(k, distance, reach):
        return k + max(0, distance - reach)

    def left_of(k, at):
        return l_s.at[k, at, seq], l_recv.at[k, at, seq]

    def left_slot(slot):
        for distance in range(1, col_size):
            for k in range(CHUNKS):
                if stage(k, distance, LEFT_REACH) == slot:
                    relay(left_of, k, distance, LEFT_REACH)
        if slot + 2 < CHUNKS:
            relay(left_of, slot + 2, 0, LEFT_REACH)

    relay(left_of, 0, 0, LEFT_REACH)
    relay(left_of, 1, 0, LEFT_REACH)

    for load in loads[3:]:
        load.wait()
    first_col = seq * half_cols
    flat_pair = pair_ref.reshape(rows * cols, channels)
    flat_revised = revised_ref.reshape(rows * cols, channels)

    def turn_in(column, carry):
        turned_s[column] = flat_pair[pl.ds(first_col + column, rows, stride=cols), :].T
        return carry

    lax.fori_loop(0, half_cols // 2, turn_in, 0, unroll=2)

    @pl.when(own_right)
    def _():
        for j in straight:
            r_s[seq, j * cut : (j + 1) * cut] = r_own[j * cut : (j + 1) * cut]

    for j in crossed:
        at = pl.ds(j * cut, cut)
        arrived(hop_s.at[at], hop_recv.at[j])
        ship(
            hop_s.at[at],
            r_s.at[seq, at],
            right_target(other_mine),
            r_recv.at[seq, j],
            jnp.logical_not(own_crossed),
        )

    @pl.when(own_crossed)
    def _():
        for j in crossed:
            r_s[seq, j * cut : (j + 1) * cut] = hop_s[j * cut : (j + 1) * cut]

    left_slot(0)
    source_here = lax.rem(column_slot, col_size) == col
    for js, kind in ((straight, here), (crossed, elsewhere)):
        for j in js:
            for source in range(seq_size):
                kept = jnp.logical_and(source_here, seq == source)
                place, sem = r_s.at[source, pl.ds(j * cut, cut)], r_recv.at[source, j]
                arrived(place, sem, jnp.logical_and(kind, jnp.logical_not(kept)))
                ship(place, place, {"row": other_row}, sem, kind)
    blank = jnp.zeros(((span - seqs) * chunk, rows), f32)
    for k in range(CHUNKS):
        for source in range(seq_size):
            left_s[k, (source * span + seqs) * chunk : (source + 1) * span * chunk, :] = blank
    lax.fori_loop(half_cols // 2, half_cols, turn_in, 0, unroll=2)
    left_slot(1)
    t_high, t_low = halves(product_ref[...].T * (1.0 / total))
    product_s[...] = jnp.concatenate([t_high, t_low], axis=0)
    c_high, c_low = halves(score_ref[...])
    c_both = jnp.concatenate([c_high, c_low], axis=0)
    x_s[mine] = own_s[pl.ds(pl.multiple_of(col * share * own, share * own), share * own), :]
    left_slot(2)

    for js, kind in ((straight, elsewhere), (crossed, here)):
        for j in js:
            for source in range(seq_size):
                arrived(r_s.at[source, pl.ds(j * cut, cut)], r_recv.at[source, j], kind)
    empty = jnp.zeros((span - seqs, LANES), f32)

    def turn_right(step, carry):
        lines = [part for source in range(seq_size) for part in (r_s[source, step], empty)]
        at = pl.ds(pl.multiple_of(step * LANES, LANES), LANES)
        right_s[at, :] = jnp.concatenate(lines, axis=0).T
        return carry

    lax.fori_loop(0, sets, turn_right, 0, unroll=2)
    r_high, r_low = halves(right_s[...])
    r_both = jnp.concatenate([r_high, r_low], axis=1)

    def chunk_arrived(k):
        for at in range(col_size):
            arrived(l_s.at[k, at, other_seq], l_recv.at[k, at, other_seq])

    def place_left(k, step):
        at = pl.ds(pl.multiple_of(step * chunk, chunk), chunk)
        for source in range(seq_size):
            blocks = [l_s[k, t, source, at, :] for t in range(col_size)]
            for t in range(pairs):
                for half in range(2):
                    lane = (2 * t + half) * own
                    line = jnp.concatenate([block[:, lane : lane + own] for block in blocks], axis=1)
                    place = source * span + half * groups + t * left_steps + step
                    left_s[k, pl.ds(pl.multiple_of(place * chunk, chunk), chunk), :] = line

    def outer_chunk(k):
        def outer_step(step, carry):
            pieces = [left_s[k, pl.ds(2 * step + t, LANES, stride=chunk), :] for t in range(2)]
            l_high, l_low = halves(jnp.concatenate(pieces, axis=1))
            product = mm(r_both, jnp.concatenate([l_high, l_high], axis=0)) + mm(r_high, l_low)
            p_high, p_low = halves(product)
            for t in range(2):
                high_s[2 * step + t] = p_high[:, t * rows : (t + 1) * rows]
                low_s[2 * step + t] = p_low[:, t * rows : (t + 1) * rows]
            return carry

        lax.fori_loop(0, chunk // 2, outer_step, 0, unroll=2)

    def project(k, step):
        def block(ref):
            pieces = [
                ref[:, pl.ds(pl.multiple_of((2 * step + t) * outer, outer), outer), :].reshape(chunk * outer, rows)
                for t in range(2)
            ]
            return jnp.concatenate(pieces, axis=1)

        t_both = product_s[:, k * chunk * outer : (k + 1) * chunk * outer]
        joint = mm(t_both, block(high_s))
        update = joint[:channels] + (joint[channels:] + mm(t_both[:channels], block(low_s)))
        return jnp.concatenate([turned_s[2 * step + t] for t in range(2)], axis=1) + update

    def send_x():
        for offset in range(1, col_size):
            target = lax.rem(col + offset, col_size)
            ship(
                own_s.at[pl.ds(pl.multiple_of(target * share * own, share * own), share * own), :],
                x_s.at[mine],
                {"col": target},
                x_recv.at[mine],
            )
        ship(x_s.at[mine], x_s.at[mine], {"row": other_row}, x_recv.at[mine])

    chunk_arrived(0)

    def place_first(step, carry):
        place_left(0, step)
        return carry

    lax.fori_loop(0, left_steps, place_first, 0, unroll=6)
    for k in range(CHUNKS - 1):
        left_slot(k + CHUNKS - 1)
        outer_chunk(k)
        chunk_arrived(k + 1)
        if k == 1:
            send_x()

        def gather_step(turn, carry):
            steps = [GATHERED * turn + u for u in range(GATHERED)]
            share_steps = left_steps * 2 * GATHERED // half_cols
            for u in range(share_steps):
                place_left(k + 1, share_steps * turn + u)
            for step, revised in [(step, project(k, step)) for step in steps]:
                for t in range(2):
                    turned_s[2 * step + t] = revised[:, t * rows : (t + 1) * rows]
            return carry

        lax.fori_loop(0, half_cols // 2 // GATHERED, gather_step, 0)
    outer_chunk(CHUNKS - 1)

    def pair_step(turn, carry):
        steps = [PAIRED * turn + u for u in range(PAIRED)]
        results = []
        for step in steps:
            revised = project(CHUNKS - 1, step)
            center = revised - jnp.mean(revised, axis=0, keepdims=True)
            spread = jnp.mean(center * center, axis=0, keepdims=True)
            n_high, n_low = halves(center)
            turned = mm(c_both, n_high)
            logits = turned[:heads] + (turned[heads:] + mm(c_high, n_low))
            results.append((step, revised, logits / jnp.sqrt(spread + epsilon)))
        for step, revised, logits in results:
            for t in range(2):
                turned_s[2 * step + t] = revised[:, t * rows : (t + 1) * rows]
                logit_s[me, 2 * step + t] = logits[:, t * rows : (t + 1) * rows]
        return carry

    section = half_cols // CHUNKS

    def logits_of(k, at):
        slot = at * seq_size + seq
        return logit_s.at[slot, pl.ds(k * section, section)], logit_recv.at[slot, k]

    def logit_slot(slot):
        for distance in range(1, col_size):
            for k in range(CHUNKS):
                if stage(k, distance, LOGIT_REACH) == slot:
                    relay(logits_of, k, distance, LOGIT_REACH)

    for k in range(CHUNKS):
        lax.fori_loop(k * section // 2 // PAIRED, (k + 1) * section // 2 // PAIRED, pair_step, 0)
        relay(logits_of, k, 0, LOGIT_REACH)
        if k == 2:
            for offset in range(1, col_size):
                at = row * col_size + lax.rem(col + offset, col_size)
                arrived(x_s.at[at], x_recv.at[at])
                ship(x_s.at[at], x_s.at[at], {"row": other_row}, x_recv.at[at])
    logit_slot(0)

    def turn_out(column, carry):
        flat_revised[pl.ds(first_col + column, rows, stride=cols), :] = turned_s[column].T
        return carry

    lax.fori_loop(0, half_cols // 2, turn_out, 0, unroll=4)
    logit_slot(1)
    lax.fori_loop(half_cols // 2, half_cols, turn_out, 0, unroll=4)
    half_pair = revised_ref.at[:, pl.ds(pl.multiple_of(first_col, half_cols), half_cols), :]
    pair_copy = pltpu.make_async_remote_copy(
        src_ref=half_pair,
        dst_ref=half_pair,
        send_sem=pair_sem.at[0],
        recv_sem=pair_sem.at[1],
        device_id={"seq": other_seq},
        device_id_type=mesh_ids,
    )
    pair_copy.start()
    logit_slot(2)

    def spread_heads(matrix):
        width = matrix.shape[1] // heads
        zero = jnp.zeros((matrix.shape[0], width), f32)
        upper, lower = [], []
        for head in range(heads):
            piece = matrix[:, head * width : (head + 1) * width]
            upper += [piece, zero]
            lower += [zero, piece]
        return jnp.concatenate([jnp.concatenate(upper, axis=1), jnp.concatenate(lower, axis=1)], axis=0)

    g_high, g_low = halves(spread_heads(gate_ref[...]))
    g_twice = jnp.concatenate([g_high, g_high], axis=0)

    def gate_step(group, carry):
        at = pl.ds(pl.multiple_of(group * own, own), own)
        x_high, x_low = halves(x_s[pl.ds(row * col_size, col_size), at, :].reshape(rows, LANES))
        inner = mm(jnp.concatenate([x_high, x_low], axis=1), g_twice) + mm(x_high, g_low)
        gates_s[group] = jax.nn.sigmoid(inner)
        return carry

    lax.fori_loop(0, share, gate_step, 0, unroll=2)
    logit_slot(3)
    for at in range(col_size):
        arrived(x_s.at[other_row * col_size + at], x_recv.at[other_row * col_size + at])
    s_high, s_low = halves(spread_heads(source_ref[...]))
    s_twice = jnp.concatenate([s_high, s_high], axis=0)

    def value_step(group, carry):
        at = pl.ds(pl.multiple_of(group * own, own), own)
        x_high, x_low = halves(x_s[:, at, :].reshape(tokens_all, LANES))
        values = mm(jnp.concatenate([x_high, x_low], axis=1), s_twice) + mm(x_high, s_low)
        v_high, v_low = halves(values)
        v_high_s[group] = v_high
        v_low_s[group] = v_low
        return carry

    lax.fori_loop(0, share // 3, value_step, 0, unroll=2)
    logit_slot(4)
    lax.fori_loop(share // 3, share, value_step, 0, unroll=2)
    f_halves = halves(spread_heads(final_ref[...]))
    for slot in range(5, CHUNKS + col_size - 2):
        logit_slot(slot)
    for k in range(CHUNKS):
        for at in range(col_size):
            slot = at * seq_size + other_seq
            arrived(logit_s.at[slot, pl.ds(k * section, section)], logit_recv.at[slot, k])

    logits = logit_s[...].reshape(tokens_all, heads, rows)
    powers = jnp.exp(logits - jnp.max(logits, axis=0)[None])
    weights = powers * (1.0 / jnp.sum(powers, axis=0))[None]
    weight_s[...] = weights.reshape(tokens_all * heads, rows)
    for head in range(heads):
        w_high, w_low = halves(weight_s[pl.ds(head, tokens_all, stride=heads), :].T)
        at = head % 2 * rows
        mixer_s[head // 2, at : at + rows, :] = w_high
        mixer_s[head // 2, 2 * rows + at : 2 * rows + at + rows, :] = w_low
    lane_head = lax.broadcasted_iota(jnp.int32, (rows, 2 * LANES), 1) % LANES
    upper_head = lane_head < LANES // 2

    for turn in range(share // 2):
        parts = []
        for p in range(heads // 2):
            lanes = slice(p * LANES, (p + 1) * LANES)
            v_high, v_low = (
                jnp.concatenate([ref[2 * turn + t, :, lanes] for t in range(2)], axis=1)
                for ref in (v_high_s, v_low_s)
            )
            joint = mm(mixer_s[p], v_high)
            full = joint[: 2 * rows] + (joint[2 * rows :] + mm(mixer_s[p, : 2 * rows, :], v_low))
            parts.append(jnp.where(upper_head, full[:rows], full[rows:]))
        mixed = []
        for t in range(2):
            line = jnp.concatenate([part[:, t * LANES : (t + 1) * LANES] for part in parts], axis=1)
            mixed.append(line * gates_s[2 * turn + t])
        result = nt3(halves(jnp.concatenate(mixed, axis=0)), f_halves)
        for t in range(2):
            part_s[:, 2 * turn + t] = result[t * rows : (t + 1) * rows].reshape(col_size, own, LANES)
        at = pl.ds(col * share + 2 * turn, 2)
        for offset in range(1, col_size):
            target = lax.rem(col + offset, col_size)
            ship(
                part_s.at[target, pl.ds(2 * turn, 2)],
                whole_s.at[at],
                {"col": target},
                part_recv.at[col, turn],
            )
        whole_s[at] = part_s[col, 2 * turn : 2 * turn + 2]

    for offset in range(1, col_size):
        source = lax.rem(col + offset, col_size)
        for turn in range(share // 2):
            arrived(whole_s.at[pl.ds(source * share + 2 * turn, 2)], part_recv.at[source, turn])
    for t in range(2):
        at = pl.ds(t * groups, groups)
        out_ref[at] = raw_ref[at] + whole_s[:, :, t * depth : (t + 1) * depth]

    for copy, condition in started:
        run(condition, copy.wait_send)
    pair_copy.wait_send()
    other_half = revised_ref.at[:, pl.ds(pl.multiple_of(other_seq * half_cols, half_cols), half_cols), :]
    arrived(other_half, pair_sem.at[1])


def twice(matrix):
    zero = jnp.zeros_like(matrix)
    return jnp.concatenate(
        [jnp.concatenate([matrix, zero], axis=1), jnp.concatenate([zero, matrix], axis=1)], axis=0
    )


FINISH_CUTS = 4


def finish_kernel(*refs):
    count = len(refs) // 2
    copies = []
    for source, target in zip(refs[:count], refs[count:-1]):
        share = source.shape[0] // FINISH_CUTS
        for cut in range(FINISH_CUTS):
            at = pl.ds(cut * share, share)
            copies.append(pltpu.make_async_copy(source.at[at], target.at[at], refs[-1].at[len(copies)]))
            copies[-1].start()
    for copy in copies:
        copy.wait()


def fast_path(
    alignment_tensor,
    residue_couplings,
    first_factor_matrix,
    second_factor_matrix,
    tensor_product_matrix,
    coupling_score_matrix,
    averaged_source_matrix,
    sigmoid_matrix,
    final_matrix,
):
    seqs, _, own, depth = alignment_tensor.shape
    rows, cols, channels = residue_couplings.shape
    outer = first_factor_matrix.shape[1]
    heads = coupling_score_matrix.shape[1]
    row_size, col_size, seq_size = (lax.axis_size(a) for a in ("row", "col", "seq"))
    blocks = row_size * col_size
    half_cols = cols // seq_size
    members = col_size * seq_size
    groups = seqs // 2
    wide = 2 * averaged_source_matrix.shape[1]
    share = groups // col_size
    vmem = pl.BlockSpec(memory_space=pltpu.VMEM)
    dma = pltpu.SemaphoreType.DMA
    arrays = (
        alignment_tensor.reshape(seqs, own, depth),
        residue_couplings,
        first_factor_matrix.T,
        second_factor_matrix.T,
        tensor_product_matrix,
        coupling_score_matrix.T,
        averaged_source_matrix,
        sigmoid_matrix,
        final_matrix.T,
    )
    alignment, couplings = pl.pallas_call(
        functools.partial(block_kernel, row_size, col_size, seq_size, heads),
        out_shape=(
            pltpu.VMEM((seqs, own, depth), f32),
            pltpu.VMEM((rows, cols, channels), f32),
        ),
        in_specs=[pl.BlockSpec(memory_space=pltpu.HBM)] * 9,
        out_specs=(vmem, vmem),
        scratch_shapes=[pltpu.VMEM(a.shape, f32) for a in arrays]
        + [
            dma((len(arrays),)),
            pltpu.VMEM((groups * own, LANES), f32),
            pltpu.VMEM((CHUNKS, col_size, seq_size, groups // (LANES // 2 // own) * outer // CHUNKS, LANES), f32),
            pltpu.VMEM((groups * own, LANES), f32),
            pltpu.VMEM((half_cols * outer // LANES, seqs, LANES), f32),
            pltpu.VMEM((half_cols * outer // LANES, seqs, LANES), f32),
            pltpu.VMEM((seq_size, half_cols * outer // LANES, seqs, LANES), f32),
            pltpu.VMEM((CHUNKS, LANES * outer // CHUNKS, rows), f32),
            pltpu.VMEM((half_cols * outer, LANES), f32),
            pltpu.VMEM((outer // CHUNKS, half_cols * outer, rows), bf16),
            pltpu.VMEM((outer // CHUNKS, half_cols * outer, rows), bf16),
            pltpu.VMEM((2 * channels, outer * outer), bf16),
            pltpu.VMEM((half_cols, channels, rows), f32),
            pltpu.VMEM((blocks, share * own, LANES), f32),
            pltpu.VMEM((members, half_cols, heads, rows), f32),
            pltpu.VMEM((members * half_cols * heads, rows), f32),
            pltpu.VMEM((heads // 2, 4 * rows, members * half_cols), bf16),
            pltpu.VMEM((share, members * half_cols, wide), bf16),
            pltpu.VMEM((share, members * half_cols, wide), bf16),
            pltpu.VMEM((share, rows, wide), f32),
            pltpu.VMEM((col_size, share, own, LANES), f32),
            pltpu.VMEM((groups, own, LANES), f32),
            dma((192,)),
            dma((CHUNKS, col_size, seq_size)),
            dma((seq_size, CHUNKS)),
            dma((CHUNKS,)),
            dma((blocks,)),
            dma((members, CHUNKS)),
            dma((col_size, share // 2)),
            dma((2,)),
        ],
        compiler_params=pltpu.CompilerParams(
            collective_id=0, has_side_effects=True, vmem_limit_bytes=59 << 20
        ),
    )(*arrays)
    revised_alignment, revised_couplings = pl.pallas_call(
        finish_kernel,
        out_shape=(
            jax.ShapeDtypeStruct((seqs, own, depth), f32),
            jax.ShapeDtypeStruct((rows, cols, channels), f32),
        ),
        in_specs=[vmem] * 2,
        out_specs=(pl.BlockSpec(memory_space=pltpu.HBM),) * 2,
        scratch_shapes=[dma((2 * FINISH_CUTS,))],
        compiler_params=pltpu.CompilerParams(vmem_limit_bytes=12 << 20),
    )(alignment, couplings)
    return revised_alignment.reshape(alignment_tensor.shape), revised_couplings


def on_device(alignment_tensor, residue_couplings, first_factor_matrix, *rest):
    seqs, tiles, own, depth = alignment_tensor.shape
    rows, cols, channels = residue_couplings.shape
    row_size, col_size, seq_size = (lax.axis_size(a) for a in ("row", "col", "seq"))
    fits = (
        tiles == 1
        and rows == own * col_size == LANES
        and cols == own * seq_size
        and row_size * rows == col_size * cols
        and own % 16 == 0
        and seqs % 6 == 0
        and 2 * depth == channels == LANES
        and first_factor_matrix.shape[1] % (8 * CHUNKS) == 0
        and seqs % (4 * col_size) == 0
        and rest[3].shape[1] == 8 * LANES // 4
        and cols % (4 * CHUNKS) == 0
        and seq_size == row_size == 2
        and rest[2].shape[1] == 8 == own * own // LANES
        and seqs * seq_size <= LANES
        and seqs // 2 % (LANES // 2 // own) == 0
        and col_size == CHUNKS
    )
    path = fast_path if fits else general_path
    return path(alignment_tensor, residue_couplings, first_factor_matrix, *rest)


def solution(mesh):
    return jax.shard_map(
        on_device,
        mesh=mesh,
        in_specs=(
            P(("grp", "seq"), "row", "col", None),
            P(("grp", "row"), "col", None),
            P(),
            P(),
            P(),
            P(),
            P(),
            P(),
            P(),
        ),
        out_specs=(P(("grp", "seq"), "row", "col", None), P(("grp", "row"), "col", None)),
        check_vma=False,
    )
```

```python
import functools

import jax
import jax.numpy as jnp
from jax import lax
from jax.experimental import pallas as pl
from jax.experimental.pallas import tpu as pltpu
from jax.sharding import PartitionSpec as P

epsilon = 1e-05
exact_arithmetic = lax.Precision.HIGHEST


def broadcast(block, axis, holder):
    block = jnp.where(lax.axis_index(axis) == holder, block, jnp.zeros_like(block))
    return lax.psum(block, axis)


def standardize_entries(inputs):
    center = inputs - jnp.mean(inputs, axis=-1, keepdims=True)
    spread = jnp.mean(center * center, axis=-1, keepdims=True)
    return center / jnp.sqrt(spread + epsilon)


def pair_scores(pair_rows, coupling_score_matrix):
    return jnp.einsum(
        "ijc,ch->ihj",
        standardize_entries(pair_rows),
        coupling_score_matrix,
        precision=exact_arithmetic,
    )


def general_path(
    alignment_tensor,
    residue_couplings,
    first_factor_matrix,
    second_factor_matrix,
    tensor_product_matrix,
    coupling_score_matrix,
    averaged_source_matrix,
    sigmoid_matrix,
    final_matrix,
):
    shard_alignment_entries = alignment_tensor.shape[0]
    total_seqs = shard_alignment_entries * lax.axis_size("seq")
    coupling_lines = residue_couplings.shape[0]
    col_count = residue_couplings.shape[1]
    alignment_depth = alignment_tensor.shape[3]
    outer_width = first_factor_matrix.shape[1]
    head_count = coupling_score_matrix.shape[1]
    gathered_lines = lax.all_gather(alignment_tensor, "col", axis=2, tiled=True)
    alignment_tile_entries = gathered_lines.reshape(
        shard_alignment_entries, coupling_lines, alignment_depth
    )
    standardized_alignment = standardize_entries(alignment_tile_entries)
    first_factor_tile = jnp.einsum(
        "kgd,dl->kgl", standardized_alignment, first_factor_matrix, precision=exact_arithmetic
    )
    combined_matrix = jnp.concatenate([second_factor_matrix, averaged_source_matrix], axis=1)
    first_col = lax.axis_index("col") * col_count
    root_row = first_col // coupling_lines
    offset = first_col % coupling_lines
    raw_piece = lax.dynamic_slice_in_dim(alignment_tile_entries, offset, col_count, 1)
    raw_received = broadcast(raw_piece, "row", root_row)
    received = jnp.einsum(
        "pko,ol->pkl",
        standardize_entries(raw_received),
        combined_matrix,
        precision=exact_arithmetic,
    )
    second_factor_tile = received[:, :, :outer_width]
    averaged_sources = received[:, :, outer_width:].reshape(
        shard_alignment_entries, col_count, head_count, -1
    )
    block_rows = 16
    left_blocks = first_factor_tile.reshape(
        shard_alignment_entries, coupling_lines // block_rows, block_rows, outer_width
    ).transpose(1, 0, 2, 3)

    def outer_block(left_block):
        product = (
            jnp.einsum("sic,sje->ijce", left_block, second_factor_tile, precision=exact_arithmetic)
            / total_seqs
        )
        flat_prod = product.reshape(block_rows * col_count, -1)
        return jnp.dot(flat_prod, tensor_product_matrix, precision=exact_arithmetic).reshape(
            block_rows, col_count, -1
        )

    update = lax.map(outer_block, left_blocks).reshape(coupling_lines, col_count, -1)
    revised_couplings = residue_couplings + lax.psum(update, "seq")
    scores = pair_scores(revised_couplings, coupling_score_matrix)
    local_top = jnp.max(scores, axis=2)
    score_top = lax.pmax(local_top, "col")
    score_total = lax.psum(jnp.sum(jnp.exp(scores - score_top[:, :, None]), axis=2), "col")
    weights = jnp.exp(scores - score_top[:, :, None]) / score_total[:, :, None]
    mixed_rows = jnp.einsum(
        "ihj,sjhd->sihd", weights, averaged_sources, precision=exact_arithmetic
    ).reshape(shard_alignment_entries, coupling_lines, -1)
    summed = lax.psum_scatter(mixed_rows, "col", scatter_dimension=1, tiled=True)
    shard_standardized_alignment = standardize_entries(
        alignment_tensor.reshape(shard_alignment_entries, -1, alignment_depth)
    )
    sigmoid_factors = jax.nn.sigmoid(
        jnp.einsum(
            "pko,ol->pkl", shard_standardized_alignment, sigmoid_matrix, precision=exact_arithmetic
        )
    )
    coupling_increment = jnp.einsum(
        "snf,fc->snc", summed * sigmoid_factors, final_matrix, precision=exact_arithmetic
    )
    revised_alignment = alignment_tensor + coupling_increment.reshape(alignment_tensor.shape)
    return (revised_alignment, revised_couplings)


f32, bf16 = jnp.float32, jnp.bfloat16
LANES = 128
CHUNKS = 4
LEFT_REACH = 1
LOGIT_REACH = 1
GATHERED = 8
PAIRED = 4


def halves(values):
    high = values.astype(bf16)
    return high, (values - high.astype(f32)).astype(bf16)


def mm(a, b):
    return jnp.dot(a, b, preferred_element_type=f32)


def mm3(a, b):
    (a_high, a_low), (b_high, b_low) = a, b
    return mm(a_high, b_high) + (mm(a_high, b_low) + mm(a_low, b_high))


def nt(a, b):
    return lax.dot_general(a, b, (((1,), (1,)), ((), ())), preferred_element_type=f32)


def nt3(a, b):
    (a_high, a_low), (b_high, b_low) = a, b
    return nt(a_high, b_high) + (nt(a_high, b_low) + nt(a_low, b_high))


def block_kernel(
    row_size,
    col_size,
    seq_size,
    heads,
    raw_in,
    pair_in,
    first_in,
    second_in,
    product_in,
    score_in,
    source_in,
    gate_in,
    final_in,
    out_ref,
    revised_ref,
    raw_ref,
    pair_ref,
    first_ref,
    second_ref,
    product_ref,
    score_ref,
    source_ref,
    gate_ref,
    final_ref,
    load_sem,
    own_s,
    l_s,
    spread_s,
    r_own,
    hop_s,
    r_s,
    left_s,
    right_s,
    high_s,
    low_s,
    product_s,
    turned_s,
    x_s,
    logit_s,
    weight_s,
    mixer_s,
    v_high_s,
    v_low_s,
    gates_s,
    part_s,
    whole_s,
    send_sem,
    l_recv,
    r_recv,
    hop_recv,
    x_recv,
    logit_recv,
    part_recv,
    pair_sem,
):
    loads = []
    for source, place in (
        (raw_in, raw_ref),
        (second_in, second_ref),
        (first_in, first_ref),
        (pair_in, pair_ref),
        (product_in, product_ref),
        (source_in, source_ref),
        (gate_in, gate_ref),
        (score_in, score_ref),
        (final_in, final_ref),
    ):
        loads.append(pltpu.make_async_copy(source, place, load_sem.at[len(loads)]))
        loads[-1].start()
    seqs, own, depth = raw_ref.shape
    groups = seqs // 2
    rows, cols, channels = revised_ref.shape
    outer = first_ref.shape[0]
    half_cols = cols // seq_size
    total = seqs * seq_size
    wide = 2 * source_ref.shape[1]
    members = col_size * seq_size
    tokens_all = members * half_cols
    share = groups // col_size
    row, col, seq = (lax.axis_index(a) for a in ("row", "col", "seq"))
    other_row, other_seq = 1 - row, 1 - seq
    me = col * seq_size + seq
    mine = row * col_size + col
    mesh_ids = pl.DeviceIdType.MESH

    barrier = pltpu.get_barrier_semaphore()

    def member(offset):
        other = lax.rem(me + offset, members)
        return {"col": other // seq_size, "seq": lax.rem(other, seq_size)}

    for offset in range(1, members):
        pl.semaphore_signal(barrier, inc=1, device_id=member(offset), device_id_type=mesh_ids)
    pl.semaphore_signal(barrier, inc=1, device_id={"row": other_row}, device_id_type=mesh_ids)

    for load in loads[:3]:
        load.wait()

    def normalize(step, carry):
        parts = []
        for t in range(2):
            part = standardize_entries(raw_ref[step + t * groups])
            parts.append(part)
        at = pl.ds(pl.multiple_of(step * own, own), own)
        own_s[at, :] = jnp.concatenate(parts, axis=-1)
        return carry

    lax.fori_loop(0, groups, normalize, 0, unroll=4)

    first = halves(twice(first_ref[...]))
    second = halves(twice(second_ref[...]))
    span = LANES // 2
    packs = LANES // outer
    sets = half_cols // packs
    x_high, x_low = halves(own_s[...])
    projected = nt(x_high, second[0]) + (nt(x_high, second[1]) + nt(x_low, second[0]))
    for t in range(2):
        spread_s[:, t * outer : (t + 1) * outer] = projected[:, t * outer : (t + 1) * outer]

    def pack_right(step, carry):
        tokens = [spread_s[pl.ds(packs * step + u, groups, stride=own), :] for u in range(packs)]
        for t in range(2):
            line = jnp.concatenate([token[:, t * outer : (t + 1) * outer] for token in tokens], axis=1)
            r_own[step, t * groups : (t + 1) * groups, :] = line
        return carry

    lax.fori_loop(0, sets, pack_right, 0, unroll=2)

    started = []

    def run(condition, action):
        if condition is None:
            action()
        else:
            pl.when(condition)(action)

    def both(a, b):
        return b if a is None else (a if b is None else jnp.logical_and(a, b))

    def ship(source, place, target, sem, condition=None):
        copy = pltpu.make_async_remote_copy(
            src_ref=source,
            dst_ref=place,
            send_sem=send_sem.at[len(started)],
            recv_sem=sem,
            device_id=target,
            device_id_type=mesh_ids,
        )
        started.append((copy, condition))
        run(condition, copy.start)

    def arrived(place, sem, condition=None):
        copy = pltpu.make_async_remote_copy(
            src_ref=place,
            dst_ref=place,
            send_sem=send_sem.at[0],
            recv_sem=sem,
            device_id={"row": other_row},
            device_id_type=mesh_ids,
        )
        run(condition, copy.wait_recv)

    pl.semaphore_wait(barrier, members)
    column_slot = me
    here = column_slot // col_size == row
    elsewhere = jnp.logical_not(here)
    other_mine = other_row * col_size + col
    cut = sets // CHUNKS
    straight, crossed = range(CHUNKS // 2), range(CHUNKS // 2, CHUNKS)

    def right_target(block):
        return {"col": block // seq_size, "seq": lax.rem(block, seq_size)}

    own_right = column_slot == mine
    own_crossed = column_slot == other_mine
    for j in crossed:
        at = pl.ds(j * cut, cut)
        ship(r_own.at[at], hop_s.at[at], {"row": other_row}, hop_recv.at[j])
    for j in straight:
        at = pl.ds(j * cut, cut)
        ship(
            r_own.at[at],
            r_s.at[seq, at],
            right_target(mine),
            r_recv.at[seq, j],
            jnp.logical_not(own_right),
        )

    chunk = outer // CHUNKS
    pairs = LANES // 2 // own
    left_steps = groups // pairs

    def project_left(step, carry):
        parts = []
        for t in range(pairs):
            at = pl.ds(pl.multiple_of((t * left_steps + step) * own, own), own)
            result = nt3(first, halves(own_s[at, :]))
            parts += [result[:outer], result[outer:]]
        line = jnp.concatenate(parts, axis=1)
        at = pl.ds(pl.multiple_of(step * chunk, chunk), chunk)
        for k in range(CHUNKS):
            l_s[k, col, seq, at, :] = line[k * chunk : (k + 1) * chunk]
        return carry

    lax.fori_loop(0, left_steps, project_left, 0, unroll=4)

    def relay_left(k, at, rightward, leftward, exists):
        place, sem = l_s.at[k, at, seq], l_recv.at[k, at, seq]
        if rightward:
            ship(place, place, {"col": col + 1}, sem, both(exists, col < col_size - 1))
        if leftward:
            ship(place, place, {"col": col - 1}, sem, both(exists, col > 0))
        ship(place, place, {"seq": other_seq}, sem, exists)

    def relay(place_of, k, distance, reach):
        for sign in (-1, 1):
            at = col + sign * distance
            exists = at >= 0 if sign < 0 else at < col_size
            place, sem = place_of(k, at)
            if distance:
                arrived(place, sem, exists)
            first_hop, last_hop = (reach, 1) if distance == 0 else (1, 1 if distance >= reach else 0)
            for hop in range(first_hop, 0, -1) if last_hop else ():
                onward = col - sign * hop
                inside = onward < col_size if sign < 0 else onward >= 0
                ship(place, place, {"col": onward}, sem, both(exists, inside) if distance else inside)
            if distance or sign < 0:
                ship(place, place, {"seq": other_seq}, sem, exists if distance else None)

    def stage(k, distance, reach):
        return k + max(0, distance - reach)

    def left_of(k, at):
        return l_s.at[k, at, seq], l_recv.at[k, at, seq]

    def left_slot(slot):
        for distance in range(1, col_size):
            for k in range(CHUNKS):
                if stage(k, distance, LEFT_REACH) == slot:
                    relay(left_of, k, distance, LEFT_REACH)
        if slot + 2 < CHUNKS:
            relay(left_of, slot + 2, 0, LEFT_REACH)

    relay(left_of, 0, 0, LEFT_REACH)
    relay(left_of, 1, 0, LEFT_REACH)

    for load in loads[3:]:
        load.wait()
    first_col = seq * half_cols
    flat_pair = pair_ref.reshape(rows * cols, channels)
    flat_revised = revised_ref.reshape(rows * cols, channels)

    def turn_in(column, carry):
        turned_s[column] = flat_pair[pl.ds(first_col + column, rows, stride=cols), :].T
        return carry

    lax.fori_loop(0, half_cols // 2, turn_in, 0, unroll=2)

    @pl.when(own_right)
    def _():
        for j in straight:
            r_s[seq, j * cut : (j + 1) * cut] = r_own[j * cut : (j + 1) * cut]

    for j in crossed:
        at = pl.ds(j * cut, cut)
        arrived(hop_s.at[at], hop_recv.at[j])
        ship(
            hop_s.at[at],
            r_s.at[seq, at],
            right_target(other_mine),
            r_recv.at[seq, j],
            jnp.logical_not(own_crossed),
        )

    @pl.when(own_crossed)
    def _():
        for j in crossed:
            r_s[seq, j * cut : (j + 1) * cut] = hop_s[j * cut : (j + 1) * cut]

    left_slot(0)
    source_here = lax.rem(column_slot, col_size) == col
    for js, kind in ((straight, here), (crossed, elsewhere)):
        for j in js:
            for source in range(seq_size):
                kept = jnp.logical_and(source_here, seq == source)
                place, sem = r_s.at[source, pl.ds(j * cut, cut)], r_recv.at[source, j]
                arrived(place, sem, jnp.logical_and(kind, jnp.logical_not(kept)))
                ship(place, place, {"row": other_row}, sem, kind)
    blank = jnp.zeros(((span - seqs) * chunk, rows), f32)
    for k in range(CHUNKS):
        for source in range(seq_size):
            left_s[k, (source * span + seqs) * chunk : (source + 1) * span * chunk, :] = blank
    lax.fori_loop(half_cols // 2, half_cols, turn_in, 0, unroll=2)
    left_slot(1)
    t_high, t_low = halves(product_ref[...].T * (1.0 / total))
    product_s[...] = jnp.concatenate([t_high, t_low], axis=0)
    c_high, c_low = halves(score_ref[...])
    c_both = jnp.concatenate([c_high, c_low], axis=0)
    x_s[mine] = own_s[pl.ds(pl.multiple_of(col * share * own, share * own), share * own), :]
    left_slot(2)

    for js, kind in ((straight, elsewhere), (crossed, here)):
        for j in js:
            for source in range(seq_size):
                arrived(r_s.at[source, pl.ds(j * cut, cut)], r_recv.at[source, j], kind)
    empty = jnp.zeros((span - seqs, LANES), f32)

    def turn_right(step, carry):
        lines = [part for source in range(seq_size) for part in (r_s[source, step], empty)]
        at = pl.ds(pl.multiple_of(step * LANES, LANES), LANES)
        right_s[at, :] = jnp.concatenate(lines, axis=0).T
        return carry

    lax.fori_loop(0, sets, turn_right, 0, unroll=2)
    r_high, r_low = halves(right_s[...])
    r_both = jnp.concatenate([r_high, r_low], axis=1)

    def chunk_arrived(k):
        for at in range(col_size):
            arrived(l_s.at[k, at, other_seq], l_recv.at[k, at, other_seq])

    def place_left(k, step):
        at = pl.ds(pl.multiple_of(step * chunk, chunk), chunk)
        for source in range(seq_size):
            blocks = [l_s[k, t, source, at, :] for t in range(col_size)]
            for t in range(pairs):
                for half in range(2):
                    lane = (2 * t + half) * own
                    line = jnp.concatenate([block[:, lane : lane + own] for block in blocks], axis=1)
                    place = source * span + half * groups + t * left_steps + step
                    left_s[k, pl.ds(pl.multiple_of(place * chunk, chunk), chunk), :] = line

    def outer_chunk(k):
        def outer_step(step, carry):
            pieces = [left_s[k, pl.ds(2 * step + t, LANES, stride=chunk), :] for t in range(2)]
            l_high, l_low = halves(jnp.concatenate(pieces, axis=1))
            product = mm(r_both, jnp.concatenate([l_high, l_high], axis=0)) + mm(r_high, l_low)
            p_high, p_low = halves(product)
            for t in range(2):
                high_s[2 * step + t] = p_high[:, t * rows : (t + 1) * rows]
                low_s[2 * step + t] = p_low[:, t * rows : (t + 1) * rows]
            return carry

        lax.fori_loop(0, chunk // 2, outer_step, 0, unroll=2)

    def project(k, step):
        def block(ref):
            pieces = [
                ref[:, pl.ds(pl.multiple_of((2 * step + t) * outer, outer), outer), :].reshape(chunk * outer, rows)
                for t in range(2)
            ]
            return jnp.concatenate(pieces, axis=1)

        t_both = product_s[:, k * chunk * outer : (k + 1) * chunk * outer]
        joint = mm(t_both, block(high_s))
        update = joint[:channels] + (joint[channels:] + mm(t_both[:channels], block(low_s)))
        return jnp.concatenate([turned_s[2 * step + t] for t in range(2)], axis=1) + update

    def send_x():
        for offset in range(1, col_size):
            target = lax.rem(col + offset, col_size)
            ship(
                own_s.at[pl.ds(pl.multiple_of(target * share * own, share * own), share * own), :],
                x_s.at[mine],
                {"col": target},
                x_recv.at[mine],
            )
        ship(x_s.at[mine], x_s.at[mine], {"row": other_row}, x_recv.at[mine])

    chunk_arrived(0)

    def place_first(step, carry):
        place_left(0, step)
        return carry

    lax.fori_loop(0, left_steps, place_first, 0, unroll=6)
    for k in range(CHUNKS - 1):
        left_slot(k + CHUNKS - 1)
        outer_chunk(k)
        chunk_arrived(k + 1)
        if k == 1:
            send_x()

        def gather_step(turn, carry):
            steps = [GATHERED * turn + u for u in range(GATHERED)]
            share_steps = left_steps * 2 * GATHERED // half_cols
            for u in range(share_steps):
                place_left(k + 1, share_steps * turn + u)
            for step, revised in [(step, project(k, step)) for step in steps]:
                for t in range(2):
                    turned_s[2 * step + t] = revised[:, t * rows : (t + 1) * rows]
            return carry

        lax.fori_loop(0, half_cols // 2 // GATHERED, gather_step, 0)
    outer_chunk(CHUNKS - 1)

    def pair_step(turn, carry):
        steps = [PAIRED * turn + u for u in range(PAIRED)]
        results = []
        for step in steps:
            revised = project(CHUNKS - 1, step)
            center = revised - jnp.mean(revised, axis=0, keepdims=True)
            spread = jnp.mean(center * center, axis=0, keepdims=True)
            n_high, n_low = halves(center)
            turned = mm(c_both, n_high)
            logits = turned[:heads] + (turned[heads:] + mm(c_high, n_low))
            results.append((step, revised, logits / jnp.sqrt(spread + epsilon)))
        for step, revised, logits in results:
            for t in range(2):
                turned_s[2 * step + t] = revised[:, t * rows : (t + 1) * rows]
                logit_s[me, 2 * step + t] = logits[:, t * rows : (t + 1) * rows]
        return carry

    section = half_cols // CHUNKS

    def logits_of(k, at):
        slot = at * seq_size + seq
        return logit_s.at[slot, pl.ds(k * section, section)], logit_recv.at[slot, k]

    def logit_slot(slot):
        for distance in range(1, col_size):
            for k in range(CHUNKS):
                if stage(k, distance, LOGIT_REACH) == slot:
                    relay(logits_of, k, distance, LOGIT_REACH)

    for k in range(CHUNKS):
        lax.fori_loop(k * section // 2 // PAIRED, (k + 1) * section // 2 // PAIRED, pair_step, 0)
        relay(logits_of, k, 0, LOGIT_REACH)
        if k == CHUNKS - 1:
            for offset in range(1, col_size):
                at = row * col_size + lax.rem(col + offset, col_size)
                arrived(x_s.at[at], x_recv.at[at])
                ship(x_s.at[at], x_s.at[at], {"row": other_row}, x_recv.at[at])
    logit_slot(0)

    def turn_out(column, carry):
        flat_revised[pl.ds(first_col + column, rows, stride=cols), :] = turned_s[column].T
        return carry

    lax.fori_loop(0, half_cols // 2, turn_out, 0, unroll=4)
    logit_slot(1)
    lax.fori_loop(half_cols // 2, half_cols, turn_out, 0, unroll=4)
    half_pair = revised_ref.at[:, pl.ds(pl.multiple_of(first_col, half_cols), half_cols), :]
    pair_copy = pltpu.make_async_remote_copy(
        src_ref=half_pair,
        dst_ref=half_pair,
        send_sem=pair_sem.at[0],
        recv_sem=pair_sem.at[1],
        device_id={"seq": other_seq},
        device_id_type=mesh_ids,
    )
    pair_copy.start()
    logit_slot(2)

    def spread_heads(matrix):
        width = matrix.shape[1] // heads
        zero = jnp.zeros((matrix.shape[0], width), f32)
        upper, lower = [], []
        for head in range(heads):
            piece = matrix[:, head * width : (head + 1) * width]
            upper += [piece, zero]
            lower += [zero, piece]
        return jnp.concatenate([jnp.concatenate(upper, axis=1), jnp.concatenate(lower, axis=1)], axis=0)

    g_high, g_low = halves(spread_heads(gate_ref[...]))
    g_twice = jnp.concatenate([g_high, g_high], axis=0)

    def gate_step(group, carry):
        at = pl.ds(pl.multiple_of(group * own, own), own)
        x_high, x_low = halves(x_s[pl.ds(row * col_size, col_size), at, :].reshape(rows, LANES))
        inner = mm(jnp.concatenate([x_high, x_low], axis=1), g_twice) + mm(x_high, g_low)
        gates_s[group] = jax.nn.sigmoid(inner)
        return carry

    lax.fori_loop(0, share, gate_step, 0, unroll=2)
    logit_slot(3)
    for at in range(col_size):
        arrived(x_s.at[other_row * col_size + at], x_recv.at[other_row * col_size + at])
    s_high, s_low = halves(spread_heads(source_ref[...]))
    s_twice = jnp.concatenate([s_high, s_high], axis=0)

    def value_step(group, carry):
        at = pl.ds(pl.multiple_of(group * own, own), own)
        x_high, x_low = halves(x_s[:, at, :].reshape(tokens_all, LANES))
        values = mm(jnp.concatenate([x_high, x_low], axis=1), s_twice) + mm(x_high, s_low)
        v_high, v_low = halves(values)
        v_high_s[group] = v_high
        v_low_s[group] = v_low
        return carry

    lax.fori_loop(0, share // 3, value_step, 0, unroll=2)
    logit_slot(4)
    lax.fori_loop(share // 3, share, value_step, 0, unroll=2)
    f_halves = halves(spread_heads(final_ref[...]))
    for slot in range(5, CHUNKS + col_size - 2):
        logit_slot(slot)
    for k in range(CHUNKS):
        for at in range(col_size):
            slot = at * seq_size + other_seq
            arrived(logit_s.at[slot, pl.ds(k * section, section)], logit_recv.at[slot, k])

    logits = logit_s[...].reshape(tokens_all, heads, rows)
    powers = jnp.exp(logits - jnp.max(logits, axis=0)[None])
    weights = powers * (1.0 / jnp.sum(powers, axis=0))[None]
    weight_s[...] = weights.reshape(tokens_all * heads, rows)
    for head in range(heads):
        w_high, w_low = halves(weight_s[pl.ds(head, tokens_all, stride=heads), :].T)
        at = head % 2 * rows
        mixer_s[head // 2, at : at + rows, :] = w_high
        mixer_s[head // 2, 2 * rows + at : 2 * rows + at + rows, :] = w_low
    lane_head = lax.broadcasted_iota(jnp.int32, (rows, 2 * LANES), 1) % LANES
    upper_head = lane_head < LANES // 2

    for turn in range(share // 2):
        parts = []
        for p in range(heads // 2):
            lanes = slice(p * LANES, (p + 1) * LANES)
            v_high, v_low = (
                jnp.concatenate([ref[2 * turn + t, :, lanes] for t in range(2)], axis=1)
                for ref in (v_high_s, v_low_s)
            )
            joint = mm(mixer_s[p], v_high)
            full = joint[: 2 * rows] + (joint[2 * rows :] + mm(mixer_s[p, : 2 * rows, :], v_low))
            parts.append(jnp.where(upper_head, full[:rows], full[rows:]))
        mixed = []
        for t in range(2):
            line = jnp.concatenate([part[:, t * LANES : (t + 1) * LANES] for part in parts], axis=1)
            mixed.append(line * gates_s[2 * turn + t])
        result = nt3(halves(jnp.concatenate(mixed, axis=0)), f_halves)
        for t in range(2):
            part_s[:, 2 * turn + t] = result[t * rows : (t + 1) * rows].reshape(col_size, own, LANES)
        at = pl.ds(col * share + 2 * turn, 2)
        for offset in range(1, col_size):
            target = lax.rem(col + offset, col_size)
            ship(
                part_s.at[target, pl.ds(2 * turn, 2)],
                whole_s.at[at],
                {"col": target},
                part_recv.at[col, turn],
            )
        whole_s[at] = part_s[col, 2 * turn : 2 * turn + 2]

    for offset in range(1, col_size):
        source = lax.rem(col + offset, col_size)
        for turn in range(share // 2):
            arrived(whole_s.at[pl.ds(source * share + 2 * turn, 2)], part_recv.at[source, turn])
    for t in range(2):
        at = pl.ds(t * groups, groups)
        out_ref[at] = raw_ref[at] + whole_s[:, :, t * depth : (t + 1) * depth]

    for copy, condition in started:
        run(condition, copy.wait_send)
    pair_copy.wait_send()
    other_half = revised_ref.at[:, pl.ds(pl.multiple_of(other_seq * half_cols, half_cols), half_cols), :]
    arrived(other_half, pair_sem.at[1])


def twice(matrix):
    zero = jnp.zeros_like(matrix)
    return jnp.concatenate(
        [jnp.concatenate([matrix, zero], axis=1), jnp.concatenate([zero, matrix], axis=1)], axis=0
    )


FINISH_CUTS = 4


def finish_kernel(*refs):
    count = len(refs) // 2
    copies = []
    for source, target in zip(refs[:count], refs[count:-1]):
        share = source.shape[0] // FINISH_CUTS
        for cut in range(FINISH_CUTS):
            at = pl.ds(cut * share, share)
            copies.append(pltpu.make_async_copy(source.at[at], target.at[at], refs[-1].at[len(copies)]))
            copies[-1].start()
    for copy in copies:
        copy.wait()


def fast_path(
    alignment_tensor,
    residue_couplings,
    first_factor_matrix,
    second_factor_matrix,
    tensor_product_matrix,
    coupling_score_matrix,
    averaged_source_matrix,
    sigmoid_matrix,
    final_matrix,
):
    seqs, _, own, depth = alignment_tensor.shape
    rows, cols, channels = residue_couplings.shape
    outer = first_factor_matrix.shape[1]
    heads = coupling_score_matrix.shape[1]
    row_size, col_size, seq_size = (lax.axis_size(a) for a in ("row", "col", "seq"))
    blocks = row_size * col_size
    half_cols = cols // seq_size
    members = col_size * seq_size
    groups = seqs // 2
    wide = 2 * averaged_source_matrix.shape[1]
    share = groups // col_size
    vmem = pl.BlockSpec(memory_space=pltpu.VMEM)
    dma = pltpu.SemaphoreType.DMA
    arrays = (
        alignment_tensor.reshape(seqs, own, depth),
        residue_couplings,
        first_factor_matrix.T,
        second_factor_matrix.T,
        tensor_product_matrix,
        coupling_score_matrix.T,
        averaged_source_matrix,
        sigmoid_matrix,
        final_matrix.T,
    )
    alignment, couplings = pl.pallas_call(
        functools.partial(block_kernel, row_size, col_size, seq_size, heads),
        out_shape=(
            pltpu.VMEM((seqs, own, depth), f32),
            pltpu.VMEM((rows, cols, channels), f32),
        ),
        in_specs=[pl.BlockSpec(memory_space=pltpu.HBM)] * 9,
        out_specs=(vmem, vmem),
        scratch_shapes=[pltpu.VMEM(a.shape, f32) for a in arrays]
        + [
            dma((len(arrays),)),
            pltpu.VMEM((groups * own, LANES), f32),
            pltpu.VMEM((CHUNKS, col_size, seq_size, groups // (LANES // 2 // own) * outer // CHUNKS, LANES), f32),
            pltpu.VMEM((groups * own, LANES), f32),
            pltpu.VMEM((half_cols * outer // LANES, seqs, LANES), f32),
            pltpu.VMEM((half_cols * outer // LANES, seqs, LANES), f32),
            pltpu.VMEM((seq_size, half_cols * outer // LANES, seqs, LANES), f32),
            pltpu.VMEM((CHUNKS, LANES * outer // CHUNKS, rows), f32),
            pltpu.VMEM((half_cols * outer, LANES), f32),
            pltpu.VMEM((outer // CHUNKS, half_cols * outer, rows), bf16),
            pltpu.VMEM((outer // CHUNKS, half_cols * outer, rows), bf16),
            pltpu.VMEM((2 * channels, outer * outer), bf16),
            pltpu.VMEM((half_cols, channels, rows), f32),
            pltpu.VMEM((blocks, share * own, LANES), f32),
            pltpu.VMEM((members, half_cols, heads, rows), f32),
            pltpu.VMEM((members * half_cols * heads, rows), f32),
            pltpu.VMEM((heads // 2, 4 * rows, members * half_cols), bf16),
            pltpu.VMEM((share, members * half_cols, wide), bf16),
            pltpu.VMEM((share, members * half_cols, wide), bf16),
            pltpu.VMEM((share, rows, wide), f32),
            pltpu.VMEM((col_size, share, own, LANES), f32),
            pltpu.VMEM((groups, own, LANES), f32),
            dma((192,)),
            dma((CHUNKS, col_size, seq_size)),
            dma((seq_size, CHUNKS)),
            dma((CHUNKS,)),
            dma((blocks,)),
            dma((members, CHUNKS)),
            dma((col_size, share // 2)),
            dma((2,)),
        ],
        compiler_params=pltpu.CompilerParams(
            collective_id=0, has_side_effects=True, vmem_limit_bytes=59 << 20
        ),
    )(*arrays)
    revised_alignment, revised_couplings = pl.pallas_call(
        finish_kernel,
        out_shape=(
            jax.ShapeDtypeStruct((seqs, own, depth), f32),
            jax.ShapeDtypeStruct((rows, cols, channels), f32),
        ),
        in_specs=[vmem] * 2,
        out_specs=(pl.BlockSpec(memory_space=pltpu.HBM),) * 2,
        scratch_shapes=[dma((2 * FINISH_CUTS,))],
        compiler_params=pltpu.CompilerParams(vmem_limit_bytes=12 << 20),
    )(alignment, couplings)
    return revised_alignment.reshape(alignment_tensor.shape), revised_couplings


def on_device(alignment_tensor, residue_couplings, first_factor_matrix, *rest):
    seqs, tiles, own, depth = alignment_tensor.shape
    rows, cols, channels = residue_couplings.shape
    row_size, col_size, seq_size = (lax.axis_size(a) for a in ("row", "col", "seq"))
    fits = (
        tiles == 1
        and rows == own * col_size == LANES
        and cols == own * seq_size
        and row_size * rows == col_size * cols
        and own % 16 == 0
        and seqs % 6 == 0
        and 2 * depth == channels == LANES
        and first_factor_matrix.shape[1] % (8 * CHUNKS) == 0
        and seqs % (4 * col_size) == 0
        and rest[3].shape[1] == 8 * LANES // 4
        and cols % (4 * CHUNKS) == 0
        and seq_size == row_size == 2
        and rest[2].shape[1] == 8 == own * own // LANES
        and seqs * seq_size <= LANES
        and seqs // 2 % (LANES // 2 // own) == 0
        and col_size == CHUNKS
    )
    path = fast_path if fits else general_path
    return path(alignment_tensor, residue_couplings, first_factor_matrix, *rest)


def solution(mesh):
    return jax.shard_map(
        on_device,
        mesh=mesh,
        in_specs=(
            P(("grp", "seq"), "row", "col", None),
            P(("grp", "row"), "col", None),
            P(),
            P(),
            P(),
            P(),
            P(),
            P(),
            P(),
        ),
        out_specs=(P(("grp", "seq"), "row", "col", None), P(("grp", "row"), "col", None)),
        check_vma=False,
    )
```
